32 devices in a mesh: gy: 8 (over y, x, core), gz: 4 (over z).
Axes of the slice: x: 2, y: 2, z: 4, core: 2. Of those that a mesh axis runs over, the one named last changes fastest.
Arguments:
- volume: float32 [64, 128, 1024], P('gz', None, 'gy'), may hold values from -6 to 6
- contrast: float32 [128], replicated, may hold values from 0.1 to 1
Outputs:
- filtered: float32 [64, 128, 1024], P('gz', None, 'gy')
The draws below stay inside these ranges and needn't reach their ends.
All inputs are finite; a program needn't handle non-finite values.
Results may differ from the reference program's by a relative error of at most 0.0003.
Values sent between devices are 32-bit elements; how exact they have to be, the bound alone decides.
A program may use at most 192 MiB of HBM per device.

```python
import math
import jax
import jax.numpy as jnp
from jax import lax

NX = 128
STEPS = 2
NY = 1024
NZ = 64


def steps_of(rng, extent, split, least, largest):
    level = 1.0
    for dim, shards_of in split:
        heights = jax.random.uniform(jax.random.fold_in(jax.random.fold_in(rng, 6), dim), (shards_of,), jnp.float32, least / len(split), largest / len(split))
        level = level * jnp.repeat(jnp.exp(heights), extent[dim] // shards_of).reshape((-1,) + (1,) * (len(extent) - 1 - dim))
    return level


def scatter_about(key, dims, deviation, limit, shards=(), kind=jnp.bfloat16):
    loudness = steps_of(key, dims, shards, -0.22, 0.18) if shards else 1.0
    drawn = jax.random.normal(key, dims, jnp.float32) * deviation * loudness
    return jnp.minimum(jnp.maximum(drawn, -limit), limit).astype(kind)


def setup_inputs(seed: int = 0) -> dict:
    streams_of = jax.random.split(jax.random.key(seed), 3)
    return {
        "volume": scatter_about(streams_of[0], (NZ, NX, NY), 1.0, 6.0, ((0, 4), (2, 8)), jnp.float32),
        "contrast": jnp.clip(jnp.exp(jax.random.uniform(streams_of[1], (NX,), jnp.float32, math.log(0.1), math.log(1.0))), 0.1, 1.0),
    }


kernel_taps = (0.05448868, 0.24420134, 0.40261995, 0.24420134, 0.05448868)
half_scale = 600.0


def slice_axis(array, start, count, axis, stride=1):
    return lax.slice_in_dim(array, start, start + stride * (count - 1) + 1, stride, axis)


def reduce_solve(lower, diagonal, upper, right, axis):
    length = right.shape[axis]
    if length == 1:
        return right / diagonal
    count_even = (length + 1) // 2
    count_odd = length // 2
    evens = [slice_axis(array, 0, count_even, axis, 2) for array in (lower, diagonal, upper, right)]
    odds = [slice_axis(array, 1, count_odd, axis, 2) for array in (lower, diagonal, upper, right)]
    before = [slice_axis(array, 0, count_odd, axis) for array in evens]
    zero_one = jnp.zeros_like(slice_axis(evens[0], 0, 1, axis))
    padding = [zero_one, zero_one + 1.0, zero_one, zero_one]
    after = [slice_axis(jnp.concatenate([array, extra], axis), 1, count_odd, axis) for array, extra in zip(evens, padding)]
    factor_before = -odds[0] / before[1]
    factor_after = -odds[2] / after[1]
    new_lower = factor_before * before[0]
    new_diag = odds[1] + factor_before * before[2] + factor_after * after[0]
    new_upper = factor_after * after[2]
    new_right = odds[3] + factor_before * before[3] + factor_after * after[3]
    solved_odd = reduce_solve(new_lower, new_diag, new_upper, new_right, axis)
    zero_row = jnp.zeros_like(slice_axis(solved_odd, 0, 1, axis))
    extra_rows = [zero_row] * (count_even - count_odd)
    padded_odd = jnp.concatenate([zero_row, solved_odd] + extra_rows, axis)
    left_value = slice_axis(padded_odd, 0, count_even, axis)
    right_value = slice_axis(padded_odd, 1, count_even, axis)
    solved_even = (evens[3] - evens[0] * left_value - evens[2] * right_value) / evens[1]
    odd_full = jnp.concatenate([solved_odd] + extra_rows, axis)
    paired = jnp.stack([solved_even, odd_full], axis=axis + 1)
    shape = right.shape[:axis] + (2 * count_even,) + right.shape[axis + 1:]
    return slice_axis(paired.reshape(shape), 0, length, axis)


def line_solve(upper, right, axis):
    length = upper.shape[axis]
    lower = jnp.concatenate([jnp.zeros_like(slice_axis(upper, 0, 1, axis)), slice_axis(upper, 0, length - 1, axis)], axis)
    diagonal = 1.0 + lower + upper
    return reduce_solve(-lower, diagonal, -upper, right, axis)


def smooth_axis(padded, axis):
    count = padded.shape[axis] - 4
    total = kernel_taps[0] * slice_axis(padded, 0, count, axis)
    for offset in range(1, 5):
        total = total + kernel_taps[offset] * slice_axis(padded, offset, count, axis)
    return total


def face_upper(diffusivity, axis):
    length = diffusivity.shape[axis]
    inner = (slice_axis(diffusivity, 0, length - 1, axis) + slice_axis(diffusivity, 1, length - 1, axis)) * half_scale
    return jnp.concatenate([inner, jnp.zeros_like(slice_axis(diffusivity, 0, 1, axis))], axis)


def reference(volume, contrast):
    current = volume
    for repeat in range(STEPS):
        blurred = jnp.pad(current, 2)
        blurred = smooth_axis(blurred, 0)
        blurred = smooth_axis(blurred, 2)
        blurred = smooth_axis(blurred, 1)
        extended = jnp.pad(blurred, 1)
        grad_z = (extended[2:, 1:-1, 1:-1] - extended[:-2, 1:-1, 1:-1]) * 0.5
        grad_y = (extended[1:-1, 1:-1, 2:] - extended[1:-1, 1:-1, :-2]) * 0.5
        grad_x = (extended[1:-1, 2:, 1:-1] - extended[1:-1, :-2, 1:-1]) * 0.5
        square = grad_x * grad_x + grad_y * grad_y + grad_z * grad_z
        diffusivity = 1.0 / (1.0 + square / (contrast * contrast)[None, :, None])
        solved_x = line_solve(face_upper(diffusivity, 1), current, 1)
        solved_y = line_solve(face_upper(diffusivity, 2), current, 2)
        solved_z = line_solve(face_upper(diffusivity, 0), current, 0)
        current = (solved_x + solved_y + solved_z) / 3.0
    return current
```

```python
import functools

import jax
import jax.numpy as jnp
from jax import lax
from jax.experimental import pallas as pl
from jax.experimental.pallas import tpu as pltpu
from jax.sharding import PartitionSpec as P

STEPS = 2
TAPS = (0.05448868, 0.24420134, 0.40261995, 0.24420134, 0.05448868)
SCALE = 600.0
MESH = pl.DeviceIdType.MESH
DIRECTIONS = [(dy, dz) for dz in (-1, 1, 0) for dy in (0, -1, 1) if (dy, dz) != (0, 0)]
PAD = 8
HALO = 4
CHUNK = 32
STENCIL_ROWS = 48
SEGMENTS = 4
SKEW = 8


def merge(left, right):
    ea, ra, eb, rb, g, f = left
    ea2, ra2, eb2, rb2, g2, f2 = right
    s1 = 1.0 / (eb + g + f)
    wg, wf, q1 = g * s1, f * s1, rb * s1
    ea = ea + wg * eb
    ra = ra + wg * rb
    ea2 = ea2 + wf * eb
    ra2 = ra2 + wf * rb
    g1 = wf * g
    s2 = 1.0 / (ea2 + g1 + g2)
    vg, vf, q2 = g1 * s2, g2 * s2, ra2 * s2
    joined = (ea + vg * ea2, ra + vg * ra2, eb2 + vf * ea2, rb2 + vf * ra2, vf * g1, f2)
    return joined, (wg, wf, q1, vg, vf, q2)


def unmerge(weights, va, vb):
    wg, wf, q1, vg, vf, q2 = weights
    inner_right = vg * va + vf * vb + q2
    inner_left = wg * va + wf * inner_right + q1
    return inner_left, inner_right


def solve_pair(ea, ra, eb, rb, g):
    s = 1.0 / (ea + g)
    w = g * s
    vb = (rb + w * ra) / (eb + w * ea)
    return w * vb + ra * s, vb


def merge_all(chains):
    levels = []
    while len(chains) > 1:
        pairs = [merge(chains[i], chains[i + 1]) for i in range(0, len(chains), 2)]
        chains = [p[0] for p in pairs]
        levels.append([p[1] for p in pairs])
    return chains[0], levels


def unmerge_all(levels, va, vb):
    ends = [(va, vb)]
    for level in reversed(levels):
        split = []
        for weights, (a, b) in zip(level, ends):
            inner_left, inner_right = unmerge(weights, a, b)
            split += [(a, inner_left), (inner_right, b)]
        ends = split
    return ends


def line_start(get_d, get_r, count):
    states = []
    for base in range(0, count, count // SEGMENTS):
        d0, d1 = get_d(base), get_d(base + 1)
        one = jnp.ones_like(d0)
        states.append((one, get_r(base), d0 + d1, one, get_r(base + 1), d1))
    return tuple(states)


def line_reduce(get_d, get_r, weights, count, first, last, states):
    size = count // SEGMENTS

    def body(i, states):
        new = []
        for k, (ea, ra, g, e, r, d) in enumerate(states):
            j = k * size + i
            d1 = get_d(j + 1)
            f = d + d1
            s = 1.0 / (e + g + f)
            wf, wg = f * s, g * s
            weights[0, j] = wf
            weights[1, j] = wg
            weights[2, j] = r * s
            new.append((ea + wg * e, ra + wg * r, wf * g, 1.0 + wf * e, get_r(j + 1) + wf * r, d1))
        return tuple(new)

    return lax.fori_loop(first, last, body, states)


def line_chain(get_d, states, count, edge):
    size = count // SEGMENTS
    chains = []
    for k, (ea, ra, g, e, r, d) in enumerate(states):
        f = d + get_d((k + 1) * size) if k + 1 < SEGMENTS else edge(d)
        chains.append((ea, ra, e, r, g, f))
    return merge_all(chains)


def line_back(put, weights, count, ends):
    size = count // SEGMENTS
    for k, (a, b) in enumerate(ends):
        put(k * size, a)
        put(k * size + size - 1, b)

    def body(t, values):
        new = []
        for k, v in enumerate(values):
            j = k * size + size - 2 - t
            v = weights[0, j] * v + (weights[1, j] * ends[k][0] + weights[2, j])
            put(j, v)
            new.append(v)
        return tuple(new)

    lax.fori_loop(0, size - 2, body, tuple(b for a, b in ends), unroll=3)


def kernel(ny, nz, vol, con, out, c_ref, t_ref, b_ref, d_ref, dt_ref, wx_ref, wy_ref, wz_ref, vx_ref, vy_ref,
           vz_ref, cur_ref, zr_ref, zi_ref, zsend, zbuf, zvsend, zv, zraw_s, zraw_r, ysend, yrecv, yall, yv_ref,
           halo_s, halo_r, zs, zrs, zvs, zvr, zws, zwr, ys, yr, yas, yar):
    depth, nx, cols = vol.shape
    rows = cols + 2 * PAD
    tall = depth + 2 * HALO
    chunks = cols // CHUNK
    ky = lax.axis_index("gy")
    kz = lax.axis_index("gz")

    def at(y, z):
        return {"gy": y, "gz": z}

    def exists(dy, dz):
        ok = True
        if dy:
            ok = (ky + dy >= 0) & (ky + dy < ny)
        if dz:
            ok = ok & (kz + dz >= 0) & (kz + dz < nz)
        return ok

    direct = nz == 4
    far = lax.rem(kz + 2, nz)
    groups = ny // 2
    side = lax.rem(ky, 2)
    group = lax.div(ky, 2)
    twin = ky + 1 - 2 * side

    def member(j):
        return 2 * lax.rem(group + j, groups) + side

    barrier = pltpu.get_barrier_semaphore()
    expected = jnp.int32(groups + (1 if direct else 0))
    for dy, dz in DIRECTIONS:
        ok = exists(dy, dz)
        expected = expected + jnp.where(ok, 1, 0)

        @pl.when(ok)
        def _(dy=dy, dz=dz):
            pl.semaphore_signal(barrier, inc=1, device_id=at(ky + dy, kz + dz), device_id_type=MESH)

    for y in [twin] + [member(j) for j in range(1, groups)]:
        pl.semaphore_signal(barrier, inc=1, device_id=at(y, kz), device_id_type=MESH)
    if direct:
        pl.semaphore_signal(barrier, inc=1, device_id=at(ky, far), device_id_type=MESH)

    @pl.loop(0, depth // 4)
    def _(k):
        for z in [4 * k, 4 * k + 1, 4 * k + 2, 4 * k + 3]:
            plane = vol[z]
            cur_ref[z, 0:nx, :] = plane
            c_ref[0, z + HALO, PAD:PAD + cols, :] = plane.T

    pl.semaphore_wait(barrier, expected)

    left = kz < nz // 2
    inward = jnp.where(left, 1, -1)
    order = jnp.where(left, kz, nz - 1 - kz)
    middle = order == nz // 2 - 1
    outermost = order == 0
    slot_out = jnp.where(middle, 1, 0)

    lane = lax.broadcasted_iota(jnp.int32, (STENCIL_ROWS, nx), 1)
    keep = {s: (lane >= s) if s > 0 else (lane < nx + s) for s in (-2, -1, 1, 2)}

    def shifted(value, s):
        return jnp.where(keep[s][:value.shape[0]], pltpu.roll(value, s % nx, 1), 0.0)

    contrast = con[...]
    squared = jnp.broadcast_to(contrast * contrast, (STENCIL_ROWS, nx))

    tall_x = nx + SKEW
    tall_y = cols + SKEW
    cur2 = cur_ref.reshape(depth * tall_x, cols)
    dt2 = dt_ref.reshape(depth * tall_x, cols)
    vx2 = vx_ref.reshape(depth * tall_x, cols)
    vy2 = vy_ref.reshape(depth * tall_y, nx)
    d2 = d_ref.reshape((depth + 2) * rows, nx)

    def finish(z, target):
        plane = (vx_ref[z, 0:nx, :] + (vy_ref[z, 0:cols, :] + vz_ref[z]).T) * (1.0 / 3.0)
        if target is None:
            out[z] = plane
        else:
            cur_ref[z, 0:nx, :] = plane
            target[z + HALO, PAD:PAD + cols, :] = plane.T

    def finish_edges(target):
        @pl.loop(0, HALO // 2)
        def _(k):
            for t in range(2):
                finish(2 * k + t, target)
                finish(depth - HALO + 2 * k + t, target)

    def finish_middle(target):
        @pl.loop(0, (depth - 2 * HALO) // 4)
        def _(k):
            for t in range(4):
                finish(HALO + 4 * k + t, target)

    parts = [(r0, min(STENCIL_ROWS, cols + 8 - r0)) for r0 in range(0, cols + 8, STENCIL_ROWS)]

    for step in range(STEPS):
        c4 = c_ref.at[step]
        c2 = c4.reshape(tall * rows, nx)

        def halo(i, c4=c4, step=step):
            dy, dz = DIRECTIONS[i]
            src_y = {0: (PAD, cols), 1: (cols, PAD), -1: (PAD, PAD)}[dy]
            dst_y = {0: (PAD, cols), 1: (0, PAD), -1: (PAD + cols, PAD)}[dy]
            src_z = {0: (HALO, depth), 1: (depth, HALO), -1: (HALO, HALO)}[dz]
            dst_z = {0: (HALO, depth), 1: (0, HALO), -1: (HALO + depth, HALO)}[dz]
            src = c4.at[pl.ds(*src_z), pl.ds(*src_y), :]
            dst = c4.at[pl.ds(*dst_z), pl.ds(*dst_y), :]
            copy = pltpu.make_async_remote_copy(
                src_ref=src, dst_ref=dst, send_sem=halo_s.at[step, i], recv_sem=halo_r.at[step, i],
                device_id=at(ky + dy, kz + dz), device_id_type=MESH)
            return copy, dst_z, dst_y

        def send(layers, halo=halo, c4=c4):
            for i, (dy, dz) in enumerate(DIRECTIONS):
                if (dz != 0) != layers:
                    continue
                copy, dst_z, dst_y = halo(i)

                @pl.when(exists(dy, dz))
                def _(copy=copy):
                    copy.start()

                @pl.when(jnp.logical_not(exists(-dy, -dz)))
                def _(dst_z=dst_z, dst_y=dst_y):
                    c4[pl.ds(*dst_z), pl.ds(*dst_y), :] = jnp.zeros((dst_z[1], dst_y[1], nx), jnp.float32)

        def receive(layers):
            for i, (dy, dz) in enumerate(DIRECTIONS):
                if (dz != 0) != layers:
                    continue
                copy = halo(i)[0]

                @pl.when(exists(-dy, -dz))
                def _(copy=copy):
                    copy.wait_recv()

        if step == 0:
            send(True)
        else:
            finish_edges(c4)
            send(True)
            finish_middle(c4)
        send(False)

        def blur_layers(z0, z1, pieces):
            @pl.loop(z0, z1)
            def _(z):
                for r0, size in pieces:
                    part = pl.ds(r0, size)
                    total = TAPS[2] * c4[z + 2, part, :]
                    total = total + TAPS[1] * (c4[z + 1, part, :] + c4[z + 3, part, :])
                    total = total + TAPS[0] * (c4[z, part, :] + c4[z + 4, part, :])
                    t_ref[z, pl.ds(r0, size), :] = total

        def blur(z0, z1):
            @pl.loop(z0, z1, unroll=2)
            def _(z):
                for r0, size in parts:
                    def tap(o):
                        return t_ref[z, pl.ds(r0 + 4 + o, size), :]
                    total = TAPS[2] * tap(0) + TAPS[1] * (tap(-1) + tap(1)) + TAPS[0] * (tap(-2) + tap(2))
                    b_ref[z, pl.ds(r0, size), :] = (
                        TAPS[2] * total + TAPS[1] * (shifted(total, 1) + shifted(total, -1))
                        + TAPS[0] * (shifted(total, 2) + shifted(total, -2)))

            @pl.when(ky == 0)
            def _():
                b_ref[z0:z1, PAD - 5:PAD - 4, :] = jnp.zeros((z1 - z0, 1, nx), jnp.float32)

            @pl.when(ky == ny - 1)
            def _():
                b_ref[z0:z1, cols + PAD - 4:cols + PAD - 3, :] = jnp.zeros((z1 - z0, 1, nx), jnp.float32)

        def diffuse(z0, z1):
            @pl.loop(z0, z1, unroll=2)
            def _(z):
                for r0, size in parts:
                    mid = b_ref[z + 1, pl.ds(r0 + 4, size), :]
                    grad_z = b_ref[z + 2, pl.ds(r0 + 4, size), :] - b_ref[z, pl.ds(r0 + 4, size), :]
                    grad_y = b_ref[z + 1, pl.ds(r0 + 5, size), :] - b_ref[z + 1, pl.ds(r0 + 3, size), :]
                    grad_x = shifted(mid, -1) - shifted(mid, 1)
                    square = (grad_x * grad_x + grad_y * grad_y + grad_z * grad_z) * 0.25
                    d_ref[z, pl.ds(r0 + PAD, size), :] = (SCALE * squared[:size]) / (squared[:size] + square)

        def turn(z0, z1):
            step_by = 2 if (z1 - z0) % 2 == 0 else 1

            @pl.loop(0, (z1 - z0) // step_by)
            def _(k):
                for t in range(step_by):
                    z = z0 + k * step_by + t
                    dt_ref[z, 0:nx, :] = d_ref[z + 1, PAD:PAD + cols, :].T

        own_rows = [(r0, min(STENCIL_ROWS, cols + PAD - r0)) for r0 in range(PAD, cols + PAD, STENCIL_ROWS)]
        halo_rows = [(0, PAD), (cols + PAD, PAD)]
        blur_layers(HALO, depth, own_rows)
        receive(False)
        blur_layers(HALO, depth, halo_rows)
        blur(HALO, depth)
        diffuse(HALO, depth - 2)
        turn(HALO - 1, depth - 3)
        receive(True)
        all_rows = own_rows + halo_rows
        blur_layers(0, HALO, all_rows)
        blur_layers(depth, depth + 4, all_rows)
        blur(0, HALO)
        blur(depth, depth + 4)

        @pl.when(kz == 0)
        def _():
            b_ref[1] = jnp.zeros(b_ref.shape[1:], jnp.float32)

        @pl.when(kz == nz - 1)
        def _():
            b_ref[depth + 2] = jnp.zeros(b_ref.shape[1:], jnp.float32)

        diffuse(0, HALO)
        diffuse(depth - 2, depth + 2)
        turn(0, HALO - 1)
        turn(depth - 3, depth)

        for i, (dy, dz) in enumerate(DIRECTIONS):
            copy = halo(i)[0]

            @pl.when(exists(dy, dz))
            def _(copy=copy):
                copy.wait_send()

        def z_copy(c, slot):
            return pltpu.make_async_remote_copy(
                src_ref=zsend.at[step, c], dst_ref=zbuf.at[step, slot, c], send_sem=zs.at[step, slot, c],
                recv_sem=zrs.at[step, slot, c], device_id=at(ky, kz + inward), device_id_type=MESH)

        def z_far(c):
            return pltpu.make_async_remote_copy(
                src_ref=zsend.at[step, c], dst_ref=zbuf.at[step, 0, c], send_sem=zs.at[step, 0, c],
                recv_sem=zrs.at[step, 0, c], device_id=at(ky, far), device_id_type=MESH)

        def z_raw(c):
            return pltpu.make_async_remote_copy(
                src_ref=zraw_s.at[step, c], dst_ref=zraw_r.at[step, c], send_sem=zws.at[step, c],
                recv_sem=zwr.at[step, c], device_id=at(ky, kz - inward), device_id_type=MESH)

        def z_back(c):
            return pltpu.make_async_remote_copy(
                src_ref=zvsend.at[step, c], dst_ref=zv.at[step, c], send_sem=zvs.at[step, c],
                recv_sem=zvr.at[step, c], device_id=at(ky, kz - inward), device_id_type=MESH)

        def z_inward(c, carry):
            own = pl.ds(pl.multiple_of(c * CHUNK, CHUNK), CHUNK)

            @pl.when(jnp.logical_not(outermost))
            def _():
                z_copy(c, 0).wait_recv()
                zr_ref[0, own, :] += zbuf[step, 0, c, 0]
                zr_ref[1, own, :] += zbuf[step, 0, c, 1]

            eo, ro, ei, ri, g, f = [zr_ref[j, own, :] for j in range(6)]
            s = 1.0 / (eo + g)
            w = g * s
            ei = ei + w * eo
            ri = ri + w * ro
            s2 = 1.0 / (ei + f)
            u = f * s2
            zi_ref[0, own, :] = w
            zi_ref[1, own, :] = ro * s
            zi_ref[2, own, :] = ei
            zi_ref[3, own, :] = ri
            if not direct:
                zi_ref[4, own, :] = u
                zi_ref[5, own, :] = ri * s2
            zsend[step, c, 0] = u * ei
            zsend[step, c, 1] = u * ri
            if direct:
                @pl.when(middle)
                def _():
                    z_far(c).start()
            z_copy(c, slot_out).start()
            return carry

        def z_outward(c, carry):
            own = pl.ds(pl.multiple_of(c * CHUNK, CHUNK), CHUNK)

            @pl.when(middle)
            def _():
                z_copy(c, 1).wait_recv()
                zr_ref[0, own, :] = (zi_ref[3, own, :] + zbuf[step, 1, c, 1]) / (zi_ref[2, own, :] + zbuf[step, 1, c, 0])

            @pl.when(jnp.logical_not(middle))
            def _():
                if direct:
                    z_raw(c).wait_recv()
                    z_far(c).wait_recv()
                    eo, ro, ei, ri, g = [zraw_r[step, c, j] for j in range(5)]
                    ei = ei + zbuf[step, 0, c, 0]
                    ri = ri + zbuf[step, 0, c, 1]
                    w = g / (ei + g)
                    eo = eo + w * ei
                    ro = ro + w * ri
                    f = zr_ref[5, own, :]
                    u = f / (eo + f)
                    zr_ref[0, own, :] = (zi_ref[3, own, :] + u * ro) / (zi_ref[2, own, :] + u * eo)
                else:
                    z_back(c).wait_recv()
                    zr_ref[0, own, :] = zi_ref[4, own, :] * zv[step, c] + zi_ref[5, own, :]

            vi = zr_ref[0, own, :]
            vo = zi_ref[0, own, :] * vi + zi_ref[1, own, :]

            if not direct:
                @pl.when(jnp.logical_not(outermost))
                def _():
                    zvsend[step, c] = vo
                    z_back(c).start()

            va = jnp.where(left, vo, vi)
            v = jnp.where(left, vi, vo)
            vz_ref[0, own, :] = va
            vz_ref[depth - 1, own, :] = v
            for i in range(depth - 2, 0, -1):
                v = wz_ref[0, i, own, :] * v + (wz_ref[1, i, own, :] * va + wz_ref[2, i, own, :])
                vz_ref[i, own, :] = v
            return carry

        @pl.loop(0, chunks)
        def _(c):
            y0 = pl.multiple_of(c * CHUNK, CHUNK)
            part = pl.ds(y0 + PAD, CHUNK)
            own = pl.ds(y0, CHUNK)
            d = d_ref[1, part, :]
            f_lo = jnp.where(kz > 0, d_ref[0, part, :] + d, 0.0)
            d_next = d_ref[2, part, :]
            g = d + d_next
            d = d_next
            ea = jnp.ones_like(g)
            ra = c4[HALO, part, :]
            e = ea
            r = c4[HALO + 1, part, :]
            for i in range(1, depth - 1):
                d_next = d_ref[i + 2, part, :]
                f = d + d_next
                d = d_next
                s = 1.0 / (e + g + f)
                wf, wg = f * s, g * s
                wz_ref[0, i, own, :] = wf
                wz_ref[1, i, own, :] = wg
                wz_ref[2, i, own, :] = r * s
                ea = ea + wg * e
                ra = ra + wg * r
                e = 1.0 + wf * e
                r = c4[HALO + i + 1, part, :] + wf * r
                g = wf * g
            f_hi = jnp.where(kz < nz - 1, d + d_ref[depth + 1, part, :], 0.0)
            zr_ref[0, own, :] = jnp.where(left, ea, e)
            zr_ref[1, own, :] = jnp.where(left, ra, r)
            zr_ref[2, own, :] = jnp.where(left, e, ea)
            zr_ref[3, own, :] = jnp.where(left, r, ra)
            zr_ref[4, own, :] = g
            zr_ref[5, own, :] = jnp.where(left, f_hi, f_lo)
            if direct:
                @pl.when(middle)
                def _():
                    for j in range(5):
                        zraw_s[step, c, j] = zr_ref[j, own, :]
                    z_raw(c).start()

            @pl.when(outermost)
            def _():
                z_inward(c, 0)

        def dx(i):
            return dt2[pl.ds(i, depth, stride=tall_x), :]

        def rx(i):
            return cur2[pl.ds(i, depth, stride=tall_x), :]

        def dy_(i):
            return d2[pl.ds(i + rows + PAD, depth, stride=rows), :]

        def ry(i):
            return c2[pl.ds(i + HALO * rows + PAD, depth, stride=rows), :]

        def put_x(i, v):
            vx2[pl.ds(i, depth, stride=tall_x), :] = v

        def put_y(i, v):
            vy2[pl.ds(i, depth, stride=tall_y), :] = v

        states = line_start(dy_, ry, cols)
        states = line_reduce(dy_, ry, wy_ref, cols, 1, cols // SEGMENTS - 1, states)
        chain, levels_y = line_chain(
            dy_, states, cols, lambda d: jnp.where(ky < ny - 1, d + dy_(cols), 0.0))

        y_copy = pltpu.make_async_remote_copy(
            src_ref=ysend.at[step], dst_ref=yrecv.at[step], send_sem=ys.at[step],
            recv_sem=yr.at[step], device_id=at(twin, kz), device_id_type=MESH)

        def y_spread(j):
            return pltpu.make_async_remote_copy(
                src_ref=yall.at[step, 0], dst_ref=yall.at[step, j], send_sem=yas.at[step, j],
                recv_sem=yar.at[step, j], device_id=at(member(j), kz), device_id_type=MESH)

        for j in range(6):
            ysend[step, j] = chain[j]
        y_copy.start()

        size_x = nx // SEGMENTS
        cuts = [1 + (size_x - 2) * k // chunks for k in range(chunks + 1)]

        def x_piece(k, states):
            return line_reduce(dx, rx, wx_ref, nx, cuts[k], cuts[k + 1], states)

        def z_piece(k):
            @pl.when(jnp.logical_not(outermost))
            def _():
                z_inward(k, 0)

        states = x_piece(0, line_start(dx, rx, nx))

        y_copy.wait_recv()
        other = tuple(yrecv[step, j] for j in range(6))
        first = side == 0
        pair_l = tuple(jnp.where(first, a, b) for a, b in zip(chain, other))
        pair_r = tuple(jnp.where(first, b, a) for a, b in zip(chain, other))
        (ea, ra, eb, rb, g, f), pair = merge(pair_l, pair_r)
        s = 1.0 / (eb + g + f)
        wg, wf, q = g * s, f * s, rb * s
        for j, value in enumerate((ea + wg * eb, ra + wg * rb, wf * eb, wf * rb, wf * g)):
            yall[step, 0, j] = value
        for j in range(1, groups):
            y_spread(j).start()

        for k in range(1, chunks):
            z_piece(k - 1)
            states = x_piece(k, states)
        x_chain, levels_x = line_chain(dx, states, nx, jnp.zeros_like)
        z_piece(chunks - 1)
        line_back(put_x, wx_ref, nx, unmerge_all(levels_x, *solve_pair(*x_chain[:5])))

        for j in range(1, groups):
            y_spread(j).wait_recv()
        e, r, de, dr, link = [yall[step, lax.rem(group, groups), j] for j in range(5)]
        ways = []
        for m in range(1, groups):
            s = 1.0 / (e + link)
            w = link * s
            ways.append((w, r * s))
            e, r = w * e + de, w * r + dr
            here = [yall[step, lax.rem(group - m + groups, groups), j] for j in range(5)]
            e, r = e + here[0], r + here[1]
            de, dr, link = here[2:]
        v = r / e
        yv_ref[groups] = jnp.zeros_like(v)
        yv_ref[groups - 1] = v
        for m in range(groups - 2, -1, -1):
            v = ways[m][0] * v + ways[m][1]
            yv_ref[m] = v
        va = yv_ref[group]
        vb = wg * va + (wf * yv_ref[group + 1] + q)
        inner_l, inner_r = unmerge(pair, va, vb)
        va, vb = jnp.where(first, va, inner_r), jnp.where(first, inner_l, vb)
        line_back(put_y, wy_ref, cols, unmerge_all(levels_y, va, vb))

        lax.fori_loop(0, chunks, z_outward, 0)

        y_copy.wait_send()
        for j in range(1, groups):
            y_spread(j).wait_send()

        @pl.loop(0, chunks)
        def _(c):
            z_copy(c, slot_out).wait_send()
            if direct:
                @pl.when(middle)
                def _():
                    z_far(c).wait_send()
                    z_raw(c).wait_send()
            else:
                @pl.when(jnp.logical_not(outermost))
                def _():
                    z_back(c).wait_send()

    @pl.loop(0, depth // 4)
    def _(k):
        for t in range(4):
            finish(4 * k + t, None)


def on_device(volume, contrast):
    depth, nx, cols = volume.shape
    ny = lax.axis_size("gy")
    nz = lax.axis_size("gz")
    groups = ny // 2
    assert ny % 2 == 0 and nz % 2 == 0
    rows = cols + 2 * PAD
    chunks = cols // CHUNK
    f32 = jnp.float32
    dma = pltpu.SemaphoreType.DMA
    count = len(DIRECTIONS)
    return pl.pallas_call(
        functools.partial(kernel, ny, nz),
        out_shape=jax.ShapeDtypeStruct(volume.shape, f32),
        in_specs=[pl.BlockSpec(memory_space=pltpu.VMEM)] * 2,
        out_specs=pl.BlockSpec(memory_space=pltpu.VMEM),
        scratch_shapes=[
            pltpu.VMEM((STEPS, depth + 2 * HALO, rows, nx), f32),
            pltpu.VMEM((depth + 4, rows, nx), f32),
            pltpu.VMEM((depth + 4, rows + 16, nx), f32),
            pltpu.VMEM((depth + 2, rows, nx), f32),
            pltpu.VMEM((depth, nx + SKEW, cols), f32),
            pltpu.VMEM((3, nx, depth, cols), f32),
            pltpu.VMEM((3, cols, depth, nx), f32),
            pltpu.VMEM((3, depth, cols, nx), f32),
            pltpu.VMEM((depth, nx + SKEW, cols), f32),
            pltpu.VMEM((depth, cols + SKEW, nx), f32),
            pltpu.VMEM((depth, cols, nx), f32),
            pltpu.VMEM((depth, nx + SKEW, cols), f32),
            pltpu.VMEM((6, cols, nx), f32),
            pltpu.VMEM((6, cols, nx), f32),
            pltpu.VMEM((STEPS, chunks, 2, CHUNK, nx), f32),
            pltpu.VMEM((STEPS, 2, chunks, 2, CHUNK, nx), f32),
            pltpu.VMEM((STEPS, chunks, CHUNK, nx), f32),
            pltpu.VMEM((STEPS, chunks, CHUNK, nx), f32),
            pltpu.VMEM((STEPS, chunks, 5, CHUNK, nx), f32),
            pltpu.VMEM((STEPS, chunks, 5, CHUNK, nx), f32),
            pltpu.VMEM((STEPS, 6, depth, nx), f32),
            pltpu.VMEM((STEPS, 6, depth, nx), f32),
            pltpu.VMEM((STEPS, groups, 5, depth, nx), f32),
            pltpu.VMEM((groups + 1, depth, nx), f32),
            dma((STEPS, count)), dma((STEPS, count)),
            dma((STEPS, 2, chunks)), dma((STEPS, 2, chunks)),
            dma((STEPS, chunks)), dma((STEPS, chunks)),
            dma((STEPS, chunks)), dma((STEPS, chunks)),
            dma((STEPS,)), dma((STEPS,)),
            dma((STEPS, groups)), dma((STEPS, groups)),
        ],
        compiler_params=pltpu.CompilerParams(
            collective_id=0, has_side_effects=True, vmem_limit_bytes=48 * 2 ** 20
        ),
    )(volume, contrast.reshape(1, nx))


def solution(mesh):
    in_specs = (P("gz", None, "gy"), P())
    out_specs = P("gz", None, "gy")
    return jax.shard_map(
        on_device, mesh=mesh, in_specs=in_specs, out_specs=out_specs, check_vma=False
    )
```

```python
import functools

import jax
import jax.numpy as jnp
from jax import lax
from jax.experimental import pallas as pl
from jax.experimental.pallas import tpu as pltpu
from jax.sharding import PartitionSpec as P

STEPS = 2
TAPS = (0.05448868, 0.24420134, 0.40261995, 0.24420134, 0.05448868)
SCALE = 600.0
MESH = pl.DeviceIdType.MESH
DIRECTIONS = [(dy, dz) for dz in (-1, 1, 0) for dy in (0, -1, 1) if (dy, dz) != (0, 0)]
PAD = 8
HALO = 4
CHUNK = 32
STENCIL_ROWS = 48
SEGMENTS = 4
SKEW = 8


def message_plan(cols):
    messages = []
    groups = []
    chunks = cols // CHUNK
    for c in range(chunks):
        start = c * CHUNK + PAD if c else 0
        stop = (c + 1) * CHUNK + PAD if c + 1 < chunks else cols
        group = []
        for dz in (-1, 1):
            pieces = [(0, dz, start, stop - start)]
            if c == 0:
                pieces.append((1, dz, 0, 0))
            if c + 1 == chunks:
                pieces.append((-1, dz, 0, 0))
            for piece in pieces:
                group.append(len(messages))
                messages.append(piece)
        groups.append(group)
    rows = [len(messages), len(messages) + 1]
    messages += [(-1, 0, 0, 0), (1, 0, 0, 0)]
    return messages, groups, rows


def merge(left, right):
    ea, ra, eb, rb, g, f = left
    ea2, ra2, eb2, rb2, g2, f2 = right
    s1 = 1.0 / (eb + g + f)
    wg, wf, q1 = g * s1, f * s1, rb * s1
    ea = ea + wg * eb
    ra = ra + wg * rb
    ea2 = ea2 + wf * eb
    ra2 = ra2 + wf * rb
    g1 = wf * g
    s2 = 1.0 / (ea2 + g1 + g2)
    vg, vf, q2 = g1 * s2, g2 * s2, ra2 * s2
    joined = (ea + vg * ea2, ra + vg * ra2, eb2 + vf * ea2, rb2 + vf * ra2, vf * g1, f2)
    return joined, (wg, wf, q1, vg, vf, q2)


def unmerge(weights, va, vb):
    wg, wf, q1, vg, vf, q2 = weights
    inner_right = vg * va + vf * vb + q2
    inner_left = wg * va + wf * inner_right + q1
    return inner_left, inner_right


def solve_pair(ea, ra, eb, rb, g):
    s = 1.0 / (ea + g)
    w = g * s
    vb = (rb + w * ra) / (eb + w * ea)
    return w * vb + ra * s, vb


def merge_all(chains):
    levels = []
    while len(chains) > 1:
        pairs = [merge(chains[i], chains[i + 1]) for i in range(0, len(chains), 2)]
        chains = [p[0] for p in pairs]
        levels.append([p[1] for p in pairs])
    return chains[0], levels


def unmerge_all(levels, va, vb):
    ends = [(va, vb)]
    for level in reversed(levels):
        split = []
        for weights, (a, b) in zip(level, ends):
            inner_left, inner_right = unmerge(weights, a, b)
            split += [(a, inner_left), (inner_right, b)]
        ends = split
    return ends


def line_start(get_d, get_r, count):
    states = []
    for base in range(0, count, count // SEGMENTS):
        d0, d1 = get_d(base), get_d(base + 1)
        one = jnp.ones_like(d0)
        states.append((one, get_r(base), d0 + d1, one, get_r(base + 1), d1))
    return tuple(states)


def line_reduce(get_d, get_r, weights, count, first, last, states):
    size = count // SEGMENTS

    def body(i, states):
        new = []
        for k, (ea, ra, g, e, r, d) in enumerate(states):
            j = k * size + i
            d1 = get_d(j + 1)
            f = d + d1
            s = 1.0 / (e + g + f)
            wf, wg = f * s, g * s
            weights[0, j] = wf
            weights[1, j] = wg
            weights[2, j] = r * s
            new.append((ea + wg * e, ra + wg * r, wf * g, 1.0 + wf * e, get_r(j + 1) + wf * r, d1))
        return tuple(new)

    return lax.fori_loop(first, last, body, states)


def line_chain(get_d, states, count, edge):
    size = count // SEGMENTS
    chains = []
    for k, (ea, ra, g, e, r, d) in enumerate(states):
        f = d + get_d((k + 1) * size) if k + 1 < SEGMENTS else edge(d)
        chains.append((ea, ra, e, r, g, f))
    return merge_all(chains)


def line_back(put, weights, count, ends):
    size = count // SEGMENTS
    for k, (a, b) in enumerate(ends):
        put(k * size, a)
        put(k * size + size - 1, b)

    def body(t, values):
        new = []
        for k, v in enumerate(values):
            j = k * size + size - 2 - t
            v = weights[0, j] * v + (weights[1, j] * ends[k][0] + weights[2, j])
            put(j, v)
            new.append(v)
        return tuple(new)

    lax.fori_loop(0, size - 2, body, tuple(b for a, b in ends), unroll=3)


def kernel(ny, nz, vol, con, out, c_ref, t_ref, b_ref, gx_ref, w_ref, d_ref, dt_ref, wx_ref, wy_ref, wz_ref, vx_ref, vy_ref,
           vz_ref, cur_ref, zr_ref, zi_ref, zsend, zbuf, zvsend, zv, ysend, yrecv, yall, yv_ref,
           halo_s, halo_r, zs, zrs, zvs, zvr, ys, yr, yas, yar):
    depth, nx, cols = vol.shape
    rows = cols + 2 * PAD
    tall = depth + 2 * HALO
    chunks = cols // CHUNK
    ky = lax.axis_index("gy")
    kz = lax.axis_index("gz")

    def at(y, z):
        return {"gy": y, "gz": z}

    def exists(dy, dz):
        ok = True
        if dy:
            ok = (ky + dy >= 0) & (ky + dy < ny)
        if dz:
            ok = ok & (kz + dz >= 0) & (kz + dz < nz)
        return ok

    groups = ny // 2
    side = lax.rem(ky, 2)
    group = lax.div(ky, 2)
    twin = ky + 1 - 2 * side

    def member(j):
        return 2 * lax.rem(group + j, groups) + side

    barrier = pltpu.get_barrier_semaphore()
    expected = jnp.int32(groups)
    for dy, dz in DIRECTIONS:
        ok = exists(dy, dz)
        expected = expected + jnp.where(ok, 1, 0)

        @pl.when(ok)
        def _(dy=dy, dz=dz):
            pl.semaphore_signal(barrier, inc=1, device_id=at(ky + dy, kz + dz), device_id_type=MESH)

    for y in [twin] + [member(j) for j in range(1, groups)]:
        pl.semaphore_signal(barrier, inc=1, device_id=at(y, kz), device_id_type=MESH)

    def take(z):
        plane = vol[z]
        cur_ref[z, 0:nx, :] = plane
        c_ref[0, z + HALO, PAD:PAD + cols, :] = plane.T

    @pl.loop(0, 2)
    def _(k):
        for t in range(HALO):
            take(k * (depth - HALO) + t)

    source = lax.broadcasted_iota(jnp.int32, (nx, nx), 0)
    target = lax.broadcasted_iota(jnp.int32, (nx, nx), 1)

    def taps_at(target):
        apart = jnp.where((target >= 0) & (target < nx), jnp.abs(source - target), 3)
        return jnp.where(apart == 0, TAPS[2], jnp.where(apart == 1, TAPS[1], jnp.where(apart == 2, TAPS[0], 0.0)))

    for half, matrix in enumerate((taps_at(target), taps_at(target + 1) - taps_at(target - 1))):
        part = slice(half * nx, half * nx + nx)
        coarse = matrix.astype(jnp.bfloat16)
        w_ref[0, :, part] = coarse
        w_ref[1, :, part] = (matrix - coarse.astype(jnp.float32)).astype(jnp.bfloat16)

    pl.semaphore_wait(barrier, expected)

    left = kz < nz // 2
    inward = jnp.where(left, 1, -1)
    order = jnp.where(left, kz, nz - 1 - kz)
    middle = order == nz // 2 - 1
    outermost = order == 0
    slot_out = jnp.where(middle, 1, 0)

    contrast = con[...]
    squared = jnp.broadcast_to(contrast * contrast, (STENCIL_ROWS, nx))

    tall_x = nx + SKEW
    tall_y = cols + SKEW
    cur2 = cur_ref.reshape(depth * tall_x, cols)
    dt2 = dt_ref.reshape(depth * tall_x, cols)
    vx2 = vx_ref.reshape(depth * tall_x, cols)
    vy2 = vy_ref.reshape(depth * tall_y, nx)
    d2 = d_ref.reshape((depth + 2) * rows, nx)

    def finish(z, target):
        plane = (vx_ref[z, 0:nx, :] + (vy_ref[z, 0:cols, :] + vz_ref[z]).T) * (1.0 / 3.0)
        if target is None:
            out[z] = plane
        else:
            cur_ref[z, 0:nx, :] = plane
            target[z + HALO, PAD:PAD + cols, :] = plane.T

    def finish_edges(target):
        @pl.loop(0, HALO // 2)
        def _(k):
            for t in range(2):
                finish(2 * k + t, target)
                finish(depth - HALO + 2 * k + t, target)

    def finish_middle(target):
        @pl.loop(0, (depth - 2 * HALO) // 4)
        def _(k):
            for t in range(4):
                finish(HALO + 4 * k + t, target)

    parts = [(r0, min(STENCIL_ROWS, cols + 8 - r0)) for r0 in range(0, cols + 8, STENCIL_ROWS)]

    messages, layer_groups, row_group = message_plan(cols)

    @pl.loop(0, STEPS)
    def _(step):
        c4 = c_ref.at[step]
        c2 = c4.reshape(tall * rows, nx)

        def halo(i, c4=c4, step=step):
            dy, dz, start, size = messages[i]
            src_y = {0: (PAD + start, size), 1: (cols, PAD), -1: (PAD, PAD)}[dy]
            dst_y = {0: (PAD + start, size), 1: (0, PAD), -1: (PAD + cols, PAD)}[dy]
            src_z = {0: (HALO, depth), 1: (depth, HALO), -1: (HALO, HALO)}[dz]
            dst_z = {0: (HALO, depth), 1: (0, HALO), -1: (HALO + depth, HALO)}[dz]
            src = c4.at[pl.ds(*src_z), pl.ds(*src_y), :]
            dst = c4.at[pl.ds(*dst_z), pl.ds(*dst_y), :]
            copy = pltpu.make_async_remote_copy(
                src_ref=src, dst_ref=dst, send_sem=halo_s.at[step, i], recv_sem=halo_r.at[step, i],
                device_id=at(ky + dy, kz + dz), device_id_type=MESH)
            return copy, dst_z, dst_y

        def send(batch, halo=halo, c4=c4):
            for i in batch:
                dy, dz = messages[i][:2]
                copy, dst_z, dst_y = halo(i)

                @pl.when(exists(dy, dz))
                def _(copy=copy):
                    copy.start()

                @pl.when(jnp.logical_not(exists(-dy, -dz)))
                def _(dst_z=dst_z, dst_y=dst_y):
                    c4[pl.ds(*dst_z), pl.ds(*dst_y), :] = jnp.zeros((dst_z[1], dst_y[1], nx), jnp.float32)

        def receive(batch, halo=halo):
            for i in batch:
                dy, dz = messages[i][:2]
                copy = halo(i)[0]

                @pl.when(exists(-dy, -dz))
                def _(copy=copy):
                    copy.wait_recv()

        @pl.when(step > 0)
        def _():
            finish_edges(c4)

        for batch in layer_groups:
            send(batch)

        @pl.when(step == 0)
        def _():
            @pl.loop(0, (depth - 2 * HALO) // 4)
            def _(k):
                for t in range(4):
                    take(HALO + 4 * k + t)

        @pl.when(step > 0)
        def _():
            finish_middle(c4)

        send(row_group)

        def blur_layer(z, r0, size):
            part = pl.ds(r0, size)
            total = TAPS[2] * c4[z + 2, part, :]
            total = total + TAPS[1] * (c4[z + 1, part, :] + c4[z + 3, part, :])
            total = total + TAPS[0] * (c4[z, part, :] + c4[z + 4, part, :])
            t_ref[z, pl.ds(r0, size), :] = total

        def blur_planes(planes, pieces):
            totals = []
            for z in planes:
                for r0, size in pieces:
                    def tap(o):
                        return t_ref[z, pl.ds(r0 + 4 + o, size), :]
                    totals.append(TAPS[2] * tap(0) + TAPS[1] * (tap(-1) + tap(1)) + TAPS[0] * (tap(-2) + tap(2)))
            total = jnp.concatenate(totals)
            coarse = total.astype(jnp.bfloat16)
            fine = (total - coarse.astype(jnp.float32)).astype(jnp.bfloat16)

            def times(value, k):
                return jnp.dot(value, w_ref[k], preferred_element_type=jnp.float32)

            both = times(coarse, 0) + times(fine, 0) + times(coarse, 1)
            start = 0
            for z in planes:
                for r0, size in pieces:
                    b_ref[z, pl.ds(r0, size), :] = both[start:start + size, :nx]
                    gx_ref[z, pl.ds(r0, size), :] = both[start:start + size, nx:]
                    start += size

        def blur_edges(spans, low, high):
            for row, present in ((PAD - 5, ky > 0), (cols + PAD - 4, ky < ny - 1)):
                if low <= row < high:
                    @pl.when(jnp.logical_not(present))
                    def _(row=row):
                        for z0, z1 in spans:
                            b_ref[z0:z1, row:row + 1, :] = jnp.zeros((z1 - z0, 1, nx), jnp.float32)

        def diffuse(z, r0, size):
            grad_x = gx_ref[z + 1, pl.ds(r0 + 4, size), :]
            grad_z = b_ref[z + 2, pl.ds(r0 + 4, size), :] - b_ref[z, pl.ds(r0 + 4, size), :]
            grad_y = b_ref[z + 1, pl.ds(r0 + 5, size), :] - b_ref[z + 1, pl.ds(r0 + 3, size), :]
            square = (grad_x * grad_x + grad_y * grad_y + grad_z * grad_z) * 0.25
            d_ref[z, pl.ds(r0 + PAD, size), :] = (SCALE * squared[:size]) / (squared[:size] + square)

        def turn(z0, z1):
            step_by = 2 if (z1 - z0) % 2 == 0 else 1

            @pl.loop(0, (z1 - z0) // step_by)
            def _(k):
                for t in range(step_by):
                    z = z0 + k * step_by + t
                    dt_ref[z, 0:nx, :] = d_ref[z + 1, PAD:PAD + cols, :].T

        own_rows = [(r0, min(STENCIL_ROWS, cols + PAD - r0)) for r0 in range(PAD, cols + PAD, STENCIL_ROWS)]
        halo_rows = [(0, PAD), (cols + PAD, PAD)]

        @pl.loop(HALO, depth)
        def _(z):
            for piece in own_rows:
                blur_layer(z, *piece)

        receive(row_group)

        @pl.loop(0, (depth - HALO) // 4)
        def _(k):
            for t in range(4):
                for piece in halo_rows:
                    blur_layer(HALO + 4 * k + t, *piece)

        @pl.loop(0, (depth - HALO) // 2)
        def _(k):
            blur_planes([HALO + 2 * k, HALO + 2 * k + 1], parts)

        blur_edges([(HALO, depth)], 0, cols + PAD)

        @pl.loop(0, (depth - HALO - 2) // 2)
        def _(k):
            for t in range(2):
                for piece in parts:
                    diffuse(HALO + 2 * k + t, *piece)

        turn(HALO - 1, depth - 3)

        def z_copy(c, slot):
            return pltpu.make_async_remote_copy(
                src_ref=zsend.at[step, c], dst_ref=zbuf.at[step, slot, c], send_sem=zs.at[step, slot, c],
                recv_sem=zrs.at[step, slot, c], device_id=at(ky, kz + inward), device_id_type=MESH)

        def z_back(c):
            return pltpu.make_async_remote_copy(
                src_ref=zvsend.at[step, c], dst_ref=zv.at[step, c], send_sem=zvs.at[step, c],
                recv_sem=zvr.at[step, c], device_id=at(ky, kz - inward), device_id_type=MESH)

        def z_inward(c, carry):
            own = pl.ds(pl.multiple_of(c * CHUNK, CHUNK), CHUNK)

            @pl.when(jnp.logical_not(outermost))
            def _():
                z_copy(c, 0).wait_recv()
                zr_ref[0, own, :] += zbuf[step, 0, c, 0]
                zr_ref[1, own, :] += zbuf[step, 0, c, 1]

            eo, ro, ei, ri, g, f = [zr_ref[j, own, :] for j in range(6)]
            s = 1.0 / (eo + g)
            w = g * s
            ei = ei + w * eo
            ri = ri + w * ro
            s2 = 1.0 / (ei + f)
            u = f * s2
            zi_ref[0, own, :] = w
            zi_ref[1, own, :] = ro * s
            zi_ref[2, own, :] = ei
            zi_ref[3, own, :] = ri
            zi_ref[4, own, :] = u
            zi_ref[5, own, :] = ri * s2
            zsend[step, c, 0] = u * ei
            zsend[step, c, 1] = u * ri
            z_copy(c, slot_out).start()
            return carry

        def z_outward(c, carry):
            own = pl.ds(pl.multiple_of(c * CHUNK, CHUNK), CHUNK)

            @pl.when(middle)
            def _():
                z_copy(c, 1).wait_recv()
                zr_ref[0, own, :] = (zi_ref[3, own, :] + zbuf[step, 1, c, 1]) / (zi_ref[2, own, :] + zbuf[step, 1, c, 0])

            @pl.when(jnp.logical_not(middle))
            def _():
                z_back(c).wait_recv()
                zr_ref[0, own, :] = zi_ref[4, own, :] * zv[step, c] + zi_ref[5, own, :]

            vi = zr_ref[0, own, :]
            vo = zi_ref[0, own, :] * vi + zi_ref[1, own, :]

            @pl.when(jnp.logical_not(outermost))
            def _():
                zvsend[step, c] = vo
                z_back(c).start()

            va = jnp.where(left, vo, vi)
            v = jnp.where(left, vi, vo)
            vz_ref[0, own, :] = va
            vz_ref[depth - 1, own, :] = v
            for i in range(depth - 2, 0, -1):
                v = wz_ref[0, i, own, :] * v + (wz_ref[1, i, own, :] * va + wz_ref[2, i, own, :])
                vz_ref[i, own, :] = v
            return carry

        def z_chain(c):
            y0 = c * CHUNK
            part = pl.ds(y0 + PAD, CHUNK)
            own = pl.ds(y0, CHUNK)
            d = d_ref[1, part, :]
            f_lo = jnp.where(kz > 0, d_ref[0, part, :] + d, 0.0)
            d_next = d_ref[2, part, :]
            g = d + d_next
            d = d_next
            ea = jnp.ones_like(g)
            ra = c4[HALO, part, :]
            e = ea
            r = c4[HALO + 1, part, :]
            for i in range(1, depth - 1):
                d_next = d_ref[i + 2, part, :]
                f = d + d_next
                d = d_next
                s = 1.0 / (e + g + f)
                wf, wg = f * s, g * s
                wz_ref[0, i, own, :] = wf
                wz_ref[1, i, own, :] = wg
                wz_ref[2, i, own, :] = r * s
                ea = ea + wg * e
                ra = ra + wg * r
                e = 1.0 + wf * e
                r = c4[HALO + i + 1, part, :] + wf * r
                g = wf * g
            f_hi = jnp.where(kz < nz - 1, d + d_ref[depth + 1, part, :], 0.0)
            zr_ref[0, own, :] = jnp.where(left, ea, e)
            zr_ref[1, own, :] = jnp.where(left, ra, r)
            zr_ref[2, own, :] = jnp.where(left, e, ea)
            zr_ref[3, own, :] = jnp.where(left, r, ra)
            zr_ref[4, own, :] = g
            zr_ref[5, own, :] = jnp.where(left, f_hi, f_lo)

            @pl.when(outermost)
            def _():
                z_inward(c, 0)

        outer = list(range(HALO)) + list(range(depth, depth + HALO))
        for c, batch in enumerate(layer_groups):
            start, stop = c * CHUNK, (c + 1) * CHUNK
            tail = PAD if c + 1 == chunks else 0
            receive(batch)
            t0 = start + 2 * PAD if c else 0
            for z in outer:
                blur_layer(z, t0, stop + 2 * PAD - t0)
            b0 = start + PAD if c else 0
            b1 = stop + PAD
            blur_planes(outer, [(b0, b1 - b0)])
            blur_edges([(0, HALO), (depth, depth + HALO)], b0, b1)

            @pl.when(kz == 0)
            def _(b0=b0, b1=b1):
                b_ref[1, b0:b1, :] = jnp.zeros((b1 - b0, nx), jnp.float32)

            @pl.when(kz == nz - 1)
            def _(b0=b0, b1=b1):
                b_ref[depth + 2, b0:b1, :] = jnp.zeros((b1 - b0, nx), jnp.float32)

            for z in list(range(HALO)) + list(range(depth - 2, depth + 2)):
                diffuse(z, start, stop + tail - start)
            z_chain(c)

        turn(0, HALO - 1)
        turn(depth - 3, depth)

        for i in range(len(messages)):
            dy, dz = messages[i][:2]
            copy = halo(i)[0]

            @pl.when(exists(dy, dz))
            def _(copy=copy):
                copy.wait_send()

        def dx(i):
            return dt2[pl.ds(i, depth, stride=tall_x), :]

        def rx(i):
            return cur2[pl.ds(i, depth, stride=tall_x), :]

        def dy_(i):
            return d2[pl.ds(i + rows + PAD, depth, stride=rows), :]

        def ry(i):
            return c2[pl.ds(i + HALO * rows + PAD, depth, stride=rows), :]

        def put_x(i, v):
            vx2[pl.ds(i, depth, stride=tall_x), :] = v

        def put_y(i, v):
            vy2[pl.ds(i, depth, stride=tall_y), :] = v

        states = line_start(dy_, ry, cols)
        states = line_reduce(dy_, ry, wy_ref, cols, 1, cols // SEGMENTS - 1, states)
        chain, levels_y = line_chain(
            dy_, states, cols, lambda d: jnp.where(ky < ny - 1, d + dy_(cols), 0.0))

        y_copy = pltpu.make_async_remote_copy(
            src_ref=ysend.at[step], dst_ref=yrecv.at[step], send_sem=ys.at[step],
            recv_sem=yr.at[step], device_id=at(twin, kz), device_id_type=MESH)

        def y_spread(j):
            return pltpu.make_async_remote_copy(
                src_ref=yall.at[step, 0], dst_ref=yall.at[step, j], send_sem=yas.at[step, j],
                recv_sem=yar.at[step, j], device_id=at(member(j), kz), device_id_type=MESH)

        for j in range(6):
            ysend[step, j] = chain[j]
        y_copy.start()

        size_x = nx // SEGMENTS
        cuts = [1 + (size_x - 2) * k // chunks for k in range(chunks + 1)]

        def x_piece(k, states):
            return line_reduce(dx, rx, wx_ref, nx, cuts[k], cuts[k + 1], states)

        def z_piece(k):
            @pl.when(jnp.logical_not(outermost))
            def _():
                z_inward(k, 0)

        states = x_piece(0, line_start(dx, rx, nx))

        y_copy.wait_recv()
        other = tuple(yrecv[step, j] for j in range(6))
        first = side == 0
        pair_l = tuple(jnp.where(first, a, b) for a, b in zip(chain, other))
        pair_r = tuple(jnp.where(first, b, a) for a, b in zip(chain, other))
        (ea, ra, eb, rb, g, f), pair = merge(pair_l, pair_r)
        s = 1.0 / (eb + g + f)
        wg, wf, q = g * s, f * s, rb * s
        for j, value in enumerate((ea + wg * eb, ra + wg * rb, wf * eb, wf * rb, wf * g)):
            yall[step, 0, j] = value
        for j in range(1, groups):
            y_spread(j).start()

        for k in range(1, chunks):
            z_piece(k - 1)
            states = x_piece(k, states)
        x_chain, levels_x = line_chain(dx, states, nx, jnp.zeros_like)
        z_piece(chunks - 1)
        line_back(put_x, wx_ref, nx, unmerge_all(levels_x, *solve_pair(*x_chain[:5])))

        @pl.when(jnp.logical_not(outermost))
        def _():
            lax.fori_loop(0, chunks, z_outward, 0)

        for j in range(1, groups):
            y_spread(j).wait_recv()
        e, r, de, dr, link = [yall[step, lax.rem(group, groups), j] for j in range(5)]
        ways = []
        for m in range(1, groups):
            s = 1.0 / (e + link)
            w = link * s
            ways.append((w, r * s))
            e, r = w * e + de, w * r + dr
            here = [yall[step, lax.rem(group - m + groups, groups), j] for j in range(5)]
            e, r = e + here[0], r + here[1]
            de, dr, link = here[2:]
        v = r / e
        yv_ref[groups] = jnp.zeros_like(v)
        yv_ref[groups - 1] = v
        for m in range(groups - 2, -1, -1):
            v = ways[m][0] * v + ways[m][1]
            yv_ref[m] = v
        va = yv_ref[group]
        vb = wg * va + (wf * yv_ref[group + 1] + q)
        inner_l, inner_r = unmerge(pair, va, vb)
        va, vb = jnp.where(first, va, inner_r), jnp.where(first, inner_l, vb)
        line_back(put_y, wy_ref, cols, unmerge_all(levels_y, va, vb))

        @pl.when(outermost)
        def _():
            lax.fori_loop(0, chunks, z_outward, 0)

        y_copy.wait_send()
        for j in range(1, groups):
            y_spread(j).wait_send()

        @pl.loop(0, chunks)
        def _(c):
            z_copy(c, slot_out).wait_send()

            @pl.when(jnp.logical_not(outermost))
            def _():
                z_back(c).wait_send()

    @pl.loop(0, depth // 4)
    def _(k):
        for t in range(4):
            finish(4 * k + t, None)


def on_device(volume, contrast):
    depth, nx, cols = volume.shape
    ny = lax.axis_size("gy")
    nz = lax.axis_size("gz")
    groups = ny // 2
    assert ny % 2 == 0 and nz % 2 == 0
    rows = cols + 2 * PAD
    chunks = cols // CHUNK
    f32 = jnp.float32
    dma = pltpu.SemaphoreType.DMA
    count = len(message_plan(cols)[0])
    return pl.pallas_call(
        functools.partial(kernel, ny, nz),
        out_shape=jax.ShapeDtypeStruct(volume.shape, f32),
        in_specs=[pl.BlockSpec(memory_space=pltpu.VMEM)] * 2,
        out_specs=pl.BlockSpec(memory_space=pltpu.VMEM),
        scratch_shapes=[
            pltpu.VMEM((STEPS, depth + 2 * HALO, rows, nx), f32),
            pltpu.VMEM((depth + 4, rows, nx), f32),
            pltpu.VMEM((depth + 4, rows + 16, nx), f32),
            pltpu.VMEM((depth + 4, rows, nx), f32),
            pltpu.VMEM((2, nx, 2 * nx), jnp.bfloat16),
            pltpu.VMEM((depth + 2, rows, nx), f32),
            pltpu.VMEM((depth, nx + SKEW, cols), f32),
            pltpu.VMEM((3, nx, depth, cols), f32),
            pltpu.VMEM((3, cols, depth, nx), f32),
            pltpu.VMEM((3, depth, cols, nx), f32),
            pltpu.VMEM((depth, nx + SKEW, cols), f32),
            pltpu.VMEM((depth, cols + SKEW, nx), f32),
            pltpu.VMEM((depth, cols, nx), f32),
            pltpu.VMEM((depth, nx + SKEW, cols), f32),
            pltpu.VMEM((6, cols, nx), f32),
            pltpu.VMEM((6, cols, nx), f32),
            pltpu.VMEM((STEPS, chunks, 2, CHUNK, nx), f32),
            pltpu.VMEM((STEPS, 2, chunks, 2, CHUNK, nx), f32),
            pltpu.VMEM((STEPS, chunks, CHUNK, nx), f32),
            pltpu.VMEM((STEPS, chunks, CHUNK, nx), f32),
            pltpu.VMEM((STEPS, 6, depth, nx), f32),
            pltpu.VMEM((STEPS, 6, depth, nx), f32),
            pltpu.VMEM((STEPS, groups, 5, depth, nx), f32),
            pltpu.VMEM((groups + 1, depth, nx), f32),
            dma((STEPS, count)), dma((STEPS, count)),
            dma((STEPS, 2, chunks)), dma((STEPS, 2, chunks)),
            dma((STEPS, chunks)), dma((STEPS, chunks)),
            dma((STEPS,)), dma((STEPS,)),
            dma((STEPS, groups)), dma((STEPS, groups)),
        ],
        compiler_params=pltpu.CompilerParams(
            collective_id=0, has_side_effects=True, vmem_limit_bytes=48 * 2 ** 20
        ),
    )(volume, contrast.reshape(1, nx))


def solution(mesh):
    in_specs = (P("gz", None, "gy"), P())
    out_specs = P("gz", None, "gy")
    return jax.shard_map(
        on_device, mesh=mesh, in_specs=in_specs, out_specs=out_specs, check_vma=False
    )
```

```python
import functools

import jax
import jax.numpy as jnp
from jax import lax
from jax.experimental import pallas as pl
from jax.experimental.pallas import tpu as pltpu
from jax.sharding import PartitionSpec as P

STEPS = 2
TAPS = (0.05448868, 0.24420134, 0.40261995, 0.24420134, 0.05448868)
SCALE = 600.0
MESH = pl.DeviceIdType.MESH
DIRECTIONS = [(dy, dz) for dz in (-1, 1, 0) for dy in (0, -1, 1) if (dy, dz) != (0, 0)]
PAD = 8
HALO = 4
CHUNK = 32
STENCIL_ROWS = 48
SEGMENTS = 4
SEGMENTS_Y = 8
BATCH = 8
SKEW = 8


def message_plan(cols):
    chunks = cols // CHUNK
    last = chunks - 1
    messages, sends, needs, edge_rows = [], [[] for _ in range(chunks)], [[] for _ in range(chunks)], []

    def add(message, sent, needed):
        sends[sent].append(len(messages))
        (edge_rows if needed is None else needs[needed]).append(len(messages))
        messages.append(message)

    add((-1, 0, 0, 0), 0, None)
    add((1, 0, 0, 0), last, None)
    for dz in (-1, 1):
        add((1, dz, 0, 0), last, 0)
        add((-1, dz, 0, 0), 0, last)
    starts = [c * CHUNK for c in range(chunks)] + [last * CHUNK + PAD]
    for start, stop in zip(starts, starts[1:] + [cols]):
        for dz in (-1, 1):
            needed = max(0, (start - PAD) // CHUNK) if start < last * CHUNK + PAD else last
            add((0, dz, start, stop - start), start // CHUNK, needed)
    return messages, sends, needs, edge_rows


def merge(left, right):
    ea, ra, eb, rb, g, f = left
    ea2, ra2, eb2, rb2, g2, f2 = right
    s1 = 1.0 / (eb + g + f)
    wg, wf, q1 = g * s1, f * s1, rb * s1
    ea = ea + wg * eb
    ra = ra + wg * rb
    ea2 = ea2 + wf * eb
    ra2 = ra2 + wf * rb
    g1 = wf * g
    s2 = 1.0 / (ea2 + g1 + g2)
    vg, vf, q2 = g1 * s2, g2 * s2, ra2 * s2
    joined = (ea + vg * ea2, ra + vg * ra2, eb2 + vf * ea2, rb2 + vf * ra2, vf * g1, f2)
    return joined, (wg, wf, q1, vg, vf, q2)


def unmerge(weights, va, vb):
    wg, wf, q1, vg, vf, q2 = weights
    inner_right = vg * va + vf * vb + q2
    inner_left = wg * va + wf * inner_right + q1
    return inner_left, inner_right


def solve_pair(ea, ra, eb, rb, g):
    s = 1.0 / (ea + g)
    w = g * s
    vb = (rb + w * ra) / (eb + w * ea)
    return w * vb + ra * s, vb


def merge_all(chains):
    levels = []
    while len(chains) > 1:
        pairs = [merge(chains[i], chains[i + 1]) for i in range(0, len(chains), 2)]
        chains = [p[0] for p in pairs]
        levels.append([p[1] for p in pairs])
    return chains[0], levels


def unmerge_all(levels, va, vb):
    ends = [(va, vb)]
    for level in reversed(levels):
        split = []
        for weights, (a, b) in zip(level, ends):
            inner_left, inner_right = unmerge(weights, a, b)
            split += [(a, inner_left), (inner_right, b)]
        ends = split
    return ends


def line_start(get_d, get_r, count, segments):
    states = []
    for base in range(0, count, count // segments):
        d0, d1 = get_d(base), get_d(base + 1)
        one = jnp.ones_like(d0)
        states.append((one, get_r(base), d0 + d1, one, get_r(base + 1), d1))
    return tuple(states)


def line_reduce(get_d, get_r, weights, count, segments):
    size = count // segments

    def body(i, states):
        new = []
        for k, (ea, ra, g, e, r, d) in enumerate(states):
            j = k * size + i
            d1 = get_d(j + 1)
            f = d + d1
            s = 1.0 / (e + g + f)
            wf, wg = f * s, g * s
            weights[0, j] = wf
            weights[1, j] = wg
            weights[2, j] = r * s
            new.append((ea + wg * e, ra + wg * r, wf * g, 1.0 + wf * e, get_r(j + 1) + wf * r, d1))
        return tuple(new)

    return lax.fori_loop(1, size - 1, body, line_start(get_d, get_r, count, segments))


def line_chain(get_d, states, count, edge):
    segments = len(states)
    size = count // segments
    chains = []
    for k, (ea, ra, g, e, r, d) in enumerate(states):
        f = d + get_d((k + 1) * size) if k + 1 < segments else edge(d)
        chains.append((ea, ra, e, r, g, f))
    return merge_all(chains)


def line_back(put, weights, count, ends):
    size = count // len(ends)
    for k, (a, b) in enumerate(ends):
        put(k * size, a)
        put(k * size + size - 1, b)

    def body(t, values):
        new = []
        for k, v in enumerate(values):
            j = k * size + size - 2 - t
            v = weights[0, j] * v + (weights[1, j] * ends[k][0] + weights[2, j])
            put(j, v)
            new.append(v)
        return tuple(new)

    lax.fori_loop(0, size - 2, body, tuple(b for a, b in ends), unroll=3 if (size - 2) % 3 == 0 else 2)


def kernel(ny, nz, vol, con, out, c_ref, t_ref, b_ref, gx_ref, w_ref, d_ref, dt_ref, wx_ref, wy_ref, wz_ref, vx_ref, vy_ref,
           xt_ref, ce_ref, cur_ref, zr_ref, zi_ref, zsend, zbuf, zvsend, zv, ysend, yrecv, yall, yv_ref,
           halo_s, halo_r, zs, zrs, zvs, zvr, ys, yr, yas, yar):
    depth, nx, cols = vol.shape
    rows = cols + 3 * PAD
    tall = depth + 2 * HALO
    chunks = cols // CHUNK
    ky = lax.axis_index("gy")
    kz = lax.axis_index("gz")

    def at(y, z):
        return {"gy": y, "gz": z}

    def exists(dy, dz):
        ok = True
        if dy:
            ok = (ky + dy >= 0) & (ky + dy < ny)
        if dz:
            ok = ok & (kz + dz >= 0) & (kz + dz < nz)
        return ok

    groups = ny // 2
    side = lax.rem(ky, 2)
    group = lax.div(ky, 2)
    twin = ky + 1 - 2 * side

    def member(j):
        return 2 * lax.rem(group + j, groups) + side

    barrier = pltpu.get_barrier_semaphore()
    expected = jnp.int32(groups)
    for dy, dz in DIRECTIONS:
        ok = exists(dy, dz)
        expected = expected + jnp.where(ok, 1, 0)

        @pl.when(ok)
        def _(dy=dy, dz=dz):
            pl.semaphore_signal(barrier, inc=1, device_id=at(ky + dy, kz + dz), device_id_type=MESH)

    for y in [twin] + [member(j) for j in range(1, groups)]:
        pl.semaphore_signal(barrier, inc=1, device_id=at(y, kz), device_id_type=MESH)

    def take(z):
        plane = vol[z]
        cur_ref[z, 0:nx, :] = plane
        c_ref[0, z + HALO, PAD:PAD + cols, :] = plane.T

    @pl.loop(0, depth // 4)
    def _(k):
        for t in range(4):
            take(4 * k + t)

    source = lax.broadcasted_iota(jnp.int32, (nx, nx), 0)
    target = lax.broadcasted_iota(jnp.int32, (nx, nx), 1)

    def taps_at(target):
        apart = jnp.where((target >= 0) & (target < nx), jnp.abs(source - target), 3)
        return jnp.where(apart == 0, TAPS[2], jnp.where(apart == 1, TAPS[1], jnp.where(apart == 2, TAPS[0], 0.0)))

    for half, matrix in enumerate((taps_at(target), taps_at(target + 1) - taps_at(target - 1))):
        part = slice(half * nx, half * nx + nx)
        coarse = matrix.astype(jnp.bfloat16)
        w_ref[0, :, part] = coarse
        w_ref[1, :, part] = (matrix - coarse.astype(jnp.float32)).astype(jnp.bfloat16)

    pl.semaphore_wait(barrier, expected)

    left = kz < nz // 2
    inward = jnp.where(left, 1, -1)
    order = jnp.where(left, kz, nz - 1 - kz)
    middle = order == nz // 2 - 1
    outermost = order == 0
    slot_out = jnp.where(middle, 1, 0)

    contrast = con[...]
    squared = jnp.broadcast_to(contrast * contrast, (STENCIL_ROWS, nx))

    tall_x = nx + SKEW
    tall_y = cols + SKEW
    cur2 = cur_ref.reshape(depth * tall_x, cols)
    dt2 = dt_ref.reshape(depth * tall_x, cols)
    vx2 = vx_ref.reshape(depth * tall_x, cols)
    vy2 = vy_ref.reshape(depth * tall_y, nx)
    d2 = d_ref.reshape((depth + 2) * rows, nx)
    ce2 = ce_ref.reshape(BATCH * tall_y, nx)

    def place(z):
        if z < 0 or z >= depth:
            return depth if z < 0 else depth + 1
        if z < HALO:
            return z
        return z - BATCH if z >= depth - HALO else z + HALO

    messages, sends, needs, edge_rows = message_plan(cols)

    def halo(i, slot):
        dy, dz, start, size = messages[i]
        src_y = {0: (PAD + start, size), 1: (cols, PAD), -1: (PAD, PAD)}[dy]
        dst_y = {0: (PAD + start, size), 1: (0, PAD), -1: (PAD + cols, PAD)}[dy]
        src_z = {0: (HALO, depth), 1: (depth, HALO), -1: (HALO, HALO)}[dz]
        dst_z = {0: (HALO, depth), 1: (0, HALO), -1: (HALO + depth, HALO)}[dz]
        volume = c_ref.at[slot]
        copy = pltpu.make_async_remote_copy(
            src_ref=volume.at[pl.ds(*src_z), pl.ds(*src_y), :], dst_ref=volume.at[pl.ds(*dst_z), pl.ds(*dst_y), :],
            send_sem=halo_s.at[slot, i], recv_sem=halo_r.at[slot, i],
            device_id=at(ky + dy, kz + dz), device_id_type=MESH)
        return copy, dst_z, dst_y

    def send(batch, slot):
        for i in batch:
            dy, dz = messages[i][:2]
            copy, dst_z, dst_y = halo(i, slot)

            @pl.when(exists(dy, dz))
            def _(copy=copy):
                copy.start()

            @pl.when(jnp.logical_not(exists(-dy, -dz)))
            def _(dst_z=dst_z, dst_y=dst_y):
                c_ref[slot, pl.ds(*dst_z), pl.ds(*dst_y), :] = jnp.zeros((dst_z[1], dst_y[1], nx), jnp.float32)

    def receive(batch, slot):
        for i in batch:
            dy, dz = messages[i][:2]
            copy = halo(i, slot)[0]

            @pl.when(exists(-dy, -dz))
            def _(copy=copy):
                copy.wait_recv()

    send(range(len(messages)), 0)

    @pl.loop(0, STEPS)
    def _(step):
        c4 = c_ref.at[step]
        c2 = c4.reshape(tall * rows, nx)
        later = lax.rem(step + 1, STEPS)

        def blur_layer(z, r0, size):
            part = pl.ds(r0, size)
            total = TAPS[2] * c4[z + 2, part, :]
            total = total + TAPS[1] * (c4[z + 1, part, :] + c4[z + 3, part, :])
            total = total + TAPS[0] * (c4[z, part, :] + c4[z + 4, part, :])
            t_ref[z, pl.ds(r0, size), :] = total

        def blur_planes(planes, pieces):
            totals = []
            for z in planes:
                for r0, size in pieces:
                    def tap(o):
                        return t_ref[z, pl.ds(r0 + 4 + o, size), :]
                    totals.append(TAPS[2] * tap(0) + TAPS[1] * (tap(-1) + tap(1)) + TAPS[0] * (tap(-2) + tap(2)))
            total = jnp.concatenate(totals)
            coarse = total.astype(jnp.bfloat16)
            fine = (total - coarse.astype(jnp.float32)).astype(jnp.bfloat16)

            def times(value, k):
                return jnp.dot(value, w_ref[k], preferred_element_type=jnp.float32)

            both = times(coarse, 0) + times(fine, 0) + times(coarse, 1)
            start = 0
            for z in planes:
                for r0, size in pieces:
                    b_ref[z, pl.ds(r0, size), :] = both[start:start + size, :nx]
                    gx_ref[z, pl.ds(r0, size), :] = both[start:start + size, nx:]
                    start += size

        def blur_edges(spans, low, high):
            for row, present in ((PAD - 5, ky > 0), (cols + PAD - 4, ky < ny - 1)):
                if low <= row < high:
                    @pl.when(jnp.logical_not(present))
                    def _(row=row):
                        for z0, z1 in spans:
                            b_ref[z0:z1, row:row + 1, :] = jnp.zeros((z1 - z0, 1, nx), jnp.float32)

        def diffuse(z, r0, size, spot=None):
            grad_x = gx_ref[z + 1, pl.ds(r0 + 4, size), :]
            grad_z = b_ref[z + 2, pl.ds(r0 + 4, size), :] - b_ref[z, pl.ds(r0 + 4, size), :]
            grad_y = b_ref[z + 1, pl.ds(r0 + 5, size), :] - b_ref[z + 1, pl.ds(r0 + 3, size), :]
            square = (grad_x * grad_x + grad_y * grad_y + grad_z * grad_z) * 0.25
            d_ref[place(z - 1) if spot is None else spot, pl.ds(r0 + PAD, size), :] = (SCALE * squared[:size]) / (squared[:size] + square)

        inner = list(range(HALO, depth))
        own_rows = [(r0, min(STENCIL_ROWS, cols + PAD - r0)) for r0 in range(PAD, cols + PAD, STENCIL_ROWS)]
        bulk = [(r0, min(STENCIL_ROWS, cols - r0)) for r0 in range(PAD, cols, STENCIL_ROWS)]
        bulk_d = [(r0, min(STENCIL_ROWS, cols - PAD - r0)) for r0 in range(PAD, cols - PAD, STENCIL_ROWS)]

        @pl.loop(HALO, depth)
        def _(z):
            for piece in own_rows:
                blur_layer(z, *piece)

        @pl.loop(0, (depth - HALO) // 2)
        def _(k):
            blur_planes([HALO + 2 * k, HALO + 2 * k + 1], bulk)

        for piece in bulk_d:
            diffuse(HALO, *piece)
            diffuse(depth - HALO + 1, *piece)

        @pl.loop(0, BATCH // 2)
        def _(k):
            for t in range(2):
                for piece in bulk_d:
                    diffuse(HALO + 1 + 2 * k + t, *piece, BATCH + 2 * k + t)

        @pl.loop(0, 2)
        def _(k):
            for t in range(HALO):
                ce_ref[HALO * k + t, 0:cols, :] = c4[HALO + (depth - HALO) * k + t, PAD:PAD + cols, :]

        @pl.when(step > 0)
        def _():
            @pl.loop(0, depth // 4)
            def _(k):
                for t in range(4):
                    z = 4 * k + t
                    cur_ref[z, 0:nx, :] = c4[z + HALO, PAD:PAD + cols, :].T

        receive(edge_rows, step)
        for z in inner:
            blur_layer(z, 0, PAD)
            blur_layer(z, cols + PAD, PAD)
        blur_planes(inner, [(0, PAD), (cols, PAD)])
        blur_edges([(HALO, depth)], 0, cols + PAD)
        for z in range(HALO, depth - 2):
            diffuse(z, 0, PAD)
            diffuse(z, cols - PAD, 2 * PAD)

        def y_at(b):
            def get_d(i):
                return d2[pl.ds(i + b * BATCH * rows + PAD, BATCH, stride=rows), :]

            def get_r(i):
                if b:
                    return c2[pl.ds(i + 2 * HALO * rows + PAD, BATCH, stride=rows), :]
                return ce2[pl.ds(i, BATCH, stride=tall_y), :]

            def put(i, v):
                vy2[pl.ds(i + b * BATCH * tall_y, BATCH, stride=tall_y), :] = v

            return get_d, get_r, put

        def y_copy(b):
            return pltpu.make_async_remote_copy(
                src_ref=ysend.at[step, b], dst_ref=yrecv.at[step, b], send_sem=ys.at[step, b],
                recv_sem=yr.at[step, b], device_id=at(twin, kz), device_id_type=MESH)

        def y_spread(b, j):
            return pltpu.make_async_remote_copy(
                src_ref=yall.at[step, b, 0], dst_ref=yall.at[step, b, j], send_sem=yas.at[step, b, j],
                recv_sem=yar.at[step, b, j], device_id=at(member(j), kz), device_id_type=MESH)

        first = side == 0
        held = [None, None]

        def y_begin(b):
            get_d, get_r, _ = y_at(b)
            states = line_reduce(get_d, get_r, wy_ref.at[b], cols, SEGMENTS_Y)
            chain, levels = line_chain(
                get_d, states, cols, lambda d: jnp.where(ky < ny - 1, d + get_d(cols), 0.0))
            for j in range(6):
                ysend[step, b, j] = chain[j]
            y_copy(b).start()
            held[b] = levels

        def y_join(b):
            chain = tuple(ysend[step, b, j] for j in range(6))
            y_copy(b).wait_recv()
            other = tuple(yrecv[step, b, j] for j in range(6))
            pair_l = tuple(jnp.where(first, a, b) for a, b in zip(chain, other))
            pair_r = tuple(jnp.where(first, b, a) for a, b in zip(chain, other))
            (ea, ra, eb, rb, g, f), pair = merge(pair_l, pair_r)
            s = 1.0 / (eb + g + f)
            wg, wf, q = g * s, f * s, rb * s
            for j, value in enumerate((ea + wg * eb, ra + wg * rb, wf * eb, wf * rb, wf * g)):
                yall[step, b, 0, j] = value
            for j in range(1, groups):
                y_spread(b, j).start()
            held[b] = (held[b], pair, wg, wf, q)

        def y_end(b):
            levels, pair, wg, wf, q = held[b]
            for j in range(1, groups):
                y_spread(b, j).wait_recv()
            e, r, de, dr, link = [yall[step, b, lax.rem(group, groups), j] for j in range(5)]
            ways = []
            for m in range(1, groups):
                s = 1.0 / (e + link)
                w = link * s
                ways.append((w, r * s))
                e, r = w * e + de, w * r + dr
                here = [yall[step, b, lax.rem(group - m + groups, groups), j] for j in range(5)]
                e, r = e + here[0], r + here[1]
                de, dr, link = here[2:]
            v = r / e
            yv_ref[b, groups] = jnp.zeros_like(v)
            yv_ref[b, groups - 1] = v
            for m in range(groups - 2, -1, -1):
                v = ways[m][0] * v + ways[m][1]
                yv_ref[b, m] = v
            va = yv_ref[b, group]
            vb = wg * va + (wf * yv_ref[b, group + 1] + q)
            inner_l, inner_r = unmerge(pair, va, vb)
            va, vb = jnp.where(first, va, inner_r), jnp.where(first, inner_l, vb)
            line_back(y_at(b)[2], wy_ref.at[b], cols, unmerge_all(levels, va, vb))

        def turn(b):
            @pl.loop(0, 2)
            def _(k):
                for t in range(HALO):
                    z = HALO + HALO * k + t if b else (depth - HALO) * k + t
                    dt_ref[z, 0:nx, :] = d_ref[b * BATCH + HALO * k + t, PAD:PAD + cols, :].T

        y_begin(1)
        turn(1)

        def z_copy(c, slot):
            return pltpu.make_async_remote_copy(
                src_ref=zsend.at[step, c], dst_ref=zbuf.at[step, slot, c], send_sem=zs.at[step, slot, c],
                recv_sem=zrs.at[step, slot, c], device_id=at(ky, kz + inward), device_id_type=MESH)

        def z_back(c):
            return pltpu.make_async_remote_copy(
                src_ref=zvsend.at[step, c], dst_ref=zv.at[step, c], send_sem=zvs.at[step, c],
                recv_sem=zvr.at[step, c], device_id=at(ky, kz - inward), device_id_type=MESH)

        def z_inward(c, carry):
            own = pl.ds(pl.multiple_of(c * CHUNK, CHUNK), CHUNK)

            @pl.when(jnp.logical_not(outermost))
            def _():
                z_copy(c, 0).wait_recv()
                zr_ref[0, own, :] += zbuf[step, 0, c, 0]
                zr_ref[1, own, :] += zbuf[step, 0, c, 1]

            eo, ro, ei, ri, g, f = [zr_ref[j, own, :] for j in range(6)]
            s = 1.0 / (eo + g)
            w = g * s
            ei = ei + w * eo
            ri = ri + w * ro
            s2 = 1.0 / (ei + f)
            u = f * s2
            zi_ref[0, own, :] = w
            zi_ref[1, own, :] = ro * s
            zi_ref[2, own, :] = ei
            zi_ref[3, own, :] = ri
            zi_ref[4, own, :] = u
            zi_ref[5, own, :] = ri * s2
            zsend[step, c, 0] = u * ei
            zsend[step, c, 1] = u * ri
            z_copy(c, slot_out).start()
            return carry

        def z_solve(c):
            own = pl.ds(pl.multiple_of(c * CHUNK, CHUNK), CHUNK)

            @pl.when(middle)
            def _():
                z_copy(c, 1).wait_recv()
                zr_ref[0, own, :] = (zi_ref[3, own, :] + zbuf[step, 1, c, 1]) / (zi_ref[2, own, :] + zbuf[step, 1, c, 0])

            @pl.when(jnp.logical_not(middle))
            def _():
                z_back(c).wait_recv()
                zr_ref[0, own, :] = zi_ref[4, own, :] * zv[step, c] + zi_ref[5, own, :]

            vo = zi_ref[0, own, :] * zr_ref[0, own, :] + zi_ref[1, own, :]
            zr_ref[1, own, :] = vo

            @pl.when(jnp.logical_not(outermost))
            def _():
                zvsend[step, c] = vo
                z_back(c).start()

        def z_finish(c):
            own = pl.ds(c * CHUNK, CHUNK)
            padded = pl.ds(c * CHUNK + PAD, CHUNK)

            def put(i, v):
                c_ref[later, HALO + i, padded, :] = (vy_ref[place(i), own, :] + xt_ref[i, own, :] + v) * (1.0 / 3.0)

            vi, vo = zr_ref[0, own, :], zr_ref[1, own, :]
            va = jnp.where(left, vo, vi)
            v = jnp.where(left, vi, vo)
            put(0, va)
            put(depth - 1, v)
            for i in range(depth - 2, 0, -1):
                v = wz_ref[0, i, own, :] * v + (wz_ref[1, i, own, :] * va + wz_ref[2, i, own, :])
                put(i, v)

        def z_chain(c):
            y0 = c * CHUNK
            part = pl.ds(y0 + PAD, CHUNK)
            own = pl.ds(y0, CHUNK)
            d = d_ref[place(0), part, :]
            f_lo = jnp.where(kz > 0, d_ref[place(-1), part, :] + d, 0.0)
            d_next = d_ref[place(1), part, :]
            g = d + d_next
            d = d_next
            ea = jnp.ones_like(g)
            ra = c4[HALO, part, :]
            e = ea
            r = c4[HALO + 1, part, :]
            for i in range(1, depth - 1):
                d_next = d_ref[place(i + 1), part, :]
                f = d + d_next
                d = d_next
                s = 1.0 / (e + g + f)
                wf, wg = f * s, g * s
                wz_ref[0, i, own, :] = wf
                wz_ref[1, i, own, :] = wg
                wz_ref[2, i, own, :] = r * s
                ea = ea + wg * e
                ra = ra + wg * r
                e = 1.0 + wf * e
                r = c4[HALO + i + 1, part, :] + wf * r
                g = wf * g
            f_hi = jnp.where(kz < nz - 1, d + d_ref[place(depth), part, :], 0.0)
            zr_ref[0, own, :] = jnp.where(left, ea, e)
            zr_ref[1, own, :] = jnp.where(left, ra, r)
            zr_ref[2, own, :] = jnp.where(left, e, ea)
            zr_ref[3, own, :] = jnp.where(left, r, ra)
            zr_ref[4, own, :] = g
            zr_ref[5, own, :] = jnp.where(left, f_hi, f_lo)

            @pl.when(outermost)
            def _():
                z_inward(c, 0)

        outer = list(range(HALO)) + list(range(depth, depth + HALO))
        for c, batch in enumerate(needs):
            start, stop = c * CHUNK, (c + 1) * CHUNK
            tail = PAD if c + 1 == chunks else 0
            receive(batch, step)
            t0 = start + 2 * PAD if c else 0
            for z in outer:
                blur_layer(z, t0, stop + 2 * PAD - t0)
            b0 = start + PAD if c else 0
            b1 = stop + PAD
            blur_planes(outer, [(b0, b1 - b0)])
            blur_edges([(0, HALO), (depth, depth + HALO)], b0, b1)

            @pl.when(kz == 0)
            def _(b0=b0, b1=b1):
                b_ref[1, b0:b1, :] = jnp.zeros((b1 - b0, nx), jnp.float32)

            @pl.when(kz == nz - 1)
            def _(b0=b0, b1=b1):
                b_ref[depth + 2, b0:b1, :] = jnp.zeros((b1 - b0, nx), jnp.float32)

            for z in list(range(HALO)) + list(range(depth - 2, depth + 2)):
                diffuse(z, start, stop + tail - start)
            z_chain(c)
            if c == 0:
                y_join(1)

        def dx(i):
            return dt2[pl.ds(i, depth, stride=tall_x), :]

        def rx(i):
            return cur2[pl.ds(i, depth, stride=tall_x), :]

        def put_x(i, v):
            vx2[pl.ds(i, depth, stride=tall_x), :] = v

        y_begin(0)
        turn(0)
        y_join(0)

        def z_piece(k):
            @pl.when(jnp.logical_not(outermost))
            def _():
                z_inward(k, 0)

        for k in range(chunks):
            z_piece(k)

        states = line_reduce(dx, rx, wx_ref, nx, SEGMENTS)
        x_chain, levels_x = line_chain(dx, states, nx, jnp.zeros_like)
        line_back(put_x, wx_ref, nx, unmerge_all(levels_x, *solve_pair(*x_chain[:5])))

        @pl.loop(0, depth // 4)
        def _(k):
            for t in range(4):
                z = 4 * k + t
                xt_ref[z] = vx_ref[z, 0:nx, :].T

        @pl.when(jnp.logical_not(outermost))
        def _():
            @pl.loop(0, chunks)
            def _(c):
                z_solve(c)

        y_end(1)
        y_end(0)

        for c in range(chunks):
            @pl.when(outermost)
            def _(c=c):
                z_solve(c)

            z_finish(c)

            @pl.when(step + 1 < STEPS)
            def _(c=c):
                send(sends[c], later)

        for b in range(2):
            y_copy(b).wait_send()
            for j in range(1, groups):
                y_spread(b, j).wait_send()

        for i in range(len(messages)):
            dy, dz = messages[i][:2]
            copy = halo(i, step)[0]

            @pl.when(exists(dy, dz))
            def _(copy=copy):
                copy.wait_send()

        @pl.loop(0, chunks)
        def _(c):
            z_copy(c, slot_out).wait_send()

            @pl.when(jnp.logical_not(outermost))
            def _():
                z_back(c).wait_send()

    @pl.loop(0, depth // 4)
    def _(k):
        for t in range(4):
            z = 4 * k + t
            out[z] = c_ref[0, z + HALO, PAD:PAD + cols, :].T


def on_device(volume, contrast):
    depth, nx, cols = volume.shape
    ny = lax.axis_size("gy")
    nz = lax.axis_size("gz")
    groups = ny // 2
    assert ny % 2 == 0 and nz % 2 == 0 and depth == 2 * BATCH == 4 * HALO
    rows = cols + 3 * PAD
    chunks = cols // CHUNK
    f32 = jnp.float32
    dma = pltpu.SemaphoreType.DMA
    count = len(message_plan(cols)[0])
    return pl.pallas_call(
        functools.partial(kernel, ny, nz),
        out_shape=jax.ShapeDtypeStruct(volume.shape, f32),
        in_specs=[pl.BlockSpec(memory_space=pltpu.VMEM)] * 2,
        out_specs=pl.BlockSpec(memory_space=pltpu.VMEM),
        scratch_shapes=[
            pltpu.VMEM((STEPS, depth + 2 * HALO, rows, nx), f32),
            pltpu.VMEM((depth + 4, rows, nx), f32),
            pltpu.VMEM((depth + 4, rows + 16, nx), f32),
            pltpu.VMEM((depth + 4, rows, nx), f32),
            pltpu.VMEM((2, nx, 2 * nx), jnp.bfloat16),
            pltpu.VMEM((depth + 2, rows, nx), f32),
            pltpu.VMEM((depth, nx + SKEW, cols), f32),
            pltpu.VMEM((3, nx, depth, cols), f32),
            pltpu.VMEM((2, 3, cols, BATCH, nx), f32),
            pltpu.VMEM((3, depth, cols, nx), f32),
            pltpu.VMEM((depth, nx + SKEW, cols), f32),
            pltpu.VMEM((depth, cols + SKEW, nx), f32),
            pltpu.VMEM((depth, cols, nx), f32),
            pltpu.VMEM((BATCH, cols + SKEW, nx), f32),
            pltpu.VMEM((depth, nx + SKEW, cols), f32),
            pltpu.VMEM((6, cols, nx), f32),
            pltpu.VMEM((6, cols, nx), f32),
            pltpu.VMEM((STEPS, chunks, 2, CHUNK, nx), f32),
            pltpu.VMEM((STEPS, 2, chunks, 2, CHUNK, nx), f32),
            pltpu.VMEM((STEPS, chunks, CHUNK, nx), f32),
            pltpu.VMEM((STEPS, chunks, CHUNK, nx), f32),
            pltpu.VMEM((STEPS, 2, 6, BATCH, nx), f32),
            pltpu.VMEM((STEPS, 2, 6, BATCH, nx), f32),
            pltpu.VMEM((STEPS, 2, groups, 5, BATCH, nx), f32),
            pltpu.VMEM((2, groups + 1, BATCH, nx), f32),
            dma((STEPS, count)), dma((STEPS, count)),
            dma((STEPS, 2, chunks)), dma((STEPS, 2, chunks)),
            dma((STEPS, chunks)), dma((STEPS, chunks)),
            dma((STEPS, 2)), dma((STEPS, 2)),
            dma((STEPS, 2, groups)), dma((STEPS, 2, groups)),
        ],
        compiler_params=pltpu.CompilerParams(
            collective_id=0, has_side_effects=True, vmem_limit_bytes=48 * 2 ** 20
        ),
    )(volume, contrast.reshape(1, nx))


def solution(mesh):
    in_specs = (P("gz", None, "gy"), P())
    out_specs = P("gz", None, "gy")
    return jax.shard_map(
        on_device, mesh=mesh, in_specs=in_specs, out_specs=out_specs, check_vma=False
    )
```

```python
import functools

import jax
import jax.numpy as jnp
from jax import lax
from jax.experimental import pallas as pl
from jax.experimental.pallas import tpu as pltpu
from jax.sharding import PartitionSpec as P

STEPS = 2
TAPS = (0.05448868, 0.24420134, 0.40261995, 0.24420134, 0.05448868)
SCALE = 600.0
MESH = pl.DeviceIdType.MESH
DIRECTIONS = [(dy, dz) for dz in (-1, 1, 0) for dy in (0, -1, 1) if (dy, dz) != (0, 0)]
PAD = 8
HALO = 4
CHUNK = 32
STENCIL_ROWS = 48
SEGMENTS = 4
SEGMENTS_Y = 8
BATCH = 8
SKEW = 8


def message_plan(cols):
    chunks = cols // CHUNK
    last = chunks - 1
    messages, sends, needs, edge_rows = [], [[] for _ in range(chunks)], [[] for _ in range(chunks)], []

    def add(message, sent, needed):
        sends[sent].append(len(messages))
        (edge_rows if needed is None else needs[needed]).append(len(messages))
        messages.append(message)

    add((-1, 0, 0, 0), 0, None)
    add((1, 0, 0, 0), last, None)
    for dz in (-1, 1):
        add((1, dz, 0, 0), last, 0)
        add((-1, dz, 0, 0), 0, last)
    starts = [c * CHUNK for c in range(chunks)] + [last * CHUNK + PAD]
    for start, stop in zip(starts, starts[1:] + [cols]):
        for dz in (-1, 1):
            needed = max(0, (start - PAD) // CHUNK) if start < last * CHUNK + PAD else last
            add((0, dz, start, stop - start), start // CHUNK, needed)
    return messages, sends, needs, edge_rows


def merge(left, right):
    ea, ra, eb, rb, g, f = left
    ea2, ra2, eb2, rb2, g2, f2 = right
    s1 = 1.0 / (eb + g + f)
    wg, wf, q1 = g * s1, f * s1, rb * s1
    ea = ea + wg * eb
    ra = ra + wg * rb
    ea2 = ea2 + wf * eb
    ra2 = ra2 + wf * rb
    g1 = wf * g
    s2 = 1.0 / (ea2 + g1 + g2)
    vg, vf, q2 = g1 * s2, g2 * s2, ra2 * s2
    joined = (ea + vg * ea2, ra + vg * ra2, eb2 + vf * ea2, rb2 + vf * ra2, vf * g1, f2)
    return joined, (wg, wf, q1, vg, vf, q2)


def unmerge(weights, va, vb):
    wg, wf, q1, vg, vf, q2 = weights
    inner_right = vg * va + vf * vb + q2
    inner_left = wg * va + wf * inner_right + q1
    return inner_left, inner_right


def solve_pair(ea, ra, eb, rb, g):
    s = 1.0 / (ea + g)
    w = g * s
    vb = (rb + w * ra) / (eb + w * ea)
    return w * vb + ra * s, vb


def merge_all(chains):
    levels = []
    while len(chains) > 1:
        pairs = [merge(chains[i], chains[i + 1]) for i in range(0, len(chains), 2)]
        chains = [p[0] for p in pairs]
        levels.append([p[1] for p in pairs])
    return chains[0], levels


def unmerge_all(levels, va, vb):
    ends = [(va, vb)]
    for level in reversed(levels):
        split = []
        for weights, (a, b) in zip(level, ends):
            inner_left, inner_right = unmerge(weights, a, b)
            split += [(a, inner_left), (inner_right, b)]
        ends = split
    return ends


def line_start(get_d, get_r, count, segments):
    states = []
    for base in range(0, count, count // segments):
        d0, d1 = get_d(base), get_d(base + 1)
        one = jnp.ones_like(d0)
        states.append((one, get_r(base), d0 + d1, one, get_r(base + 1), d1))
    return tuple(states)


def line_reduce(get_d, get_r, weights, count, segments):
    size = count // segments

    def body(i, states):
        new = []
        for k, (ea, ra, g, e, r, d) in enumerate(states):
            j = k * size + i
            d1 = get_d(j + 1)
            f = d + d1
            s = 1.0 / (e + g + f)
            wf, wg = f * s, g * s
            weights[0, j] = wf
            weights[1, j] = wg
            weights[2, j] = r * s
            new.append((ea + wg * e, ra + wg * r, wf * g, 1.0 + wf * e, get_r(j + 1) + wf * r, d1))
        return tuple(new)

    return lax.fori_loop(1, size - 1, body, line_start(get_d, get_r, count, segments))


def line_chain(get_d, states, count, edge):
    segments = len(states)
    size = count // segments
    chains = []
    for k, (ea, ra, g, e, r, d) in enumerate(states):
        f = d + get_d((k + 1) * size) if k + 1 < segments else edge(d)
        chains.append((ea, ra, e, r, g, f))
    return merge_all(chains)


def line_back(put, weights, count, ends):
    size = count // len(ends)
    for k, (a, b) in enumerate(ends):
        put(k * size, a)
        put(k * size + size - 1, b)

    def body(t, values):
        new = []
        for k, v in enumerate(values):
            j = k * size + size - 2 - t
            v = weights[0, j] * v + (weights[1, j] * ends[k][0] + weights[2, j])
            put(j, v)
            new.append(v)
        return tuple(new)

    lax.fori_loop(0, size - 2, body, tuple(b for a, b in ends), unroll=3 if (size - 2) % 3 == 0 else 2)


def kernel(ny, nz, vol, contrast_in, out, c_ref, t_ref, b_ref, gx_ref, w_ref, d_ref, dt_ref, wx_ref, wy_ref, wz_ref, vx_ref, vy_ref,
           xt_ref, ce_ref, cur_ref, zr_ref, zi_ref, zsend, zbuf, zvsend, zv, ysend, yrecv, yall, yv_ref,
           con, load_s, halo_s, halo_r, zs, zrs, zvs, zvr, ys, yr, yas, yar):
    depth, nx, cols = vol.shape
    rows = cols + 3 * PAD
    tall = depth + 2 * HALO
    chunks = cols // CHUNK
    ky = lax.axis_index("gy")
    kz = lax.axis_index("gz")

    def at(y, z):
        return {"gy": y, "gz": z}

    def exists(dy, dz):
        ok = True
        if dy:
            ok = (ky + dy >= 0) & (ky + dy < ny)
        if dz:
            ok = ok & (kz + dz >= 0) & (kz + dz < nz)
        return ok

    groups = ny // 2
    side = lax.rem(ky, 2)
    group = lax.div(ky, 2)
    twin = ky + 1 - 2 * side

    def member(j):
        return 2 * lax.rem(group + j, groups) + side

    def load(k):
        return pltpu.make_async_copy(
            vol.at[pl.ds(k * HALO, HALO)], cur_ref.at[pl.ds(k * HALO, HALO), pl.ds(0, nx), :], load_s.at[k])

    load_contrast = pltpu.make_async_copy(contrast_in, con, load_s.at[depth // HALO])
    for k in range(depth // HALO):
        load(k).start()
    load_contrast.start()

    barrier = pltpu.get_barrier_semaphore()
    expected = jnp.int32(groups)
    for dy, dz in DIRECTIONS:
        ok = exists(dy, dz)
        expected = expected + jnp.where(ok, 1, 0)

        @pl.when(ok)
        def _(dy=dy, dz=dz):
            pl.semaphore_signal(barrier, inc=1, device_id=at(ky + dy, kz + dz), device_id_type=MESH)

    for y in [twin] + [member(j) for j in range(1, groups)]:
        pl.semaphore_signal(barrier, inc=1, device_id=at(y, kz), device_id_type=MESH)

    source = lax.broadcasted_iota(jnp.int32, (nx, nx), 0)
    target = lax.broadcasted_iota(jnp.int32, (nx, nx), 1)

    def taps_at(target):
        apart = jnp.where((target >= 0) & (target < nx), jnp.abs(source - target), 3)
        return jnp.where(apart == 0, TAPS[2], jnp.where(apart == 1, TAPS[1], jnp.where(apart == 2, TAPS[0], 0.0)))

    for half, matrix in enumerate((taps_at(target), taps_at(target + 1) - taps_at(target - 1))):
        part = slice(half * nx, half * nx + nx)
        coarse = matrix.astype(jnp.bfloat16)
        w_ref[0, :, part] = coarse
        w_ref[1, :, part] = (matrix - coarse.astype(jnp.float32)).astype(jnp.bfloat16)

    load_contrast.wait()

    @pl.loop(0, depth // HALO)
    def _(k):
        load(k).wait()
        for t in range(HALO):
            z = HALO * k + t
            c_ref[0, z + HALO, PAD:PAD + cols, :] = cur_ref[z, 0:nx, :].T

    pl.semaphore_wait(barrier, expected)

    left = kz < nz // 2
    inward = jnp.where(left, 1, -1)
    order = jnp.where(left, kz, nz - 1 - kz)
    middle = order == nz // 2 - 1
    outermost = order == 0
    slot_out = jnp.where(middle, 1, 0)

    contrast = con[...]
    squared = jnp.broadcast_to(contrast * contrast, (STENCIL_ROWS, nx))

    tall_x = nx + SKEW
    tall_y = cols + SKEW
    cur2 = cur_ref.reshape(depth * tall_x, cols)
    dt2 = dt_ref.reshape(depth * tall_x, cols)
    vx2 = vx_ref.reshape(depth * tall_x, cols)
    vy2 = vy_ref.reshape(depth * tall_y, nx)
    d2 = d_ref.reshape((depth + 2) * rows, nx)
    ce2 = ce_ref.reshape(BATCH * tall_y, nx)

    def place(z):
        if z < 0 or z >= depth:
            return depth if z < 0 else depth + 1
        if z < HALO:
            return z
        return z - BATCH if z >= depth - HALO else z + HALO

    messages, sends, needs, edge_rows = message_plan(cols)

    def halo(i, slot, thin=False):
        dy, dz, start, size = messages[i]
        deep = HALO - 1 if thin else HALO
        src_y = {0: (PAD + start, size), 1: (cols, PAD), -1: (PAD, PAD)}[dy]
        dst_y = {0: (PAD + start, size), 1: (0, PAD), -1: (PAD + cols, PAD)}[dy]
        src_z = {0: (HALO, depth), 1: (depth + HALO - deep, deep), -1: (HALO, deep)}[dz]
        dst_z = {0: (HALO, depth), 1: (HALO - deep, deep), -1: (HALO + depth, deep)}[dz]
        volume = c_ref.at[slot]
        copy = pltpu.make_async_remote_copy(
            src_ref=volume.at[pl.ds(*src_z), pl.ds(*src_y), :], dst_ref=volume.at[pl.ds(*dst_z), pl.ds(*dst_y), :],
            send_sem=halo_s.at[slot, i], recv_sem=halo_r.at[slot, i],
            device_id=at(ky + dy, kz + dz), device_id_type=MESH)
        return copy, dst_z, dst_y

    def forms(i, at_sender):
        dy, dz = messages[i][:2]
        here = exists(dy, dz) if at_sender else exists(-dy, -dz)
        if dy or not dz:
            return [(here, False)]
        sender = kz if at_sender else kz - dz
        outward = sender >= nz // 2 if dz > 0 else sender < nz // 2
        return [(here & outward, True), (here & jnp.logical_not(outward), False)]

    def send(batch, slot):
        for i in batch:
            dy, dz = messages[i][:2]
            _, dst_z, dst_y = halo(i, slot)
            for chosen, thin in forms(i, True):
                @pl.when(chosen)
                def _(i=i, thin=thin):
                    halo(i, slot, thin)[0].start()

            @pl.when(jnp.logical_not(exists(-dy, -dz)))
            def _(dst_z=dst_z, dst_y=dst_y):
                c_ref[slot, pl.ds(*dst_z), pl.ds(*dst_y), :] = jnp.zeros((dst_z[1], dst_y[1], nx), jnp.float32)

    def receive(batch, slot):
        for i in batch:
            for chosen, thin in forms(i, False):
                @pl.when(chosen)
                def _(i=i, thin=thin):
                    halo(i, slot, thin)[0].wait_recv()

    send(range(len(messages)), 0)

    @pl.loop(0, STEPS)
    def _(step):
        c4 = c_ref.at[step]
        c2 = c4.reshape(tall * rows, nx)
        later = lax.rem(step + 1, STEPS)

        def blur_layer(z, r0, size):
            part = pl.ds(r0, size)
            total = TAPS[2] * c4[z + 2, part, :]
            total = total + TAPS[1] * (c4[z + 1, part, :] + c4[z + 3, part, :])
            total = total + TAPS[0] * (c4[z, part, :] + c4[z + 4, part, :])
            t_ref[z, pl.ds(r0, size), :] = total

        def blur_planes(planes, pieces):
            totals = []
            for z in planes:
                for r0, size in pieces:
                    def tap(o):
                        return t_ref[z, pl.ds(r0 + 4 + o, size), :]
                    totals.append(TAPS[2] * tap(0) + TAPS[1] * (tap(-1) + tap(1)) + TAPS[0] * (tap(-2) + tap(2)))
            total = jnp.concatenate(totals)
            coarse = total.astype(jnp.bfloat16)
            fine = (total - coarse.astype(jnp.float32)).astype(jnp.bfloat16)

            def times(value, k):
                return jnp.dot(value, w_ref[k], preferred_element_type=jnp.float32)

            both = times(coarse, 0) + times(fine, 0) + times(coarse, 1)
            start = 0
            for z in planes:
                for r0, size in pieces:
                    b_ref[z, pl.ds(r0, size), :] = both[start:start + size, :nx]
                    gx_ref[z, pl.ds(r0, size), :] = both[start:start + size, nx:]
                    start += size

        def blur_edges(spans, low, high):
            for row, present in ((PAD - 5, ky > 0), (cols + PAD - 4, ky < ny - 1)):
                if low <= row < high:
                    @pl.when(jnp.logical_not(present))
                    def _(row=row):
                        for z0, z1 in spans:
                            b_ref[z0:z1, row:row + 1, :] = jnp.zeros((z1 - z0, 1, nx), jnp.float32)

        def diffuse(z, r0, size, spot=None):
            grad_x = gx_ref[z + 1, pl.ds(r0 + 4, size), :]
            grad_z = b_ref[z + 2, pl.ds(r0 + 4, size), :] - b_ref[z, pl.ds(r0 + 4, size), :]
            grad_y = b_ref[z + 1, pl.ds(r0 + 5, size), :] - b_ref[z + 1, pl.ds(r0 + 3, size), :]
            square = (grad_x * grad_x + grad_y * grad_y + grad_z * grad_z) * 0.25
            d_ref[place(z - 1) if spot is None else spot, pl.ds(r0 + PAD, size), :] = (SCALE * squared[:size]) / (squared[:size] + square)

        inner = list(range(HALO, depth))
        own_rows = [(r0, min(STENCIL_ROWS, cols + PAD - r0)) for r0 in range(PAD, cols + PAD, STENCIL_ROWS)]
        bulk = [(r0, min(STENCIL_ROWS, cols - r0)) for r0 in range(PAD, cols, STENCIL_ROWS)]
        bulk_d = [(r0, min(STENCIL_ROWS, cols - PAD - r0)) for r0 in range(PAD, cols - PAD, STENCIL_ROWS)]

        @pl.loop(HALO, depth)
        def _(z):
            for piece in own_rows:
                blur_layer(z, *piece)

        @pl.loop(0, (depth - HALO) // 2)
        def _(k):
            blur_planes([HALO + 2 * k, HALO + 2 * k + 1], bulk)

        for piece in bulk_d:
            diffuse(HALO, *piece)
            diffuse(depth - HALO + 1, *piece)

        @pl.loop(0, BATCH // 2)
        def _(k):
            for t in range(2):
                for piece in bulk_d:
                    diffuse(HALO + 1 + 2 * k + t, *piece, BATCH + 2 * k + t)

        @pl.loop(0, 2)
        def _(k):
            for t in range(HALO):
                ce_ref[HALO * k + t, 0:cols, :] = c4[HALO + (depth - HALO) * k + t, PAD:PAD + cols, :]

        @pl.when(step > 0)
        def _():
            @pl.loop(0, depth // 4)
            def _(k):
                for t in range(4):
                    z = 4 * k + t
                    cur_ref[z, 0:nx, :] = c4[z + HALO, PAD:PAD + cols, :].T

        receive(edge_rows, step)
        for z in inner:
            blur_layer(z, 0, PAD)
            blur_layer(z, cols + PAD, PAD)
        blur_planes(inner, [(0, PAD), (cols, PAD)])
        blur_edges([(HALO, depth)], 0, cols + PAD)
        for z in range(HALO, depth - 2):
            diffuse(z, 0, PAD)
            diffuse(z, cols - PAD, 2 * PAD)

        def y_at(b):
            def get_d(i):
                return d2[pl.ds(i + b * BATCH * rows + PAD, BATCH, stride=rows), :]

            def get_r(i):
                if b:
                    return c2[pl.ds(i + 2 * HALO * rows + PAD, BATCH, stride=rows), :]
                return ce2[pl.ds(i, BATCH, stride=tall_y), :]

            def put(i, v):
                vy2[pl.ds(i + b * BATCH * tall_y, BATCH, stride=tall_y), :] = v

            return get_d, get_r, put

        def y_copy(b):
            return pltpu.make_async_remote_copy(
                src_ref=ysend.at[step, b], dst_ref=yrecv.at[step, b], send_sem=ys.at[step, b],
                recv_sem=yr.at[step, b], device_id=at(twin, kz), device_id_type=MESH)

        def y_spread(b, j):
            return pltpu.make_async_remote_copy(
                src_ref=yall.at[step, b, 0], dst_ref=yall.at[step, b, j], send_sem=yas.at[step, b, j],
                recv_sem=yar.at[step, b, j], device_id=at(member(j), kz), device_id_type=MESH)

        first = side == 0
        held = [None, None]

        def y_begin(b):
            get_d, get_r, _ = y_at(b)
            states = line_reduce(get_d, get_r, wy_ref.at[b], cols, SEGMENTS_Y)
            chain, levels = line_chain(
                get_d, states, cols, lambda d: jnp.where(ky < ny - 1, d + get_d(cols), 0.0))
            for j in range(6):
                ysend[step, b, j] = chain[j]
            y_copy(b).start()
            held[b] = levels

        def y_join(b):
            chain = tuple(ysend[step, b, j] for j in range(6))
            y_copy(b).wait_recv()
            other = tuple(yrecv[step, b, j] for j in range(6))
            pair_l = tuple(jnp.where(first, a, b) for a, b in zip(chain, other))
            pair_r = tuple(jnp.where(first, b, a) for a, b in zip(chain, other))
            (ea, ra, eb, rb, g, f), pair = merge(pair_l, pair_r)
            s = 1.0 / (eb + g + f)
            wg, wf, q = g * s, f * s, rb * s
            for j, value in enumerate((ea + wg * eb, ra + wg * rb, wf * eb, wf * rb, wf * g)):
                yall[step, b, 0, j] = value
            for j in range(1, groups):
                y_spread(b, j).start()
            held[b] = (held[b], pair, wg, wf, q)

        def y_end(b):
            levels, pair, wg, wf, q = held[b]
            for j in range(1, groups):
                y_spread(b, j).wait_recv()
            e, r, de, dr, link = [yall[step, b, lax.rem(group, groups), j] for j in range(5)]
            ways = []
            for m in range(1, groups):
                s = 1.0 / (e + link)
                w = link * s
                ways.append((w, r * s))
                e, r = w * e + de, w * r + dr
                here = [yall[step, b, lax.rem(group - m + groups, groups), j] for j in range(5)]
                e, r = e + here[0], r + here[1]
                de, dr, link = here[2:]
            v = r / e
            yv_ref[b, groups] = jnp.zeros_like(v)
            yv_ref[b, groups - 1] = v
            for m in range(groups - 2, -1, -1):
                v = ways[m][0] * v + ways[m][1]
                yv_ref[b, m] = v
            va = yv_ref[b, group]
            vb = wg * va + (wf * yv_ref[b, group + 1] + q)
            inner_l, inner_r = unmerge(pair, va, vb)
            va, vb = jnp.where(first, va, inner_r), jnp.where(first, inner_l, vb)
            line_back(y_at(b)[2], wy_ref.at[b], cols, unmerge_all(levels, va, vb))

        def turn(b):
            @pl.loop(0, 2)
            def _(k):
                for t in range(HALO):
                    z = HALO + HALO * k + t if b else (depth - HALO) * k + t
                    dt_ref[z, 0:nx, :] = d_ref[b * BATCH + HALO * k + t, PAD:PAD + cols, :].T

        y_begin(1)
        turn(1)

        def z_copy(c, slot):
            return pltpu.make_async_remote_copy(
                src_ref=zsend.at[step, c], dst_ref=zbuf.at[step, slot, c], send_sem=zs.at[step, slot, c],
                recv_sem=zrs.at[step, slot, c], device_id=at(ky, kz + inward), device_id_type=MESH)

        def z_back(c):
            return pltpu.make_async_remote_copy(
                src_ref=zvsend.at[step, c], dst_ref=zv.at[step, c], send_sem=zvs.at[step, c],
                recv_sem=zvr.at[step, c], device_id=at(ky, kz - inward), device_id_type=MESH)

        def z_inward(c, carry):
            own = pl.ds(pl.multiple_of(c * CHUNK, CHUNK), CHUNK)

            @pl.when(jnp.logical_not(outermost))
            def _():
                z_copy(c, 0).wait_recv()
                f = zr_ref[6, own, :]
                s = 1.0 / (zbuf[step, 0, c, 0] + f)
                u = f * s
                zi_ref[4, own, :] = u
                zi_ref[5, own, :] = zbuf[step, 0, c, 1] * s
                zr_ref[0, own, :] += u * zbuf[step, 0, c, 0]
                zr_ref[1, own, :] += u * zbuf[step, 0, c, 1]

            eo, ro, ei, ri, g, f = [zr_ref[j, own, :] for j in range(6)]
            s = 1.0 / (eo + g)
            w = g * s
            ei = ei + w * eo
            ri = ri + w * ro
            u = jnp.where(middle, f / (ei + f), 1.0)
            zi_ref[0, own, :] = w
            zi_ref[1, own, :] = ro * s
            zi_ref[2, own, :] = ei
            zi_ref[3, own, :] = ri
            zsend[step, c, 0] = u * ei
            zsend[step, c, 1] = u * ri
            z_copy(c, slot_out).start()
            return carry

        def z_solve(c):
            own = pl.ds(pl.multiple_of(c * CHUNK, CHUNK), CHUNK)

            @pl.when(middle)
            def _():
                z_copy(c, 1).wait_recv()
                zr_ref[0, own, :] = (zi_ref[3, own, :] + zbuf[step, 1, c, 1]) / (zi_ref[2, own, :] + zbuf[step, 1, c, 0])

            @pl.when(jnp.logical_not(middle))
            def _():
                z_back(c).wait_recv()
                zr_ref[0, own, :] = zv[step, c]

            vo = zi_ref[0, own, :] * zr_ref[0, own, :] + zi_ref[1, own, :]
            zr_ref[1, own, :] = vo

            @pl.when(jnp.logical_not(outermost))
            def _():
                zvsend[step, c] = zi_ref[4, own, :] * vo + zi_ref[5, own, :]
                z_back(c).start()

        def z_finish(c):
            own = pl.ds(c * CHUNK, CHUNK)
            padded = pl.ds(c * CHUNK + PAD, CHUNK)

            def put(i, v):
                c_ref[later, HALO + i, padded, :] = (vy_ref[place(i), own, :] + xt_ref[i, own, :] + v) * (1.0 / 3.0)

            vi, vo = zr_ref[0, own, :], zr_ref[1, own, :]
            va = jnp.where(left, vo, vi)
            v = jnp.where(left, vi, vo)
            put(0, va)
            put(depth - 1, v)
            for i in range(depth - 2, 0, -1):
                v = wz_ref[0, i, own, :] * v + (wz_ref[1, i, own, :] * va + wz_ref[2, i, own, :])
                put(i, v)

        def z_chain(c):
            y0 = c * CHUNK
            part = pl.ds(y0 + PAD, CHUNK)
            own = pl.ds(y0, CHUNK)
            d = d_ref[place(0), part, :]
            f_lo = jnp.where(kz > 0, d_ref[place(-1), part, :] + d, 0.0)
            d_next = d_ref[place(1), part, :]
            g = d + d_next
            d = d_next
            ea = jnp.ones_like(g)
            ra = c4[HALO, part, :]
            e = ea
            r = c4[HALO + 1, part, :]
            for i in range(1, depth - 1):
                d_next = d_ref[place(i + 1), part, :]
                f = d + d_next
                d = d_next
                s = 1.0 / (e + g + f)
                wf, wg = f * s, g * s
                wz_ref[0, i, own, :] = wf
                wz_ref[1, i, own, :] = wg
                wz_ref[2, i, own, :] = r * s
                ea = ea + wg * e
                ra = ra + wg * r
                e = 1.0 + wf * e
                r = c4[HALO + i + 1, part, :] + wf * r
                g = wf * g
            f_hi = jnp.where(kz < nz - 1, d + d_ref[place(depth), part, :], 0.0)
            zr_ref[0, own, :] = jnp.where(left, ea, e)
            zr_ref[1, own, :] = jnp.where(left, ra, r)
            zr_ref[2, own, :] = jnp.where(left, e, ea)
            zr_ref[3, own, :] = jnp.where(left, r, ra)
            zr_ref[4, own, :] = g
            zr_ref[5, own, :] = jnp.where(left, f_hi, f_lo)
            zr_ref[6, own, :] = jnp.where(left, f_lo, f_hi)

            @pl.when(outermost)
            def _():
                z_inward(c, 0)

        outer = list(range(HALO)) + list(range(depth, depth + HALO))
        for c, batch in enumerate(needs):
            start, stop = c * CHUNK, (c + 1) * CHUNK
            tail = PAD if c + 1 == chunks else 0
            receive(batch, step)
            t0 = start + 2 * PAD if c else 0
            for z in outer:
                blur_layer(z, t0, stop + 2 * PAD - t0)
            b0 = start + PAD if c else 0
            b1 = stop + PAD
            blur_planes(outer, [(b0, b1 - b0)])
            blur_edges([(0, HALO), (depth, depth + HALO)], b0, b1)

            @pl.when(kz == 0)
            def _(b0=b0, b1=b1):
                b_ref[1, b0:b1, :] = jnp.zeros((b1 - b0, nx), jnp.float32)

            @pl.when(kz == nz - 1)
            def _(b0=b0, b1=b1):
                b_ref[depth + 2, b0:b1, :] = jnp.zeros((b1 - b0, nx), jnp.float32)

            for z in list(range(HALO)) + list(range(depth - 2, depth + 2)):
                diffuse(z, start, stop + tail - start)
            z_chain(c)
            if c == 0:
                y_join(1)

        def dx(i):
            return dt2[pl.ds(i, depth, stride=tall_x), :]

        def rx(i):
            return cur2[pl.ds(i, depth, stride=tall_x), :]

        def put_x(i, v):
            vx2[pl.ds(i, depth, stride=tall_x), :] = v

        def z_piece(k):
            @pl.when(jnp.logical_not(outermost))
            def _():
                z_inward(k, 0)

        y_begin(0)
        for k in range(chunks):
            z_piece(k)

        y_join(0)
        turn(0)

        states = line_reduce(dx, rx, wx_ref, nx, SEGMENTS)
        x_chain, levels_x = line_chain(dx, states, nx, jnp.zeros_like)
        line_back(put_x, wx_ref, nx, unmerge_all(levels_x, *solve_pair(*x_chain[:5])))

        @pl.loop(0, depth // 4)
        def _(k):
            for t in range(4):
                z = 4 * k + t
                xt_ref[z] = vx_ref[z, 0:nx, :].T

        @pl.when(jnp.logical_not(outermost))
        def _():
            @pl.loop(0, chunks)
            def _(c):
                z_solve(c)

        y_end(1)
        y_end(0)

        for c in range(chunks):
            @pl.when(outermost)
            def _(c=c):
                z_solve(c)

            z_finish(c)

            @pl.when(step + 1 < STEPS)
            def _(c=c):
                send(sends[c], later)

        for b in range(2):
            y_copy(b).wait_send()
            for j in range(1, groups):
                y_spread(b, j).wait_send()

        for i in range(len(messages)):
            for chosen, thin in forms(i, True):
                @pl.when(chosen)
                def _(i=i, thin=thin):
                    halo(i, step, thin)[0].wait_send()

        @pl.loop(0, chunks)
        def _(c):
            z_copy(c, slot_out).wait_send()

            @pl.when(jnp.logical_not(outermost))
            def _():
                z_back(c).wait_send()

    @pl.loop(0, depth // 4)
    def _(k):
        for t in range(4):
            z = 4 * k + t
            out[z] = c_ref[0, z + HALO, PAD:PAD + cols, :].T


def on_device(volume, contrast):
    depth, nx, cols = volume.shape
    ny = lax.axis_size("gy")
    nz = lax.axis_size("gz")
    groups = ny // 2
    assert ny % 2 == 0 and nz % 2 == 0 and depth == 2 * BATCH == 4 * HALO
    rows = cols + 3 * PAD
    chunks = cols // CHUNK
    f32 = jnp.float32
    dma = pltpu.SemaphoreType.DMA
    count = len(message_plan(cols)[0])
    return pl.pallas_call(
        functools.partial(kernel, ny, nz),
        out_shape=jax.ShapeDtypeStruct(volume.shape, f32),
        in_specs=[pl.BlockSpec(memory_space=pl.ANY)] * 2,
        out_specs=pl.BlockSpec(memory_space=pltpu.VMEM),
        scratch_shapes=[
            pltpu.VMEM((STEPS, depth + 2 * HALO, rows, nx), f32),
            pltpu.VMEM((depth + 4, rows, nx), f32),
            pltpu.VMEM((depth + 4, rows + 16, nx), f32),
            pltpu.VMEM((depth + 4, rows, nx), f32),
            pltpu.VMEM((2, nx, 2 * nx), jnp.bfloat16),
            pltpu.VMEM((depth + 2, rows, nx), f32),
            pltpu.VMEM((depth, nx + SKEW, cols), f32),
            pltpu.VMEM((3, nx, depth, cols), f32),
            pltpu.VMEM((2, 3, cols, BATCH, nx), f32),
            pltpu.VMEM((3, depth, cols, nx), f32),
            pltpu.VMEM((depth, nx + SKEW, cols), f32),
            pltpu.VMEM((depth, cols + SKEW, nx), f32),
            pltpu.VMEM((depth, cols, nx), f32),
            pltpu.VMEM((BATCH, cols + SKEW, nx), f32),
            pltpu.VMEM((depth, nx + SKEW, cols), f32),
            pltpu.VMEM((7, cols, nx), f32),
            pltpu.VMEM((6, cols, nx), f32),
            pltpu.VMEM((STEPS, chunks, 2, CHUNK, nx), f32),
            pltpu.VMEM((STEPS, 2, chunks, 2, CHUNK, nx), f32),
            pltpu.VMEM((STEPS, chunks, CHUNK, nx), f32),
            pltpu.VMEM((STEPS, chunks, CHUNK, nx), f32),
            pltpu.VMEM((STEPS, 2, 6, BATCH, nx), f32),
            pltpu.VMEM((STEPS, 2, 6, BATCH, nx), f32),
            pltpu.VMEM((STEPS, 2, groups, 5, BATCH, nx), f32),
            pltpu.VMEM((2, groups + 1, BATCH, nx), f32),
            pltpu.VMEM((1, nx), f32), dma((depth // HALO + 1,)),
            dma((STEPS, count)), dma((STEPS, count)),
            dma((STEPS, 2, chunks)), dma((STEPS, 2, chunks)),
            dma((STEPS, chunks)), dma((STEPS, chunks)),
            dma((STEPS, 2)), dma((STEPS, 2)),
            dma((STEPS, 2, groups)), dma((STEPS, 2, groups)),
        ],
        compiler_params=pltpu.CompilerParams(
            collective_id=0, has_side_effects=True, vmem_limit_bytes=52 * 2 ** 20
        ),
    )(volume, contrast.reshape(1, nx))


def solution(mesh):
    in_specs = (P("gz", None, "gy"), P())
    out_specs = P("gz", None, "gy")
    return jax.shard_map(
        on_device, mesh=mesh, in_specs=in_specs, out_specs=out_specs, check_vma=False
    )
```

```python
import functools

import jax
import jax.numpy as jnp
from jax import lax
from jax.experimental import pallas as pl
from jax.experimental.pallas import tpu as pltpu
from jax.sharding import PartitionSpec as P

STEPS = 2
TAPS = (0.05448868, 0.24420134, 0.40261995, 0.24420134, 0.05448868)
SCALE = 600.0
MESH = pl.DeviceIdType.MESH
DIRECTIONS = [(dy, dz) for dz in (-1, 1, 0) for dy in (0, -1, 1) if (dy, dz) != (0, 0)]
PAD = 8
HALO = 4
CHUNK = 32
STENCIL_ROWS = 48
SEGMENTS = 4
SEGMENTS_Y = 8
BATCH = 8
SKEW = 8


def message_plan(cols):
    chunks = cols // CHUNK
    last = chunks - 1
    messages, sends, needs, edge_rows = [], [[] for _ in range(chunks)], [[] for _ in range(chunks)], []

    def add(message, sent, needed):
        sends[sent].append(len(messages))
        (edge_rows if needed is None else needs[needed]).append(len(messages))
        messages.append(message)

    add((-1, 0, 0, 0), 0, None)
    add((1, 0, 0, 0), last, None)
    for dz in (-1, 1):
        add((1, dz, 0, 0), last, 0)
        add((-1, dz, 0, 0), 0, last)
    starts = [c * CHUNK for c in range(chunks)] + [last * CHUNK + PAD]
    for start, stop in zip(starts, starts[1:] + [cols]):
        for dz in (-1, 1):
            needed = max(0, (start - PAD) // CHUNK) if start < last * CHUNK + PAD else last
            add((0, dz, start, stop - start), start // CHUNK, needed)
    return messages, sends, needs, edge_rows


def merge(left, right):
    ea, ra, eb, rb, g, f = left
    ea2, ra2, eb2, rb2, g2, f2 = right
    s1 = 1.0 / (eb + g + f)
    wg, wf, q1 = g * s1, f * s1, rb * s1
    ea = ea + wg * eb
    ra = ra + wg * rb
    ea2 = ea2 + wf * eb
    ra2 = ra2 + wf * rb
    g1 = wf * g
    s2 = 1.0 / (ea2 + g1 + g2)
    vg, vf, q2 = g1 * s2, g2 * s2, ra2 * s2
    joined = (ea + vg * ea2, ra + vg * ra2, eb2 + vf * ea2, rb2 + vf * ra2, vf * g1, f2)
    return joined, (wg, wf, q1, vg, vf, q2)


def unmerge(weights, va, vb):
    wg, wf, q1, vg, vf, q2 = weights
    inner_right = vg * va + vf * vb + q2
    inner_left = wg * va + wf * inner_right + q1
    return inner_left, inner_right


def solve_pair(ea, ra, eb, rb, g):
    s = 1.0 / (ea + g)
    w = g * s
    vb = (rb + w * ra) / (eb + w * ea)
    return w * vb + ra * s, vb


def merge_all(chains):
    levels = []
    while len(chains) > 1:
        pairs = [merge(chains[i], chains[i + 1]) for i in range(0, len(chains), 2)]
        chains = [p[0] for p in pairs]
        levels.append([p[1] for p in pairs])
    return chains[0], levels


def unmerge_all(levels, va, vb):
    ends = [(va, vb)]
    for level in reversed(levels):
        split = []
        for weights, (a, b) in zip(level, ends):
            inner_left, inner_right = unmerge(weights, a, b)
            split += [(a, inner_left), (inner_right, b)]
        ends = split
    return ends


def line_start(get_d, get_r, count, segments):
    states = []
    for base in range(0, count, count // segments):
        d0, d1 = get_d(base), get_d(base + 1)
        one = jnp.ones_like(d0)
        states.append((one, get_r(base), d0 + d1, one, get_r(base + 1), d1))
    return tuple(states)


def line_reduce(get_d, get_r, weights, count, segments):
    size = count // segments

    def body(i, states):
        new = []
        for k, (ea, ra, g, e, r, d) in enumerate(states):
            j = k * size + i
            d1 = get_d(j + 1)
            f = d + d1
            s = 1.0 / (e + g + f)
            wf, wg = f * s, g * s
            weights[0, j] = wf
            weights[1, j] = wg
            weights[2, j] = r * s
            new.append((ea + wg * e, ra + wg * r, wf * g, 1.0 + wf * e, get_r(j + 1) + wf * r, d1))
        return tuple(new)

    return lax.fori_loop(1, size - 1, body, line_start(get_d, get_r, count, segments))


def line_chain(get_d, states, count, edge):
    segments = len(states)
    size = count // segments
    chains = []
    for k, (ea, ra, g, e, r, d) in enumerate(states):
        f = d + get_d((k + 1) * size) if k + 1 < segments else edge(d)
        chains.append((ea, ra, e, r, g, f))
    return merge_all(chains)


def line_back(put, weights, count, ends):
    size = count // len(ends)
    for k, (a, b) in enumerate(ends):
        put(k * size, a)
        put(k * size + size - 1, b)

    def body(t, values):
        new = []
        for k, v in enumerate(values):
            j = k * size + size - 2 - t
            v = weights[0, j] * v + (weights[1, j] * ends[k][0] + weights[2, j])
            put(j, v)
            new.append(v)
        return tuple(new)

    lax.fori_loop(0, size - 2, body, tuple(b for a, b in ends), unroll=3 if (size - 2) % 3 == 0 else 2)


def kernel(ny, nz, vol, contrast_in, out, c_ref, t_ref, b_ref, gx_ref, w_ref, d_ref, dt_ref, wx_ref, wy_ref, wz_ref, vx_ref, vy_ref,
           xt_ref, ce_ref, cur_ref, zr_ref, zi_ref, zsend, zbuf, zvsend, zv, ysend, yrecv, yall, yv_ref,
           con, load_s, halo_s, halo_r, zs, zrs, zvs, zvr, ys, yr, yas, yar):
    depth, nx, cols = vol.shape
    rows = cols + 3 * PAD
    tall = depth + 2 * HALO
    chunks = cols // CHUNK
    ky = lax.axis_index("gy")
    kz = lax.axis_index("gz")

    def at(y, z):
        return {"gy": y, "gz": z}

    def exists(dy, dz):
        ok = True
        if dy:
            ok = (ky + dy >= 0) & (ky + dy < ny)
        if dz:
            ok = ok & (kz + dz >= 0) & (kz + dz < nz)
        return ok

    groups = ny // 2
    side = lax.rem(ky, 2)
    group = lax.div(ky, 2)
    twin = ky + 1 - 2 * side

    def member(j):
        return 2 * lax.rem(group + j, groups) + side

    def load(k):
        return pltpu.make_async_copy(
            vol.at[pl.ds(k * HALO, HALO)], cur_ref.at[pl.ds(k * HALO, HALO), pl.ds(0, nx), :], load_s.at[k])

    load_contrast = pltpu.make_async_copy(contrast_in, con, load_s.at[depth // HALO])
    for k in range(depth // HALO):
        load(k).start()
    load_contrast.start()

    barrier = pltpu.get_barrier_semaphore()
    expected = jnp.int32(groups)
    for dy, dz in DIRECTIONS:
        ok = exists(dy, dz)
        expected = expected + jnp.where(ok, 1, 0)

        @pl.when(ok)
        def _(dy=dy, dz=dz):
            pl.semaphore_signal(barrier, inc=1, device_id=at(ky + dy, kz + dz), device_id_type=MESH)

    for y in [twin] + [member(j) for j in range(1, groups)]:
        pl.semaphore_signal(barrier, inc=1, device_id=at(y, kz), device_id_type=MESH)

    source = lax.broadcasted_iota(jnp.int32, (nx, nx), 0)
    target = lax.broadcasted_iota(jnp.int32, (nx, nx), 1)

    def taps_at(target):
        apart = jnp.where((target >= 0) & (target < nx), jnp.abs(source - target), 3)
        return jnp.where(apart == 0, TAPS[2], jnp.where(apart == 1, TAPS[1], jnp.where(apart == 2, TAPS[0], 0.0)))

    for half, matrix in enumerate((taps_at(target), taps_at(target + 1) - taps_at(target - 1))):
        part = slice(half * nx, half * nx + nx)
        coarse = matrix.astype(jnp.bfloat16)
        w_ref[0:nx, part] = coarse
        w_ref[nx:2 * nx, part] = coarse
        w_ref[2 * nx:, part] = (matrix - coarse.astype(jnp.float32)).astype(jnp.bfloat16)

    load_contrast.wait()

    @pl.loop(0, depth // HALO)
    def _(k):
        load(k).wait()
        for t in range(HALO):
            z = HALO * k + t
            c_ref[0, z + HALO, PAD:PAD + cols, :] = cur_ref[z, 0:nx, :].T

    pl.semaphore_wait(barrier, expected)

    left = kz < nz // 2
    inward = jnp.where(left, 1, -1)
    order = jnp.where(left, kz, nz - 1 - kz)
    middle = order == nz // 2 - 1
    outermost = order == 0
    slot_out = jnp.where(middle, 1, 0)

    contrast = con[...]
    squared = jnp.broadcast_to(contrast * contrast, (STENCIL_ROWS, nx))

    tall_x = nx + SKEW
    tall_y = cols + SKEW
    cur2 = cur_ref.reshape(depth * tall_x, cols)
    dt2 = dt_ref.reshape(depth * tall_x, cols)
    vx2 = vx_ref.reshape(depth * tall_x, cols)
    vy2 = vy_ref.reshape(depth * tall_y, nx)
    d2 = d_ref.reshape((depth + 2) * rows, nx)
    ce2 = ce_ref.reshape(BATCH * tall_y, nx)

    def place(z):
        if z < 0 or z >= depth:
            return depth if z < 0 else depth + 1
        if z < HALO:
            return z
        return z - BATCH if z >= depth - HALO else z + HALO

    messages, sends, needs, edge_rows = message_plan(cols)

    def halo(i, slot, thin=False):
        dy, dz, start, size = messages[i]
        deep = HALO - 1 if thin else HALO
        src_y = {0: (PAD + start, size), 1: (cols, PAD), -1: (PAD, PAD)}[dy]
        dst_y = {0: (PAD + start, size), 1: (0, PAD), -1: (PAD + cols, PAD)}[dy]
        src_z = {0: (HALO, depth), 1: (depth + HALO - deep, deep), -1: (HALO, deep)}[dz]
        dst_z = {0: (HALO, depth), 1: (HALO - deep, deep), -1: (HALO + depth, deep)}[dz]
        volume = c_ref.at[slot]
        copy = pltpu.make_async_remote_copy(
            src_ref=volume.at[pl.ds(*src_z), pl.ds(*src_y), :], dst_ref=volume.at[pl.ds(*dst_z), pl.ds(*dst_y), :],
            send_sem=halo_s.at[slot, i], recv_sem=halo_r.at[slot, i],
            device_id=at(ky + dy, kz + dz), device_id_type=MESH)
        return copy, dst_z, dst_y

    def forms(i, at_sender):
        dy, dz = messages[i][:2]
        here = exists(dy, dz) if at_sender else exists(-dy, -dz)
        if dy or not dz:
            return [(here, False)]
        sender = kz if at_sender else kz - dz
        outward = sender >= nz // 2 if dz > 0 else sender < nz // 2
        return [(here & outward, True), (here & jnp.logical_not(outward), False)]

    def send(batch, slot):
        for i in batch:
            dy, dz = messages[i][:2]
            _, dst_z, dst_y = halo(i, slot)
            for chosen, thin in forms(i, True):
                @pl.when(chosen)
                def _(i=i, thin=thin):
                    halo(i, slot, thin)[0].start()

            @pl.when(jnp.logical_not(exists(-dy, -dz)))
            def _(dst_z=dst_z, dst_y=dst_y):
                c_ref[slot, pl.ds(*dst_z), pl.ds(*dst_y), :] = jnp.zeros((dst_z[1], dst_y[1], nx), jnp.float32)

    def receive(batch, slot):
        for i in batch:
            for chosen, thin in forms(i, False):
                @pl.when(chosen)
                def _(i=i, thin=thin):
                    halo(i, slot, thin)[0].wait_recv()

    send(range(len(messages)), 0)

    @pl.loop(0, STEPS)
    def _(step):
        c4 = c_ref.at[step]
        c2 = c4.reshape(tall * rows, nx)
        later = lax.rem(step + 1, STEPS)

        def blur_layer(z, r0, size):
            part = pl.ds(r0, size)
            total = TAPS[2] * c4[z + 2, part, :]
            total = total + TAPS[1] * (c4[z + 1, part, :] + c4[z + 3, part, :])
            total = total + TAPS[0] * (c4[z, part, :] + c4[z + 4, part, :])
            t_ref[z, pl.ds(r0, size), :] = total

        def blur_planes(planes, pieces):
            totals = []
            for z in planes:
                for r0, size in pieces:
                    def tap(o):
                        return t_ref[z, pl.ds(r0 + 4 + o, size), :]
                    totals.append(TAPS[2] * tap(0) + TAPS[1] * (tap(-1) + tap(1)) + TAPS[0] * (tap(-2) + tap(2)))
            total = jnp.concatenate(totals)
            coarse = total.astype(jnp.bfloat16)
            fine = (total - coarse.astype(jnp.float32)).astype(jnp.bfloat16)

            both = jnp.dot(jnp.concatenate([coarse, fine], axis=1), w_ref[0:2 * nx], preferred_element_type=jnp.float32)
            both = both + jnp.dot(coarse, w_ref[2 * nx:], preferred_element_type=jnp.float32)
            start = 0
            for z in planes:
                for r0, size in pieces:
                    b_ref[z, pl.ds(r0, size), :] = both[start:start + size, :nx]
                    gx_ref[z, pl.ds(r0, size), :] = both[start:start + size, nx:]
                    start += size

        def blur_edges(spans, low, high):
            for row, present in ((PAD - 5, ky > 0), (cols + PAD - 4, ky < ny - 1)):
                if low <= row < high:
                    @pl.when(jnp.logical_not(present))
                    def _(row=row):
                        for z0, z1 in spans:
                            b_ref[z0:z1, row:row + 1, :] = jnp.zeros((z1 - z0, 1, nx), jnp.float32)

        def diffuse(z, r0, size, spot=None):
            grad_x = gx_ref[z + 1, pl.ds(r0 + 4, size), :]
            grad_z = b_ref[z + 2, pl.ds(r0 + 4, size), :] - b_ref[z, pl.ds(r0 + 4, size), :]
            grad_y = b_ref[z + 1, pl.ds(r0 + 5, size), :] - b_ref[z + 1, pl.ds(r0 + 3, size), :]
            square = (grad_x * grad_x + grad_y * grad_y + grad_z * grad_z) * 0.25
            d_ref[place(z - 1) if spot is None else spot, pl.ds(r0 + PAD, size), :] = (SCALE * squared[:size]) / (squared[:size] + square)

        inner = list(range(HALO, depth))
        own_rows = [(r0, min(STENCIL_ROWS, cols + PAD - r0)) for r0 in range(PAD, cols + PAD, STENCIL_ROWS)]
        bulk = [(r0, min(STENCIL_ROWS, cols - r0)) for r0 in range(PAD, cols, STENCIL_ROWS)]
        bulk_d = [(r0, min(STENCIL_ROWS, cols - PAD - r0)) for r0 in range(PAD, cols - PAD, STENCIL_ROWS)]

        @pl.loop(HALO, depth)
        def _(z):
            for piece in own_rows:
                blur_layer(z, *piece)

        @pl.loop(0, (depth - HALO) // 2)
        def _(k):
            blur_planes([HALO + 2 * k, HALO + 2 * k + 1], bulk)

        for piece in bulk_d:
            diffuse(HALO, *piece)
            diffuse(depth - HALO + 1, *piece)

        @pl.loop(0, BATCH // 2)
        def _(k):
            for t in range(2):
                for piece in bulk_d:
                    diffuse(HALO + 1 + 2 * k + t, *piece, BATCH + 2 * k + t)

        @pl.loop(0, 2)
        def _(k):
            for t in range(HALO):
                ce_ref[HALO * k + t, 0:cols, :] = c4[HALO + (depth - HALO) * k + t, PAD:PAD + cols, :]

        @pl.when(step > 0)
        def _():
            @pl.loop(0, depth // 4)
            def _(k):
                for t in range(4):
                    z = 4 * k + t
                    cur_ref[z, 0:nx, :] = c4[z + HALO, PAD:PAD + cols, :].T

        receive(edge_rows, step)
        for z in inner:
            blur_layer(z, 0, PAD)
            blur_layer(z, cols + PAD, PAD)
        blur_planes(inner, [(0, PAD), (cols, PAD)])
        blur_edges([(HALO, depth)], 0, cols + PAD)
        for z in range(HALO, depth - 2):
            diffuse(z, 0, PAD)
            diffuse(z, cols - PAD, 2 * PAD)

        def y_at(b):
            def get_d(i):
                return d2[pl.ds(i + b * BATCH * rows + PAD, BATCH, stride=rows), :]

            def get_r(i):
                if b:
                    return c2[pl.ds(i + 2 * HALO * rows + PAD, BATCH, stride=rows), :]
                return ce2[pl.ds(i, BATCH, stride=tall_y), :]

            def put(i, v):
                vy2[pl.ds(i + b * BATCH * tall_y, BATCH, stride=tall_y), :] = v

            return get_d, get_r, put

        def y_copy(b):
            return pltpu.make_async_remote_copy(
                src_ref=ysend.at[step, b], dst_ref=yrecv.at[step, b], send_sem=ys.at[step, b],
                recv_sem=yr.at[step, b], device_id=at(twin, kz), device_id_type=MESH)

        def y_spread(b, j):
            return pltpu.make_async_remote_copy(
                src_ref=yall.at[step, b, 0], dst_ref=yall.at[step, b, j], send_sem=yas.at[step, b, j],
                recv_sem=yar.at[step, b, j], device_id=at(member(j), kz), device_id_type=MESH)

        first = side == 0
        held = [None, None]

        def y_begin(b):
            get_d, get_r, _ = y_at(b)
            states = line_reduce(get_d, get_r, wy_ref.at[b], cols, SEGMENTS_Y)
            chain, levels = line_chain(
                get_d, states, cols, lambda d: jnp.where(ky < ny - 1, d + get_d(cols), 0.0))
            for j in range(6):
                ysend[step, b, j] = chain[j]
            y_copy(b).start()
            held[b] = levels

        def y_join(b):
            chain = tuple(ysend[step, b, j] for j in range(6))
            y_copy(b).wait_recv()
            other = tuple(yrecv[step, b, j] for j in range(6))
            pair_l = tuple(jnp.where(first, a, b) for a, b in zip(chain, other))
            pair_r = tuple(jnp.where(first, b, a) for a, b in zip(chain, other))
            (ea, ra, eb, rb, g, f), pair = merge(pair_l, pair_r)
            s = 1.0 / (eb + g + f)
            wg, wf, q = g * s, f * s, rb * s
            for j, value in enumerate((ea + wg * eb, ra + wg * rb, wf * eb, wf * rb, wf * g)):
                yall[step, b, 0, j] = value
            for j in range(1, groups):
                y_spread(b, j).start()
            held[b] = (held[b], pair, wg, wf, q)

        def y_end(b):
            levels, pair, wg, wf, q = held[b]
            for j in range(1, groups):
                y_spread(b, j).wait_recv()
            e, r, de, dr, link = [yall[step, b, lax.rem(group, groups), j] for j in range(5)]
            ways = []
            for m in range(1, groups):
                s = 1.0 / (e + link)
                w = link * s
                ways.append((w, r * s))
                e, r = w * e + de, w * r + dr
                here = [yall[step, b, lax.rem(group - m + groups, groups), j] for j in range(5)]
                e, r = e + here[0], r + here[1]
                de, dr, link = here[2:]
            v = r / e
            yv_ref[b, groups] = jnp.zeros_like(v)
            yv_ref[b, groups - 1] = v
            for m in range(groups - 2, -1, -1):
                v = ways[m][0] * v + ways[m][1]
                yv_ref[b, m] = v
            va = yv_ref[b, group]
            vb = wg * va + (wf * yv_ref[b, group + 1] + q)
            inner_l, inner_r = unmerge(pair, va, vb)
            va, vb = jnp.where(first, va, inner_r), jnp.where(first, inner_l, vb)
            line_back(y_at(b)[2], wy_ref.at[b], cols, unmerge_all(levels, va, vb))

        def turn(b):
            @pl.loop(0, 2)
            def _(k):
                for t in range(HALO):
                    z = HALO + HALO * k + t if b else (depth - HALO) * k + t
                    dt_ref[z, 0:nx, :] = d_ref[b * BATCH + HALO * k + t, PAD:PAD + cols, :].T

        y_begin(1)
        turn(1)

        def z_copy(c, slot):
            return pltpu.make_async_remote_copy(
                src_ref=zsend.at[step, c], dst_ref=zbuf.at[step, slot, c], send_sem=zs.at[step, slot, c],
                recv_sem=zrs.at[step, slot, c], device_id=at(ky, kz + inward), device_id_type=MESH)

        def z_back(c):
            return pltpu.make_async_remote_copy(
                src_ref=zvsend.at[step, c], dst_ref=zv.at[step, c], send_sem=zvs.at[step, c],
                recv_sem=zvr.at[step, c], device_id=at(ky, kz - inward), device_id_type=MESH)

        def z_inward(c, carry):
            own = pl.ds(pl.multiple_of(c * CHUNK, CHUNK), CHUNK)

            @pl.when(jnp.logical_not(outermost))
            def _():
                z_copy(c, 0).wait_recv()
                f = zr_ref[6, own, :]
                s = 1.0 / (zbuf[step, 0, c, 0] + f)
                u = f * s
                zi_ref[4, own, :] = u
                zi_ref[5, own, :] = zbuf[step, 0, c, 1] * s
                zr_ref[0, own, :] += u * zbuf[step, 0, c, 0]
                zr_ref[1, own, :] += u * zbuf[step, 0, c, 1]

            eo, ro, ei, ri, g, f = [zr_ref[j, own, :] for j in range(6)]
            s = 1.0 / (eo + g)
            w = g * s
            ei = ei + w * eo
            ri = ri + w * ro
            u = jnp.where(middle, f / (ei + f), 1.0)
            zi_ref[0, own, :] = w
            zi_ref[1, own, :] = ro * s
            zi_ref[2, own, :] = ei
            zi_ref[3, own, :] = ri
            zsend[step, c, 0] = u * ei
            zsend[step, c, 1] = u * ri
            z_copy(c, slot_out).start()
            return carry

        def z_solve(c):
            own = pl.ds(pl.multiple_of(c * CHUNK, CHUNK), CHUNK)

            @pl.when(middle)
            def _():
                z_copy(c, 1).wait_recv()
                zr_ref[0, own, :] = (zi_ref[3, own, :] + zbuf[step, 1, c, 1]) / (zi_ref[2, own, :] + zbuf[step, 1, c, 0])

            @pl.when(jnp.logical_not(middle))
            def _():
                z_back(c).wait_recv()
                zr_ref[0, own, :] = zv[step, c]

            vo = zi_ref[0, own, :] * zr_ref[0, own, :] + zi_ref[1, own, :]
            zr_ref[1, own, :] = vo

            @pl.when(jnp.logical_not(outermost))
            def _():
                zvsend[step, c] = zi_ref[4, own, :] * vo + zi_ref[5, own, :]
                z_back(c).start()

        def z_finish(c):
            own = pl.ds(c * CHUNK, CHUNK)
            padded = pl.ds(c * CHUNK + PAD, CHUNK)

            def put(i, v):
                c_ref[later, HALO + i, padded, :] = (vy_ref[place(i), own, :] + xt_ref[i, own, :] + v) * (1.0 / 3.0)

            vi, vo = zr_ref[0, own, :], zr_ref[1, own, :]
            va = jnp.where(left, vo, vi)
            v = jnp.where(left, vi, vo)
            put(0, va)
            put(depth - 1, v)
            for i in range(depth - 2, 0, -1):
                v = wz_ref[0, i, own, :] * v + (wz_ref[1, i, own, :] * va + wz_ref[2, i, own, :])
                put(i, v)

        def z_chain(c):
            y0 = c * CHUNK
            part = pl.ds(y0 + PAD, CHUNK)
            own = pl.ds(y0, CHUNK)
            d = d_ref[place(0), part, :]
            f_lo = jnp.where(kz > 0, d_ref[place(-1), part, :] + d, 0.0)
            d_next = d_ref[place(1), part, :]
            g = d + d_next
            d = d_next
            ea = jnp.ones_like(g)
            ra = c4[HALO, part, :]
            e = ea
            r = c4[HALO + 1, part, :]
            for i in range(1, depth - 1):
                d_next = d_ref[place(i + 1), part, :]
                f = d + d_next
                d = d_next
                s = 1.0 / (e + g + f)
                wf, wg = f * s, g * s
                wz_ref[0, i, own, :] = wf
                wz_ref[1, i, own, :] = wg
                wz_ref[2, i, own, :] = r * s
                ea = ea + wg * e
                ra = ra + wg * r
                e = 1.0 + wf * e
                r = c4[HALO + i + 1, part, :] + wf * r
                g = wf * g
            f_hi = jnp.where(kz < nz - 1, d + d_ref[place(depth), part, :], 0.0)
            zr_ref[0, own, :] = jnp.where(left, ea, e)
            zr_ref[1, own, :] = jnp.where(left, ra, r)
            zr_ref[2, own, :] = jnp.where(left, e, ea)
            zr_ref[3, own, :] = jnp.where(left, r, ra)
            zr_ref[4, own, :] = g
            zr_ref[5, own, :] = jnp.where(left, f_hi, f_lo)
            zr_ref[6, own, :] = jnp.where(left, f_lo, f_hi)

            @pl.when(outermost)
            def _():
                z_inward(c, 0)

        outer = list(range(HALO)) + list(range(depth, depth + HALO))
        for c, batch in enumerate(needs):
            start, stop = c * CHUNK, (c + 1) * CHUNK
            tail = PAD if c + 1 == chunks else 0
            receive(batch, step)
            t0 = start + 2 * PAD if c else 0
            for z in outer:
                blur_layer(z, t0, stop + 2 * PAD - t0)
            b0 = start + PAD if c else 0
            b1 = stop + PAD
            blur_planes(outer, [(b0, b1 - b0)])
            blur_edges([(0, HALO), (depth, depth + HALO)], b0, b1)

            @pl.when(kz == 0)
            def _(b0=b0, b1=b1):
                b_ref[1, b0:b1, :] = jnp.zeros((b1 - b0, nx), jnp.float32)

            @pl.when(kz == nz - 1)
            def _(b0=b0, b1=b1):
                b_ref[depth + 2, b0:b1, :] = jnp.zeros((b1 - b0, nx), jnp.float32)

            for z in list(range(HALO)) + list(range(depth - 2, depth + 2)):
                diffuse(z, start, stop + tail - start)
            z_chain(c)
            if c == 0:
                y_join(1)

        def dx(i):
            return dt2[pl.ds(i, depth, stride=tall_x), :]

        def rx(i):
            return cur2[pl.ds(i, depth, stride=tall_x), :]

        def put_x(i, v):
            vx2[pl.ds(i, depth, stride=tall_x), :] = v

        def z_piece(k):
            @pl.when(jnp.logical_not(outermost))
            def _():
                z_inward(k, 0)

        y_begin(0)
        for k in range(chunks):
            z_piece(k)

        y_join(0)
        turn(0)

        states = line_reduce(dx, rx, wx_ref, nx, SEGMENTS)
        x_chain, levels_x = line_chain(dx, states, nx, jnp.zeros_like)
        line_back(put_x, wx_ref, nx, unmerge_all(levels_x, *solve_pair(*x_chain[:5])))

        @pl.loop(0, depth // 4)
        def _(k):
            for t in range(4):
                z = 4 * k + t
                xt_ref[z] = vx_ref[z, 0:nx, :].T

        @pl.when(jnp.logical_not(outermost))
        def _():
            @pl.loop(0, chunks)
            def _(c):
                z_solve(c)

        y_end(1)
        y_end(0)

        for c in range(chunks):
            @pl.when(outermost)
            def _(c=c):
                z_solve(c)

            z_finish(c)

            @pl.when(step + 1 < STEPS)
            def _(c=c):
                send(sends[c], later)

        for b in range(2):
            y_copy(b).wait_send()
            for j in range(1, groups):
                y_spread(b, j).wait_send()

        for i in range(len(messages)):
            for chosen, thin in forms(i, True):
                @pl.when(chosen)
                def _(i=i, thin=thin):
                    halo(i, step, thin)[0].wait_send()

        @pl.loop(0, chunks)
        def _(c):
            z_copy(c, slot_out).wait_send()

            @pl.when(jnp.logical_not(outermost))
            def _():
                z_back(c).wait_send()

    @pl.loop(0, depth // 4)
    def _(k):
        for t in range(4):
            z = 4 * k + t
            out[z] = c_ref[0, z + HALO, PAD:PAD + cols, :].T


def on_device(volume, contrast):
    depth, nx, cols = volume.shape
    ny = lax.axis_size("gy")
    nz = lax.axis_size("gz")
    groups = ny // 2
    assert ny % 2 == 0 and nz % 2 == 0 and depth == 2 * BATCH == 4 * HALO
    rows = cols + 3 * PAD
    chunks = cols // CHUNK
    f32 = jnp.float32
    dma = pltpu.SemaphoreType.DMA
    count = len(message_plan(cols)[0])
    return pl.pallas_call(
        functools.partial(kernel, ny, nz),
        out_shape=jax.ShapeDtypeStruct(volume.shape, f32),
        in_specs=[pl.BlockSpec(memory_space=pl.ANY)] * 2,
        out_specs=pl.BlockSpec(memory_space=pltpu.VMEM),
        scratch_shapes=[
            pltpu.VMEM((STEPS, depth + 2 * HALO, rows, nx), f32),
            pltpu.VMEM((depth + 4, rows, nx), f32),
            pltpu.VMEM((depth + 4, rows + 16, nx), f32),
            pltpu.VMEM((depth + 4, rows, nx), f32),
            pltpu.VMEM((3 * nx, 2 * nx), jnp.bfloat16),
            pltpu.VMEM((depth + 2, rows, nx), f32),
            pltpu.VMEM((depth, nx + SKEW, cols), f32),
            pltpu.VMEM((3, nx, depth, cols), f32),
            pltpu.VMEM((2, 3, cols, BATCH, nx), f32),
            pltpu.VMEM((3, depth, cols, nx), f32),
            pltpu.VMEM((depth, nx + SKEW, cols), f32),
            pltpu.VMEM((depth, cols + SKEW, nx), f32),
            pltpu.VMEM((depth, cols, nx), f32),
            pltpu.VMEM((BATCH, cols + SKEW, nx), f32),
            pltpu.VMEM((depth, nx + SKEW, cols), f32),
            pltpu.VMEM((7, cols, nx), f32),
            pltpu.VMEM((6, cols, nx), f32),
            pltpu.VMEM((STEPS, chunks, 2, CHUNK, nx), f32),
            pltpu.VMEM((STEPS, 2, chunks, 2, CHUNK, nx), f32),
            pltpu.VMEM((STEPS, chunks, CHUNK, nx), f32),
            pltpu.VMEM((STEPS, chunks, CHUNK, nx), f32),
            pltpu.VMEM((STEPS, 2, 6, BATCH, nx), f32),
            pltpu.VMEM((STEPS, 2, 6, BATCH, nx), f32),
            pltpu.VMEM((STEPS, 2, groups, 5, BATCH, nx), f32),
            pltpu.VMEM((2, groups + 1, BATCH, nx), f32),
            pltpu.VMEM((1, nx), f32), dma((depth // HALO + 1,)),
            dma((STEPS, count)), dma((STEPS, count)),
            dma((STEPS, 2, chunks)), dma((STEPS, 2, chunks)),
            dma((STEPS, chunks)), dma((STEPS, chunks)),
            dma((STEPS, 2)), dma((STEPS, 2)),
            dma((STEPS, 2, groups)), dma((STEPS, 2, groups)),
        ],
        compiler_params=pltpu.CompilerParams(
            collective_id=0, has_side_effects=True, vmem_limit_bytes=52 * 2 ** 20
        ),
    )(volume, contrast.reshape(1, nx))


def solution(mesh):
    in_specs = (P("gz", None, "gy"), P())
    out_specs = P("gz", None, "gy")
    return jax.shard_map(
        on_device, mesh=mesh, in_specs=in_specs, out_specs=out_specs, check_vma=False
    )
```

```python
import functools

import jax
import jax.numpy as jnp
from jax import lax
from jax.experimental import pallas as pl
from jax.experimental.pallas import tpu as pltpu
from jax.sharding import PartitionSpec as P

STEPS = 2
TAPS = (0.05448868, 0.24420134, 0.40261995, 0.24420134, 0.05448868)
SCALE = 600.0
MESH = pl.DeviceIdType.MESH
DIRECTIONS = [(dy, dz) for dz in (-1, 1, 0) for dy in (0, -1, 1) if (dy, dz) != (0, 0)]
PAD = 8
HALO = 4
CHUNK = 32
STENCIL_ROWS = 48
SEGMENTS = 4
SEGMENTS_Y = 8
BATCH = 8
SKEW = 8


def message_plan(cols):
    chunks = cols // CHUNK
    last = chunks - 1
    messages, sends, needs, edge_rows = [], [[] for _ in range(chunks)], [[] for _ in range(chunks)], []

    def add(message, sent, needed):
        sends[sent].append(len(messages))
        (edge_rows if needed is None else needs[needed]).append(len(messages))
        messages.append(message)

    add((-1, 0, 0, 0), 0, None)
    add((1, 0, 0, 0), last, None)
    for dz in (-1, 1):
        add((1, dz, 0, 0), last, 0)
        add((-1, dz, 0, 0), 0, last)
    starts = [c * CHUNK for c in range(chunks)] + [last * CHUNK + PAD]
    for start, stop in zip(starts, starts[1:] + [cols]):
        for dz in (-1, 1):
            needed = max(0, (start - PAD) // CHUNK) if start < last * CHUNK + PAD else last
            add((0, dz, start, stop - start), start // CHUNK, needed)
    return messages, sends, needs, edge_rows


def merge(left, right):
    ea, ra, eb, rb, g, f = left
    ea2, ra2, eb2, rb2, g2, f2 = right
    s1 = 1.0 / (eb + g + f)
    wg, wf, q1 = g * s1, f * s1, rb * s1
    ea = ea + wg * eb
    ra = ra + wg * rb
    ea2 = ea2 + wf * eb
    ra2 = ra2 + wf * rb
    g1 = wf * g
    s2 = 1.0 / (ea2 + g1 + g2)
    vg, vf, q2 = g1 * s2, g2 * s2, ra2 * s2
    joined = (ea + vg * ea2, ra + vg * ra2, eb2 + vf * ea2, rb2 + vf * ra2, vf * g1, f2)
    return joined, (wg, wf, q1, vg, vf, q2)


def unmerge(weights, va, vb):
    wg, wf, q1, vg, vf, q2 = weights
    inner_right = vg * va + vf * vb + q2
    inner_left = wg * va + wf * inner_right + q1
    return inner_left, inner_right


def solve_pair(ea, ra, eb, rb, g):
    s = 1.0 / (ea + g)
    w = g * s
    vb = (rb + w * ra) / (eb + w * ea)
    return w * vb + ra * s, vb


def merge_all(chains):
    levels = []
    while len(chains) > 1:
        pairs = [merge(chains[i], chains[i + 1]) for i in range(0, len(chains), 2)]
        chains = [p[0] for p in pairs]
        levels.append([p[1] for p in pairs])
    return chains[0], levels


def unmerge_all(levels, va, vb):
    ends = [(va, vb)]
    for level in reversed(levels):
        split = []
        for weights, (a, b) in zip(level, ends):
            inner_left, inner_right = unmerge(weights, a, b)
            split += [(a, inner_left), (inner_right, b)]
        ends = split
    return ends


def line_start(get_d, get_r, count, segments):
    states = []
    for base in range(0, count, count // segments):
        d0, d1 = get_d(base), get_d(base + 1)
        one = jnp.ones_like(d0)
        states.append((one, get_r(base), d0 + d1, one, get_r(base + 1), d1))
    return tuple(states)


def line_reduce(get_d, get_r, weights, count, segments):
    size = count // segments

    def body(i, states):
        new = []
        for k, (ea, ra, g, e, r, d) in enumerate(states):
            j = k * size + i
            d1 = get_d(j + 1)
            f = d + d1
            s = 1.0 / (e + g + f)
            wf, wg = f * s, g * s
            weights[0, j] = wf
            weights[1, j] = wg
            weights[2, j] = r * s
            new.append((ea + wg * e, ra + wg * r, wf * g, 1.0 + wf * e, get_r(j + 1) + wf * r, d1))
        return tuple(new)

    return lax.fori_loop(1, size - 1, body, line_start(get_d, get_r, count, segments))


def line_chain(get_d, states, count, edge):
    segments = len(states)
    size = count // segments
    chains = []
    for k, (ea, ra, g, e, r, d) in enumerate(states):
        f = d + get_d((k + 1) * size) if k + 1 < segments else edge(d)
        chains.append((ea, ra, e, r, g, f))
    return merge_all(chains)


def line_back(put, weights, count, ends):
    size = count // len(ends)
    for k, (a, b) in enumerate(ends):
        put(k * size, a)
        put(k * size + size - 1, b)

    def body(t, values):
        new = []
        for k, v in enumerate(values):
            j = k * size + size - 2 - t
            v = weights[0, j] * v + (weights[1, j] * ends[k][0] + weights[2, j])
            put(j, v)
            new.append(v)
        return tuple(new)

    lax.fori_loop(0, size - 2, body, tuple(b for a, b in ends), unroll=3 if (size - 2) % 3 == 0 else 2)


def kernel(ny, nz, vol, contrast_in, out, c_ref, t_ref, b_ref, gx_ref, w_ref, d_ref, dt_ref, wx_ref, wy_ref, wz_ref, vx_ref, vy_ref,
           xt_ref, ce_ref, cur_ref, zr_ref, zi_ref, zsend, zbuf, zvsend, zv, ysend, yrecv, yall, yv_ref,
           con, load_s, halo_s, halo_r, zs, zrs, zvs, zvr, ys, yr, yas, yar):
    depth, nx, cols = vol.shape
    rows = cols + 3 * PAD
    tall = depth + 2 * HALO
    chunks = cols // CHUNK
    ky = lax.axis_index("gy")
    kz = lax.axis_index("gz")

    def at(y, z):
        return {"gy": y, "gz": z}

    def exists(dy, dz):
        ok = True
        if dy:
            ok = (ky + dy >= 0) & (ky + dy < ny)
        if dz:
            ok = ok & (kz + dz >= 0) & (kz + dz < nz)
        return ok

    groups = ny // 2
    side = lax.rem(ky, 2)
    group = lax.div(ky, 2)
    twin = ky + 1 - 2 * side

    def member(j):
        return 2 * lax.rem(group + j, groups) + side

    def load(k):
        return pltpu.make_async_copy(
            vol.at[pl.ds(k * HALO, HALO)], cur_ref.at[pl.ds(k * HALO, HALO), pl.ds(0, nx), :], load_s.at[k])

    load_contrast = pltpu.make_async_copy(contrast_in, con, load_s.at[depth // HALO])
    for k in range(depth // HALO):
        load(k).start()
    load_contrast.start()

    barrier = pltpu.get_barrier_semaphore()
    expected = jnp.int32(groups)
    for dy, dz in DIRECTIONS:
        ok = exists(dy, dz)
        expected = expected + jnp.where(ok, 1, 0)

        @pl.when(ok)
        def _(dy=dy, dz=dz):
            pl.semaphore_signal(barrier, inc=1, device_id=at(ky + dy, kz + dz), device_id_type=MESH)

    for y in [twin] + [member(j) for j in range(1, groups)]:
        pl.semaphore_signal(barrier, inc=1, device_id=at(y, kz), device_id_type=MESH)

    source = lax.broadcasted_iota(jnp.int32, (nx, nx), 0)
    target = lax.broadcasted_iota(jnp.int32, (nx, nx), 1)

    def taps_at(target):
        apart = jnp.where((target >= 0) & (target < nx), jnp.abs(source - target), 3)
        return jnp.where(apart == 0, TAPS[2], jnp.where(apart == 1, TAPS[1], jnp.where(apart == 2, TAPS[0], 0.0)))

    for half, matrix in enumerate((taps_at(target), taps_at(target + 1) - taps_at(target - 1))):
        part = slice(half * nx, half * nx + nx)
        coarse = matrix.astype(jnp.bfloat16)
        w_ref[0:nx, part] = coarse
        w_ref[nx:2 * nx, part] = coarse
        w_ref[2 * nx:, part] = (matrix - coarse.astype(jnp.float32)).astype(jnp.bfloat16)

    load_contrast.wait()

    @pl.loop(0, depth // HALO)
    def _(k):
        load(k).wait()
        for t in range(HALO):
            z = HALO * k + t
            c_ref[0, z + HALO, PAD:PAD + cols, :] = cur_ref[z, 0:nx, :].T

    pl.semaphore_wait(barrier, expected)

    left = kz < nz // 2
    inward = jnp.where(left, 1, -1)
    order = jnp.where(left, kz, nz - 1 - kz)
    middle = order == nz // 2 - 1
    outermost = order == 0
    slot_out = jnp.where(middle, 1, 0)

    contrast = con[...]
    squared = jnp.broadcast_to(contrast * contrast, (STENCIL_ROWS, nx))

    tall_x = nx + SKEW
    tall_y = cols + SKEW
    cur2 = cur_ref.reshape(depth * tall_x, cols)
    dt2 = dt_ref.reshape(depth * tall_x, cols)
    vx2 = vx_ref.reshape(depth * tall_x, cols)
    vy2 = vy_ref.reshape(depth * tall_y, nx)
    d2 = d_ref.reshape((depth + 2) * rows, nx)
    ce2 = ce_ref.reshape(BATCH * tall_y, nx)

    def place(z):
        if z < 0 or z >= depth:
            return depth if z < 0 else depth + 1
        if z < HALO:
            return z
        return z - BATCH if z >= depth - HALO else z + HALO

    messages, sends, needs, edge_rows = message_plan(cols)

    def halo(i, slot, thin=False):
        dy, dz, start, size = messages[i]
        deep = HALO - 1 if thin else HALO
        src_y = {0: (PAD + start, size), 1: (cols, PAD), -1: (PAD, PAD)}[dy]
        dst_y = {0: (PAD + start, size), 1: (0, PAD), -1: (PAD + cols, PAD)}[dy]
        src_z = {0: (HALO, depth), 1: (depth + HALO - deep, deep), -1: (HALO, deep)}[dz]
        dst_z = {0: (HALO, depth), 1: (HALO - deep, deep), -1: (HALO + depth, deep)}[dz]
        volume = c_ref.at[slot]
        copy = pltpu.make_async_remote_copy(
            src_ref=volume.at[pl.ds(*src_z), pl.ds(*src_y), :], dst_ref=volume.at[pl.ds(*dst_z), pl.ds(*dst_y), :],
            send_sem=halo_s.at[slot, i], recv_sem=halo_r.at[slot, i],
            device_id=at(ky + dy, kz + dz), device_id_type=MESH)
        return copy, dst_z, dst_y

    def forms(i, at_sender):
        dy, dz = messages[i][:2]
        here = exists(dy, dz) if at_sender else exists(-dy, -dz)
        if dy or not dz:
            return [(here, False)]
        sender = kz if at_sender else kz - dz
        outward = sender >= nz // 2 if dz > 0 else sender < nz // 2
        return [(here & outward, True), (here & jnp.logical_not(outward), False)]

    def send(batch, slot):
        for i in batch:
            dy, dz = messages[i][:2]
            _, dst_z, dst_y = halo(i, slot)
            for chosen, thin in forms(i, True):
                @pl.when(chosen)
                def _(i=i, thin=thin):
                    halo(i, slot, thin)[0].start()

            @pl.when(jnp.logical_not(exists(-dy, -dz)))
            def _(dst_z=dst_z, dst_y=dst_y):
                c_ref[slot, pl.ds(*dst_z), pl.ds(*dst_y), :] = jnp.zeros((dst_z[1], dst_y[1], nx), jnp.float32)

    def receive(batch, slot):
        for i in batch:
            for chosen, thin in forms(i, False):
                @pl.when(chosen)
                def _(i=i, thin=thin):
                    halo(i, slot, thin)[0].wait_recv()

    send(range(len(messages)), 0)

    @pl.loop(0, STEPS)
    def _(step):
        c4 = c_ref.at[step]
        c2 = c4.reshape(tall * rows, nx)
        later = lax.rem(step + 1, STEPS)

        def blur_layer(z, r0, size):
            part = pl.ds(r0, size)
            total = TAPS[2] * c4[z + 2, part, :]
            total = total + TAPS[1] * (c4[z + 1, part, :] + c4[z + 3, part, :])
            total = total + TAPS[0] * (c4[z, part, :] + c4[z + 4, part, :])
            t_ref[z, pl.ds(r0, size), :] = total

        def blur_planes(planes, pieces):
            totals = []
            for z in planes:
                for r0, size in pieces:
                    def tap(o):
                        return t_ref[z, pl.ds(r0 + 4 + o, size), :]
                    totals.append(TAPS[2] * tap(0) + TAPS[1] * (tap(-1) + tap(1)) + TAPS[0] * (tap(-2) + tap(2)))
            total = jnp.concatenate(totals)
            coarse = total.astype(jnp.bfloat16)
            fine = (total - coarse.astype(jnp.float32)).astype(jnp.bfloat16)

            both = jnp.dot(jnp.concatenate([coarse, fine], axis=1), w_ref[0:2 * nx], preferred_element_type=jnp.float32)
            both = both + jnp.dot(coarse, w_ref[2 * nx:], preferred_element_type=jnp.float32)
            start = 0
            for z in planes:
                for r0, size in pieces:
                    b_ref[z, pl.ds(r0, size), :] = both[start:start + size, :nx]
                    gx_ref[z, pl.ds(r0, size), :] = both[start:start + size, nx:]
                    start += size

        def blur_edges(spans, low, high):
            for row, present in ((PAD - 5, ky > 0), (cols + PAD - 4, ky < ny - 1)):
                if low <= row < high:
                    @pl.when(jnp.logical_not(present))
                    def _(row=row):
                        for z0, z1 in spans:
                            b_ref[z0:z1, row:row + 1, :] = jnp.zeros((z1 - z0, 1, nx), jnp.float32)

        def diffuse(z, r0, size, spot=None):
            grad_x = gx_ref[z + 1, pl.ds(r0 + 4, size), :]
            grad_z = b_ref[z + 2, pl.ds(r0 + 4, size), :] - b_ref[z, pl.ds(r0 + 4, size), :]
            grad_y = b_ref[z + 1, pl.ds(r0 + 5, size), :] - b_ref[z + 1, pl.ds(r0 + 3, size), :]
            square = (grad_x * grad_x + grad_y * grad_y + grad_z * grad_z) * 0.25
            d_ref[place(z - 1) if spot is None else spot, pl.ds(r0 + PAD, size), :] = (SCALE * squared[:size]) / (squared[:size] + square)

        inner = list(range(HALO, depth))
        own_rows = [(r0, min(STENCIL_ROWS, cols + PAD - r0)) for r0 in range(PAD, cols + PAD, STENCIL_ROWS)]
        bulk = [(r0, min(STENCIL_ROWS, cols - r0)) for r0 in range(PAD, cols, STENCIL_ROWS)]
        bulk_d = [(r0, min(STENCIL_ROWS, cols - PAD - r0)) for r0 in range(PAD, cols - PAD, STENCIL_ROWS)]

        @pl.loop(HALO, depth)
        def _(z):
            for piece in own_rows:
                blur_layer(z, *piece)

        @pl.loop(0, (depth - HALO) // 2)
        def _(k):
            blur_planes([HALO + 2 * k, HALO + 2 * k + 1], bulk)

        for piece in bulk_d:
            diffuse(HALO, *piece)
            diffuse(depth - HALO + 1, *piece)

        @pl.loop(0, BATCH // 2)
        def _(k):
            for t in range(2):
                for piece in bulk_d:
                    diffuse(HALO + 1 + 2 * k + t, *piece, BATCH + 2 * k + t)

        @pl.loop(0, 2)
        def _(k):
            for t in range(HALO):
                ce_ref[HALO * k + t, 0:cols, :] = c4[HALO + (depth - HALO) * k + t, PAD:PAD + cols, :]

        @pl.when(step > 0)
        def _():
            @pl.loop(0, depth // 4)
            def _(k):
                for t in range(4):
                    z = 4 * k + t
                    cur_ref[z, 0:nx, :] = c4[z + HALO, PAD:PAD + cols, :].T

        receive(edge_rows, step)
        for z in inner:
            blur_layer(z, 0, PAD)
            blur_layer(z, cols + PAD, PAD)
        blur_planes(inner, [(0, PAD), (cols, PAD)])
        blur_edges([(HALO, depth)], 0, cols + PAD)
        for z in range(HALO, depth - 2):
            diffuse(z, 0, PAD)
            diffuse(z, cols - PAD, 2 * PAD)

        def y_at(b):
            def get_d(i):
                return d2[pl.ds(i + b * BATCH * rows + PAD, BATCH, stride=rows), :]

            def get_r(i):
                if b:
                    return c2[pl.ds(i + 2 * HALO * rows + PAD, BATCH, stride=rows), :]
                return ce2[pl.ds(i, BATCH, stride=tall_y), :]

            def put(i, v):
                vy2[pl.ds(i + b * BATCH * tall_y, BATCH, stride=tall_y), :] = v

            return get_d, get_r, put

        def y_copy(b):
            return pltpu.make_async_remote_copy(
                src_ref=ysend.at[step, b], dst_ref=yrecv.at[step, b], send_sem=ys.at[step, b],
                recv_sem=yr.at[step, b], device_id=at(twin, kz), device_id_type=MESH)

        def y_spread(b, j):
            return pltpu.make_async_remote_copy(
                src_ref=yall.at[step, b, 0], dst_ref=yall.at[step, b, j], send_sem=yas.at[step, b, j],
                recv_sem=yar.at[step, b, j], device_id=at(member(j), kz), device_id_type=MESH)

        first = side == 0
        held = [None, None]

        def y_begin(b):
            get_d, get_r, _ = y_at(b)
            states = line_reduce(get_d, get_r, wy_ref.at[b], cols, SEGMENTS_Y)
            chain, levels = line_chain(
                get_d, states, cols, lambda d: jnp.where(ky < ny - 1, d + get_d(cols), 0.0))
            for j in range(6):
                ysend[step, b, j] = chain[j]
            y_copy(b).start()
            held[b] = levels

        def y_join(b):
            chain = tuple(ysend[step, b, j] for j in range(6))
            y_copy(b).wait_recv()
            other = tuple(yrecv[step, b, j] for j in range(6))
            pair_l = tuple(jnp.where(first, a, b) for a, b in zip(chain, other))
            pair_r = tuple(jnp.where(first, b, a) for a, b in zip(chain, other))
            (ea, ra, eb, rb, g, f), pair = merge(pair_l, pair_r)
            s = 1.0 / (eb + g + f)
            wg, wf, q = g * s, f * s, rb * s
            for j, value in enumerate((ea + wg * eb, ra + wg * rb, wf * eb, wf * rb, wf * g)):
                yall[step, b, 0, j] = value
            for j in range(1, groups):
                y_spread(b, j).start()
            held[b] = (held[b], pair, wg, wf, q)

        def y_end(b):
            levels, pair, wg, wf, q = held[b]
            for j in range(1, groups):
                y_spread(b, j).wait_recv()
            e, r, de, dr, link = [yall[step, b, lax.rem(group, groups), j] for j in range(5)]
            ways = []
            for m in range(1, groups):
                s = 1.0 / (e + link)
                w = link * s
                ways.append((w, r * s))
                e, r = w * e + de, w * r + dr
                here = [yall[step, b, lax.rem(group - m + groups, groups), j] for j in range(5)]
                e, r = e + here[0], r + here[1]
                de, dr, link = here[2:]
            v = r / e
            yv_ref[b, groups] = jnp.zeros_like(v)
            yv_ref[b, groups - 1] = v
            for m in range(groups - 2, -1, -1):
                v = ways[m][0] * v + ways[m][1]
                yv_ref[b, m] = v
            va = yv_ref[b, group]
            vb = wg * va + (wf * yv_ref[b, group + 1] + q)
            inner_l, inner_r = unmerge(pair, va, vb)
            va, vb = jnp.where(first, va, inner_r), jnp.where(first, inner_l, vb)
            line_back(y_at(b)[2], wy_ref.at[b], cols, unmerge_all(levels, va, vb))

        def turn(b):
            @pl.loop(0, 2)
            def _(k):
                for t in range(HALO):
                    z = HALO + HALO * k + t if b else (depth - HALO) * k + t
                    dt_ref[z, 0:nx, :] = d_ref[b * BATCH + HALO * k + t, PAD:PAD + cols, :].T

        y_begin(1)
        turn(1)

        def z_copy(c, slot):
            return pltpu.make_async_remote_copy(
                src_ref=zsend.at[step, c], dst_ref=zbuf.at[step, slot, c], send_sem=zs.at[step, slot, c],
                recv_sem=zrs.at[step, slot, c], device_id=at(ky, kz + inward), device_id_type=MESH)

        def z_back(c):
            return pltpu.make_async_remote_copy(
                src_ref=zvsend.at[step, c], dst_ref=zv.at[step, c], send_sem=zvs.at[step, c],
                recv_sem=zvr.at[step, c], device_id=at(ky, kz - inward), device_id_type=MESH)

        def z_inward(c, carry):
            own = pl.ds(pl.multiple_of(c * CHUNK, CHUNK), CHUNK)

            @pl.when(jnp.logical_not(outermost))
            def _():
                z_copy(c, 0).wait_recv()
                f = zr_ref[6, own, :]
                s = 1.0 / (zbuf[step, 0, c, 0] + f)
                u = f * s
                zi_ref[4, own, :] = u
                zi_ref[5, own, :] = zbuf[step, 0, c, 1] * s
                zr_ref[0, own, :] += u * zbuf[step, 0, c, 0]
                zr_ref[1, own, :] += u * zbuf[step, 0, c, 1]

            eo, ro, ei, ri, g, f = [zr_ref[j, own, :] for j in range(6)]
            s = 1.0 / (eo + g)
            w = g * s
            ei = ei + w * eo
            ri = ri + w * ro
            u = jnp.where(middle, f / (ei + f), 1.0)
            zi_ref[0, own, :] = w
            zi_ref[1, own, :] = ro * s
            zi_ref[2, own, :] = ei
            zi_ref[3, own, :] = ri
            zsend[step, c, 0] = u * ei
            zsend[step, c, 1] = u * ri
            z_copy(c, slot_out).start()
            return carry

        def z_solve(c):
            own = pl.ds(pl.multiple_of(c * CHUNK, CHUNK), CHUNK)

            @pl.when(middle)
            def _():
                z_copy(c, 1).wait_recv()
                zr_ref[0, own, :] = (zi_ref[3, own, :] + zbuf[step, 1, c, 1]) / (zi_ref[2, own, :] + zbuf[step, 1, c, 0])

            @pl.when(jnp.logical_not(middle))
            def _():
                z_back(c).wait_recv()
                zr_ref[0, own, :] = zv[step, c]

            vo = zi_ref[0, own, :] * zr_ref[0, own, :] + zi_ref[1, own, :]
            zr_ref[1, own, :] = vo

            @pl.when(jnp.logical_not(outermost))
            def _():
                zvsend[step, c] = zi_ref[4, own, :] * vo + zi_ref[5, own, :]
                z_back(c).start()

        def z_finish(c):
            own = pl.ds(c * CHUNK, CHUNK)
            padded = pl.ds(c * CHUNK + PAD, CHUNK)

            def put(i, v):
                c_ref[later, HALO + i, padded, :] = (vy_ref[place(i), own, :] + xt_ref[i, own, :] + v) * (1.0 / 3.0)

            vi, vo = zr_ref[0, own, :], zr_ref[1, own, :]
            va = jnp.where(left, vo, vi)
            v = jnp.where(left, vi, vo)
            put(0, va)
            put(depth - 1, v)
            for i in range(depth - 2, 0, -1):
                v = wz_ref[0, i, own, :] * v + (wz_ref[1, i, own, :] * va + wz_ref[2, i, own, :])
                put(i, v)

        def z_chain(c):
            y0 = c * CHUNK
            part = pl.ds(y0 + PAD, CHUNK)
            own = pl.ds(y0, CHUNK)
            d = d_ref[place(0), part, :]
            f_lo = jnp.where(kz > 0, d_ref[place(-1), part, :] + d, 0.0)
            d_next = d_ref[place(1), part, :]
            g = d + d_next
            d = d_next
            ea = jnp.ones_like(g)
            ra = c4[HALO, part, :]
            e = ea
            r = c4[HALO + 1, part, :]
            for i in range(1, depth - 1):
                d_next = d_ref[place(i + 1), part, :]
                f = d + d_next
                d = d_next
                s = 1.0 / (e + g + f)
                wf, wg = f * s, g * s
                wz_ref[0, i, own, :] = wf
                wz_ref[1, i, own, :] = wg
                wz_ref[2, i, own, :] = r * s
                ea = ea + wg * e
                ra = ra + wg * r
                e = 1.0 + wf * e
                r = c4[HALO + i + 1, part, :] + wf * r
                g = wf * g
            f_hi = jnp.where(kz < nz - 1, d + d_ref[place(depth), part, :], 0.0)
            zr_ref[0, own, :] = jnp.where(left, ea, e)
            zr_ref[1, own, :] = jnp.where(left, ra, r)
            zr_ref[2, own, :] = jnp.where(left, e, ea)
            zr_ref[3, own, :] = jnp.where(left, r, ra)
            zr_ref[4, own, :] = g
            zr_ref[5, own, :] = jnp.where(left, f_hi, f_lo)
            zr_ref[6, own, :] = jnp.where(left, f_lo, f_hi)

            @pl.when(outermost)
            def _():
                z_inward(c, 0)

        outer = list(range(HALO)) + list(range(depth, depth + HALO))
        for c, batch in enumerate(needs):
            start, stop = c * CHUNK, (c + 1) * CHUNK
            tail = PAD if c + 1 == chunks else 0
            receive(batch, step)
            t0 = start + 2 * PAD if c else 0
            for z in outer:
                blur_layer(z, t0, stop + 2 * PAD - t0)
            b0 = start + PAD if c else 0
            b1 = stop + PAD
            blur_planes(outer, [(b0, b1 - b0)])
            blur_edges([(0, HALO), (depth, depth + HALO)], b0, b1)

            @pl.when(kz == 0)
            def _(b0=b0, b1=b1):
                b_ref[1, b0:b1, :] = jnp.zeros((b1 - b0, nx), jnp.float32)

            @pl.when(kz == nz - 1)
            def _(b0=b0, b1=b1):
                b_ref[depth + 2, b0:b1, :] = jnp.zeros((b1 - b0, nx), jnp.float32)

            for z in list(range(HALO)) + list(range(depth - 2, depth + 2)):
                diffuse(z, start, stop + tail - start)
            z_chain(c)
            if c == 0:
                y_join(1)

        def dx(i):
            return dt2[pl.ds(i, depth, stride=tall_x), :]

        def rx(i):
            return cur2[pl.ds(i, depth, stride=tall_x), :]

        def put_x(i, v):
            vx2[pl.ds(i, depth, stride=tall_x), :] = v

        def z_piece(k):
            @pl.when(jnp.logical_not(outermost))
            def _():
                z_inward(k, 0)

        z_piece(0)
        y_begin(0)
        for k in range(1, chunks):
            z_piece(k)

        y_join(0)
        turn(0)

        states = line_reduce(dx, rx, wx_ref, nx, SEGMENTS)
        x_chain, levels_x = line_chain(dx, states, nx, jnp.zeros_like)
        line_back(put_x, wx_ref, nx, unmerge_all(levels_x, *solve_pair(*x_chain[:5])))

        @pl.when(jnp.logical_not(outermost))
        def _():
            @pl.loop(0, chunks)
            def _(c):
                z_solve(c)

        @pl.loop(0, depth // 4)
        def _(k):
            for t in range(4):
                z = 4 * k + t
                xt_ref[z] = vx_ref[z, 0:nx, :].T

        y_end(1)
        y_end(0)

        for c in range(chunks):
            @pl.when(outermost)
            def _(c=c):
                z_solve(c)

            z_finish(c)

            @pl.when(step + 1 < STEPS)
            def _(c=c):
                send(sends[c], later)

        for b in range(2):
            y_copy(b).wait_send()
            for j in range(1, groups):
                y_spread(b, j).wait_send()

        for i in range(len(messages)):
            for chosen, thin in forms(i, True):
                @pl.when(chosen)
                def _(i=i, thin=thin):
                    halo(i, step, thin)[0].wait_send()

        @pl.loop(0, chunks)
        def _(c):
            z_copy(c, slot_out).wait_send()

            @pl.when(jnp.logical_not(outermost))
            def _():
                z_back(c).wait_send()

    @pl.loop(0, depth // 4)
    def _(k):
        for t in range(4):
            z = 4 * k + t
            out[z] = c_ref[0, z + HALO, PAD:PAD + cols, :].T


def on_device(volume, contrast):
    depth, nx, cols = volume.shape
    ny = lax.axis_size("gy")
    nz = lax.axis_size("gz")
    groups = ny // 2
    assert ny % 2 == 0 and nz % 2 == 0 and depth == 2 * BATCH == 4 * HALO
    rows = cols + 3 * PAD
    chunks = cols // CHUNK
    f32 = jnp.float32
    dma = pltpu.SemaphoreType.DMA
    count = len(message_plan(cols)[0])
    return pl.pallas_call(
        functools.partial(kernel, ny, nz),
        out_shape=jax.ShapeDtypeStruct(volume.shape, f32),
        in_specs=[pl.BlockSpec(memory_space=pl.ANY)] * 2,
        out_specs=pl.BlockSpec(memory_space=pltpu.VMEM),
        scratch_shapes=[
            pltpu.VMEM((STEPS, depth + 2 * HALO, rows, nx), f32),
            pltpu.VMEM((depth + 4, rows, nx), f32),
            pltpu.VMEM((depth + 4, rows + 16, nx), f32),
            pltpu.VMEM((depth + 4, rows, nx), f32),
            pltpu.VMEM((3 * nx, 2 * nx), jnp.bfloat16),
            pltpu.VMEM((depth + 2, rows, nx), f32),
            pltpu.VMEM((depth, nx + SKEW, cols), f32),
            pltpu.VMEM((3, nx, depth, cols), f32),
            pltpu.VMEM((2, 3, cols, BATCH, nx), f32),
            pltpu.VMEM((3, depth, cols, nx), f32),
            pltpu.VMEM((depth, nx + SKEW, cols), f32),
            pltpu.VMEM((depth, cols + SKEW, nx), f32),
            pltpu.VMEM((depth, cols, nx), f32),
            pltpu.VMEM((BATCH, cols + SKEW, nx), f32),
            pltpu.VMEM((depth, nx + SKEW, cols), f32),
            pltpu.VMEM((7, cols, nx), f32),
            pltpu.VMEM((6, cols, nx), f32),
            pltpu.VMEM((STEPS, chunks, 2, CHUNK, nx), f32),
            pltpu.VMEM((STEPS, 2, chunks, 2, CHUNK, nx), f32),
            pltpu.VMEM((STEPS, chunks, CHUNK, nx), f32),
            pltpu.VMEM((STEPS, chunks, CHUNK, nx), f32),
            pltpu.VMEM((STEPS, 2, 6, BATCH, nx), f32),
            pltpu.VMEM((STEPS, 2, 6, BATCH, nx), f32),
            pltpu.VMEM((STEPS, 2, groups, 5, BATCH, nx), f32),
            pltpu.VMEM((2, groups + 1, BATCH, nx), f32),
            pltpu.VMEM((1, nx), f32), dma((depth // HALO + 1,)),
            dma((STEPS, count)), dma((STEPS, count)),
            dma((STEPS, 2, chunks)), dma((STEPS, 2, chunks)),
            dma((STEPS, chunks)), dma((STEPS, chunks)),
            dma((STEPS, 2)), dma((STEPS, 2)),
            dma((STEPS, 2, groups)), dma((STEPS, 2, groups)),
        ],
        compiler_params=pltpu.CompilerParams(
            collective_id=0, has_side_effects=True, vmem_limit_bytes=52 * 2 ** 20
        ),
    )(volume, contrast.reshape(1, nx))


def solution(mesh):
    in_specs = (P("gz", None, "gy"), P())
    out_specs = P("gz", None, "gy")
    return jax.shard_map(
        on_device, mesh=mesh, in_specs=in_specs, out_specs=out_specs, check_vma=False
    )
```

```python
import functools

import jax
import jax.numpy as jnp
from jax import lax
from jax.experimental import pallas as pl
from jax.experimental.pallas import tpu as pltpu
from jax.sharding import PartitionSpec as P

STEPS = 2
TAPS = (0.05448868, 0.24420134, 0.40261995, 0.24420134, 0.05448868)
SCALE = 600.0
MESH = pl.DeviceIdType.MESH
DIRECTIONS = [(dy, dz) for dz in (-1, 1, 0) for dy in (0, -1, 1) if (dy, dz) != (0, 0)]
PAD = 8
HALO = 4
CHUNK = 32
STENCIL_ROWS = 48
SEGMENTS = 4
SEGMENTS_Y = 8
BATCH = 8
SKEW = 8


def message_plan(cols):
    chunks = cols // CHUNK
    last = chunks - 1
    messages, sends, needs, edge_rows = [], [[] for _ in range(chunks)], [[] for _ in range(chunks)], []

    def add(message, sent, needed):
        sends[sent].append(len(messages))
        (edge_rows if needed is None else needs[needed]).append(len(messages))
        messages.append(message)

    add((-1, 0, 0, 0), 0, None)
    add((1, 0, 0, 0), last, None)
    for dz in (-1, 1):
        add((1, dz, 0, 0), last, 0)
        add((-1, dz, 0, 0), 0, last)
    starts = [c * CHUNK for c in range(chunks)] + [last * CHUNK + PAD]
    for start, stop in zip(starts, starts[1:] + [cols]):
        for dz in (-1, 1):
            needed = max(0, (start - PAD) // CHUNK) if start < last * CHUNK + PAD else last
            add((0, dz, start, stop - start), start // CHUNK, needed)
    return messages, sends, needs, edge_rows


def merge(left, right):
    ea, ra, eb, rb, g, f = left
    ea2, ra2, eb2, rb2, g2, f2 = right
    s1 = 1.0 / (eb + g + f)
    wg, wf, q1 = g * s1, f * s1, rb * s1
    ea = ea + wg * eb
    ra = ra + wg * rb
    ea2 = ea2 + wf * eb
    ra2 = ra2 + wf * rb
    g1 = wf * g
    s2 = 1.0 / (ea2 + g1 + g2)
    vg, vf, q2 = g1 * s2, g2 * s2, ra2 * s2
    joined = (ea + vg * ea2, ra + vg * ra2, eb2 + vf * ea2, rb2 + vf * ra2, vf * g1, f2)
    return joined, (wg, wf, q1, vg, vf, q2)


def unmerge(weights, va, vb):
    wg, wf, q1, vg, vf, q2 = weights
    inner_right = vg * va + vf * vb + q2
    inner_left = wg * va + wf * inner_right + q1
    return inner_left, inner_right


def solve_pair(ea, ra, eb, rb, g):
    s = 1.0 / (ea + g)
    w = g * s
    vb = (rb + w * ra) / (eb + w * ea)
    return w * vb + ra * s, vb


def merge_all(chains):
    levels = []
    while len(chains) > 1:
        pairs = [merge(chains[i], chains[i + 1]) for i in range(0, len(chains), 2)]
        chains = [p[0] for p in pairs]
        levels.append([p[1] for p in pairs])
    return chains[0], levels


def unmerge_all(levels, va, vb):
    ends = [(va, vb)]
    for level in reversed(levels):
        split = []
        for weights, (a, b) in zip(level, ends):
            inner_left, inner_right = unmerge(weights, a, b)
            split += [(a, inner_left), (inner_right, b)]
        ends = split
    return ends


def line_start(get_d, get_r, count, segments):
    states = []
    for base in range(0, count, count // segments):
        d0, d1 = get_d(base), get_d(base + 1)
        one = jnp.ones_like(d0)
        states.append((one, get_r(base), d0 + d1, one, get_r(base + 1), d1))
    return tuple(states)


def line_reduce(get_d, get_r, weights, count, segments):
    size = count // segments

    def body(i, states):
        new = []
        for k, (ea, ra, g, e, r, d) in enumerate(states):
            j = k * size + i
            d1 = get_d(j + 1)
            f = d + d1
            s = 1.0 / (e + g + f)
            wf, wg = f * s, g * s
            weights[0, j] = wf
            weights[1, j] = wg
            weights[2, j] = r * s
            new.append((ea + wg * e, ra + wg * r, wf * g, 1.0 + wf * e, get_r(j + 1) + wf * r, d1))
        return tuple(new)

    return lax.fori_loop(1, size - 1, body, line_start(get_d, get_r, count, segments))


def line_chain(get_d, states, count, edge):
    segments = len(states)
    size = count // segments
    chains = []
    for k, (ea, ra, g, e, r, d) in enumerate(states):
        f = d + get_d((k + 1) * size) if k + 1 < segments else edge(d)
        chains.append((ea, ra, e, r, g, f))
    return merge_all(chains)


def line_back(put, weights, count, ends):
    size = count // len(ends)
    for k, (a, b) in enumerate(ends):
        put(k * size, a)
        put(k * size + size - 1, b)

    def body(t, values):
        new = []
        for k, v in enumerate(values):
            j = k * size + size - 2 - t
            v = weights[0, j] * v + (weights[1, j] * ends[k][0] + weights[2, j])
            put(j, v)
            new.append(v)
        return tuple(new)

    lax.fori_loop(0, size - 2, body, tuple(b for a, b in ends), unroll=3 if (size - 2) % 3 == 0 else 2)


def kernel(ny, nz, vol, contrast_in, out, c_ref, t_ref, b_ref, gx_ref, w_ref, d_ref, dt_ref, wx_ref, wy_ref, wz_ref, vx_ref, vy_ref,
           xt_ref, ce_ref, cur_ref, zr_ref, zi_ref, zsend, zbuf, zvsend, zv, ysend, yrecv, yall, yv_ref,
           con, load_s, halo_s, halo_r, zs, zrs, zvs, zvr, ys, yr, yas, yar):
    depth, nx, cols = vol.shape
    rows = cols + 3 * PAD
    tall = depth + 2 * HALO
    chunks = cols // CHUNK
    ky = lax.axis_index("gy")
    kz = lax.axis_index("gz")

    def at(y, z):
        return {"gy": y, "gz": z}

    def exists(dy, dz):
        ok = True
        if dy:
            ok = (ky + dy >= 0) & (ky + dy < ny)
        if dz:
            ok = ok & (kz + dz >= 0) & (kz + dz < nz)
        return ok

    groups = ny // 2
    side = lax.rem(ky, 2)
    group = lax.div(ky, 2)
    twin = ky + 1 - 2 * side

    def member(j):
        return 2 * lax.rem(group + j, groups) + side

    def load(k):
        return pltpu.make_async_copy(
            vol.at[pl.ds(k * HALO, HALO)], cur_ref.at[pl.ds(k * HALO, HALO), pl.ds(0, nx), :], load_s.at[k])

    load_contrast = pltpu.make_async_copy(contrast_in, con, load_s.at[depth // HALO])
    for k in range(depth // HALO):
        load(k).start()
    load_contrast.start()

    barrier = pltpu.get_barrier_semaphore()
    expected = jnp.int32(groups)
    for dy, dz in DIRECTIONS:
        ok = exists(dy, dz)
        expected = expected + jnp.where(ok, 1, 0)

        @pl.when(ok)
        def _(dy=dy, dz=dz):
            pl.semaphore_signal(barrier, inc=1, device_id=at(ky + dy, kz + dz), device_id_type=MESH)

    for y in [twin] + [member(j) for j in range(1, groups)]:
        pl.semaphore_signal(barrier, inc=1, device_id=at(y, kz), device_id_type=MESH)

    source = lax.broadcasted_iota(jnp.int32, (nx, nx), 0)
    target = lax.broadcasted_iota(jnp.int32, (nx, nx), 1)

    def taps_at(target):
        apart = jnp.where((target >= 0) & (target < nx), jnp.abs(source - target), 3)
        return jnp.where(apart == 0, TAPS[2], jnp.where(apart == 1, TAPS[1], jnp.where(apart == 2, TAPS[0], 0.0)))

    for half, matrix in enumerate((taps_at(target), taps_at(target + 1) - taps_at(target - 1))):
        part = slice(half * nx, half * nx + nx)
        coarse = matrix.astype(jnp.bfloat16)
        w_ref[0:nx, part] = coarse
        w_ref[nx:2 * nx, part] = coarse
        w_ref[2 * nx:, part] = (matrix - coarse.astype(jnp.float32)).astype(jnp.bfloat16)

    load_contrast.wait()

    @pl.loop(0, depth // HALO)
    def _(k):
        load(k).wait()
        for t in range(HALO):
            z = HALO * k + t
            c_ref[0, z + HALO, PAD:PAD + cols, :] = cur_ref[z, 0:nx, :].T

    pl.semaphore_wait(barrier, expected)

    left = kz < nz // 2
    inward = jnp.where(left, 1, -1)
    order = jnp.where(left, kz, nz - 1 - kz)
    middle = order == nz // 2 - 1
    outermost = order == 0
    slot_out = jnp.where(middle, 1, 0)

    contrast = con[...]
    squared = jnp.broadcast_to(contrast * contrast, (STENCIL_ROWS, nx))

    tall_x = nx + SKEW
    tall_y = cols + SKEW
    cur2 = cur_ref.reshape(depth * tall_x, cols)
    dt2 = dt_ref.reshape(depth * tall_x, cols)
    vx2 = vx_ref.reshape(depth * tall_x, cols)
    vy2 = vy_ref.reshape(depth * tall_y, nx)
    d2 = d_ref.reshape((depth + 2) * rows, nx)
    ce2 = ce_ref.reshape(BATCH * tall_y, nx)

    def place(z):
        if z < 0 or z >= depth:
            return depth if z < 0 else depth + 1
        if z < HALO:
            return z
        return z - BATCH if z >= depth - HALO else z + HALO

    messages, sends, needs, edge_rows = message_plan(cols)

    def halo(i, slot, thin=False):
        dy, dz, start, size = messages[i]
        deep = HALO - 1 if thin else HALO
        src_y = {0: (PAD + start, size), 1: (cols, PAD), -1: (PAD, PAD)}[dy]
        dst_y = {0: (PAD + start, size), 1: (0, PAD), -1: (PAD + cols, PAD)}[dy]
        src_z = {0: (HALO, depth), 1: (depth + HALO - deep, deep), -1: (HALO, deep)}[dz]
        dst_z = {0: (HALO, depth), 1: (HALO - deep, deep), -1: (HALO + depth, deep)}[dz]
        volume = c_ref.at[slot]
        copy = pltpu.make_async_remote_copy(
            src_ref=volume.at[pl.ds(*src_z), pl.ds(*src_y), :], dst_ref=volume.at[pl.ds(*dst_z), pl.ds(*dst_y), :],
            send_sem=halo_s.at[slot, i], recv_sem=halo_r.at[slot, i],
            device_id=at(ky + dy, kz + dz), device_id_type=MESH)
        return copy, dst_z, dst_y

    def forms(i, at_sender):
        dy, dz = messages[i][:2]
        here = exists(dy, dz) if at_sender else exists(-dy, -dz)
        if dy or not dz:
            return [(here, False)]
        sender = kz if at_sender else kz - dz
        outward = sender >= nz // 2 if dz > 0 else sender < nz // 2
        return [(here & outward, True), (here & jnp.logical_not(outward), False)]

    def send(batch, slot):
        for i in batch:
            dy, dz = messages[i][:2]
            _, dst_z, dst_y = halo(i, slot)
            for chosen, thin in forms(i, True):
                @pl.when(chosen)
                def _(i=i, thin=thin):
                    halo(i, slot, thin)[0].start()

            @pl.when(jnp.logical_not(exists(-dy, -dz)))
            def _(dst_z=dst_z, dst_y=dst_y):
                c_ref[slot, pl.ds(*dst_z), pl.ds(*dst_y), :] = jnp.zeros((dst_z[1], dst_y[1], nx), jnp.float32)

    def receive(batch, slot):
        for i in batch:
            for chosen, thin in forms(i, False):
                @pl.when(chosen)
                def _(i=i, thin=thin):
                    halo(i, slot, thin)[0].wait_recv()

    send(range(len(messages)), 0)

    @pl.loop(0, STEPS)
    def _(step):
        c4 = c_ref.at[step]
        c2 = c4.reshape(tall * rows, nx)
        later = lax.rem(step + 1, STEPS)

        def blur_layer(z, r0, size):
            part = pl.ds(r0, size)
            total = TAPS[2] * c4[z + 2, part, :]
            total = total + TAPS[1] * (c4[z + 1, part, :] + c4[z + 3, part, :])
            total = total + TAPS[0] * (c4[z, part, :] + c4[z + 4, part, :])
            t_ref[z, pl.ds(r0, size), :] = total

        def blur_planes(planes, pieces):
            totals = []
            for z in planes:
                for r0, size in pieces:
                    def tap(o):
                        return t_ref[z, pl.ds(r0 + 4 + o, size), :]
                    totals.append(TAPS[2] * tap(0) + TAPS[1] * (tap(-1) + tap(1)) + TAPS[0] * (tap(-2) + tap(2)))
            total = jnp.concatenate(totals)
            coarse = total.astype(jnp.bfloat16)
            fine = (total - coarse.astype(jnp.float32)).astype(jnp.bfloat16)

            both = jnp.dot(jnp.concatenate([coarse, fine], axis=1), w_ref[0:2 * nx], preferred_element_type=jnp.float32)
            both = both + jnp.dot(coarse, w_ref[2 * nx:], preferred_element_type=jnp.float32)
            start = 0
            for z in planes:
                for r0, size in pieces:
                    b_ref[z, pl.ds(r0, size), :] = both[start:start + size, :nx]
                    gx_ref[z, pl.ds(r0, size), :] = both[start:start + size, nx:]
                    start += size

        def blur_edges(spans, low, high):
            for row, present in ((PAD - 5, ky > 0), (cols + PAD - 4, ky < ny - 1)):
                if low <= row < high:
                    @pl.when(jnp.logical_not(present))
                    def _(row=row):
                        for z0, z1 in spans:
                            b_ref[z0:z1, row:row + 1, :] = jnp.zeros((z1 - z0, 1, nx), jnp.float32)

        def diffuse(z, r0, size, spot=None):
            grad_x = gx_ref[z + 1, pl.ds(r0 + 4, size), :]
            grad_z = b_ref[z + 2, pl.ds(r0 + 4, size), :] - b_ref[z, pl.ds(r0 + 4, size), :]
            grad_y = b_ref[z + 1, pl.ds(r0 + 5, size), :] - b_ref[z + 1, pl.ds(r0 + 3, size), :]
            square = (grad_x * grad_x + grad_y * grad_y + grad_z * grad_z) * 0.25
            d_ref[place(z - 1) if spot is None else spot, pl.ds(r0 + PAD, size), :] = (SCALE * squared[:size]) / (squared[:size] + square)

        inner = list(range(HALO, depth))
        own_rows = [(r0, min(STENCIL_ROWS, cols + PAD - r0)) for r0 in range(PAD, cols + PAD, STENCIL_ROWS)]
        bulk = [(r0, min(STENCIL_ROWS, cols - r0)) for r0 in range(PAD, cols, STENCIL_ROWS)]
        bulk_d = [(r0, min(STENCIL_ROWS, cols - PAD - r0)) for r0 in range(PAD, cols - PAD, STENCIL_ROWS)]

        @pl.loop(HALO, depth)
        def _(z):
            for piece in own_rows:
                blur_layer(z, *piece)

        @pl.loop(0, (depth - HALO) // 2)
        def _(k):
            blur_planes([HALO + 2 * k, HALO + 2 * k + 1], bulk)

        for piece in bulk_d:
            diffuse(HALO, *piece)
            diffuse(depth - HALO + 1, *piece)

        @pl.loop(0, BATCH // 2)
        def _(k):
            for t in range(2):
                for piece in bulk_d:
                    diffuse(HALO + 1 + 2 * k + t, *piece, BATCH + 2 * k + t)

        @pl.loop(0, 2)
        def _(k):
            for t in range(HALO):
                ce_ref[HALO * k + t, 0:cols, :] = c4[HALO + (depth - HALO) * k + t, PAD:PAD + cols, :]

        @pl.when(step > 0)
        def _():
            @pl.loop(0, depth // 4)
            def _(k):
                for t in range(4):
                    z = 4 * k + t
                    cur_ref[z, 0:nx, :] = c4[z + HALO, PAD:PAD + cols, :].T

        receive(edge_rows, step)
        for z in inner:
            blur_layer(z, 0, PAD)
            blur_layer(z, cols + PAD, PAD)
        blur_planes(inner, [(0, PAD), (cols, PAD)])
        blur_edges([(HALO, depth)], 0, cols + PAD)
        for z in range(HALO, depth - 2):
            diffuse(z, 0, PAD)
            diffuse(z, cols - PAD, 2 * PAD)

        def y_at(b):
            def get_d(i):
                return d2[pl.ds(i + b * BATCH * rows + PAD, BATCH, stride=rows), :]

            def get_r(i):
                if b:
                    return c2[pl.ds(i + 2 * HALO * rows + PAD, BATCH, stride=rows), :]
                return ce2[pl.ds(i, BATCH, stride=tall_y), :]

            def put(i, v):
                vy2[pl.ds(i + b * BATCH * tall_y, BATCH, stride=tall_y), :] = v

            return get_d, get_r, put

        def y_copy(b):
            return pltpu.make_async_remote_copy(
                src_ref=ysend.at[step, b], dst_ref=yrecv.at[step, b], send_sem=ys.at[step, b],
                recv_sem=yr.at[step, b], device_id=at(twin, kz), device_id_type=MESH)

        def y_spread(b, j):
            return pltpu.make_async_remote_copy(
                src_ref=yall.at[step, b, 0], dst_ref=yall.at[step, b, j], send_sem=yas.at[step, b, j],
                recv_sem=yar.at[step, b, j], device_id=at(member(j), kz), device_id_type=MESH)

        first = side == 0
        held = [None, None]

        def y_begin(b):
            get_d, get_r, _ = y_at(b)
            states = line_reduce(get_d, get_r, wy_ref.at[b], cols, SEGMENTS_Y)
            chain, levels = line_chain(
                get_d, states, cols, lambda d: jnp.where(ky < ny - 1, d + get_d(cols), 0.0))
            for j in range(6):
                ysend[step, b, j] = chain[j]
            y_copy(b).start()
            held[b] = levels

        def y_join(b):
            chain = tuple(ysend[step, b, j] for j in range(6))
            y_copy(b).wait_recv()
            other = tuple(yrecv[step, b, j] for j in range(6))
            pair_l = tuple(jnp.where(first, a, b) for a, b in zip(chain, other))
            pair_r = tuple(jnp.where(first, b, a) for a, b in zip(chain, other))
            (ea, ra, eb, rb, g, f), pair = merge(pair_l, pair_r)
            s = 1.0 / (eb + g + f)
            wg, wf, q = g * s, f * s, rb * s
            for j, value in enumerate((ea + wg * eb, ra + wg * rb, wf * eb, wf * rb, wf * g)):
                yall[step, b, 0, j] = value
            for j in range(1, groups):
                y_spread(b, j).start()
            held[b] = (held[b], pair, wg, wf, q)

        def y_end(b):
            levels, pair, wg, wf, q = held[b]
            for j in range(1, groups):
                y_spread(b, j).wait_recv()
            e, r, de, dr, link = [yall[step, b, lax.rem(group, groups), j] for j in range(5)]
            ways = []
            for m in range(1, groups):
                s = 1.0 / (e + link)
                w = link * s
                ways.append((w, r * s))
                e, r = w * e + de, w * r + dr
                here = [yall[step, b, lax.rem(group - m + groups, groups), j] for j in range(5)]
                e, r = e + here[0], r + here[1]
                de, dr, link = here[2:]
            v = r / e
            yv_ref[b, groups] = jnp.zeros_like(v)
            yv_ref[b, groups - 1] = v
            for m in range(groups - 2, -1, -1):
                v = ways[m][0] * v + ways[m][1]
                yv_ref[b, m] = v
            va = yv_ref[b, group]
            vb = wg * va + (wf * yv_ref[b, group + 1] + q)
            inner_l, inner_r = unmerge(pair, va, vb)
            va, vb = jnp.where(first, va, inner_r), jnp.where(first, inner_l, vb)
            line_back(y_at(b)[2], wy_ref.at[b], cols, unmerge_all(levels, va, vb))

        def turn(b):
            @pl.loop(0, 2)
            def _(k):
                for t in range(HALO):
                    z = HALO + HALO * k + t if b else (depth - HALO) * k + t
                    dt_ref[z, 0:nx, :] = d_ref[b * BATCH + HALO * k + t, PAD:PAD + cols, :].T

        y_begin(1)
        turn(1)

        def z_copy(c, slot):
            return pltpu.make_async_remote_copy(
                src_ref=zsend.at[step, c], dst_ref=zbuf.at[step, slot, c], send_sem=zs.at[step, slot, c],
                recv_sem=zrs.at[step, slot, c], device_id=at(ky, kz + inward), device_id_type=MESH)

        def z_back(c):
            return pltpu.make_async_remote_copy(
                src_ref=zvsend.at[step, c], dst_ref=zv.at[step, c], send_sem=zvs.at[step, c],
                recv_sem=zvr.at[step, c], device_id=at(ky, kz - inward), device_id_type=MESH)

        def z_inward(c, carry):
            own = pl.ds(pl.multiple_of(c * CHUNK, CHUNK), CHUNK)

            @pl.when(jnp.logical_not(outermost))
            def _():
                z_copy(c, 0).wait_recv()
                f = zr_ref[6, own, :]
                s = 1.0 / (zbuf[step, 0, c, 0] + f)
                u = f * s
                zi_ref[4, own, :] = u
                zi_ref[5, own, :] = zbuf[step, 0, c, 1] * s
                zr_ref[0, own, :] += u * zbuf[step, 0, c, 0]
                zr_ref[1, own, :] += u * zbuf[step, 0, c, 1]

            eo, ro, ei, ri, g, f = [zr_ref[j, own, :] for j in range(6)]
            s = 1.0 / (eo + g)
            w = g * s
            ei = ei + w * eo
            ri = ri + w * ro
            u = jnp.where(middle, f / (ei + f), 1.0)
            zi_ref[0, own, :] = w
            zi_ref[1, own, :] = ro * s
            zi_ref[2, own, :] = ei
            zi_ref[3, own, :] = ri
            zsend[step, c, 0] = u * ei
            zsend[step, c, 1] = u * ri
            z_copy(c, slot_out).start()
            return carry

        def z_solve(c):
            own = pl.ds(pl.multiple_of(c * CHUNK, CHUNK), CHUNK)

            @pl.when(middle)
            def _():
                z_copy(c, 1).wait_recv()
                zr_ref[0, own, :] = (zi_ref[3, own, :] + zbuf[step, 1, c, 1]) / (zi_ref[2, own, :] + zbuf[step, 1, c, 0])

            @pl.when(jnp.logical_not(middle))
            def _():
                z_back(c).wait_recv()
                zr_ref[0, own, :] = zv[step, c]

            vo = zi_ref[0, own, :] * zr_ref[0, own, :] + zi_ref[1, own, :]
            zr_ref[1, own, :] = vo

            @pl.when(jnp.logical_not(outermost))
            def _():
                zvsend[step, c] = zi_ref[4, own, :] * vo + zi_ref[5, own, :]
                z_back(c).start()

        def z_finish(c):
            own = pl.ds(c * CHUNK, CHUNK)
            padded = pl.ds(c * CHUNK + PAD, CHUNK)

            def put(i, v):
                c_ref[later, HALO + i, padded, :] = (vy_ref[place(i), own, :] + xt_ref[i, own, :] + v) * (1.0 / 3.0)

            vi, vo = zr_ref[0, own, :], zr_ref[1, own, :]
            va = jnp.where(left, vo, vi)
            v = jnp.where(left, vi, vo)
            put(0, va)
            put(depth - 1, v)
            for i in range(depth - 2, 0, -1):
                v = wz_ref[0, i, own, :] * v + (wz_ref[1, i, own, :] * va + wz_ref[2, i, own, :])
                put(i, v)

        def z_chain(c):
            y0 = c * CHUNK
            part = pl.ds(y0 + PAD, CHUNK)
            own = pl.ds(y0, CHUNK)
            d = d_ref[place(0), part, :]
            f_lo = jnp.where(kz > 0, d_ref[place(-1), part, :] + d, 0.0)
            d_next = d_ref[place(1), part, :]
            g = d + d_next
            d = d_next
            ea = jnp.ones_like(g)
            ra = c4[HALO, part, :]
            e = ea
            r = c4[HALO + 1, part, :]
            for i in range(1, depth - 1):
                d_next = d_ref[place(i + 1), part, :]
                f = d + d_next
                d = d_next
                s = 1.0 / (e + g + f)
                wf, wg = f * s, g * s
                wz_ref[0, i, own, :] = wf
                wz_ref[1, i, own, :] = wg
                wz_ref[2, i, own, :] = r * s
                ea = ea + wg * e
                ra = ra + wg * r
                e = 1.0 + wf * e
                r = c4[HALO + i + 1, part, :] + wf * r
                g = wf * g
            f_hi = jnp.where(kz < nz - 1, d + d_ref[place(depth), part, :], 0.0)
            zr_ref[0, own, :] = jnp.where(left, ea, e)
            zr_ref[1, own, :] = jnp.where(left, ra, r)
            zr_ref[2, own, :] = jnp.where(left, e, ea)
            zr_ref[3, own, :] = jnp.where(left, r, ra)
            zr_ref[4, own, :] = g
            zr_ref[5, own, :] = jnp.where(left, f_hi, f_lo)
            zr_ref[6, own, :] = jnp.where(left, f_lo, f_hi)

            @pl.when(outermost)
            def _():
                z_inward(c, 0)

        outer = list(range(HALO)) + list(range(depth, depth + HALO))
        for c, batch in enumerate(needs):
            start, stop = c * CHUNK, (c + 1) * CHUNK
            tail = PAD if c + 1 == chunks else 0
            receive(batch, step)
            t0 = start + 2 * PAD if c else 0
            for z in outer:
                blur_layer(z, t0, stop + 2 * PAD - t0)
            b0 = start + PAD if c else 0
            b1 = stop + PAD
            blur_planes(outer, [(b0, b1 - b0)])
            blur_edges([(0, HALO), (depth, depth + HALO)], b0, b1)

            @pl.when(kz == 0)
            def _(b0=b0, b1=b1):
                b_ref[1, b0:b1, :] = jnp.zeros((b1 - b0, nx), jnp.float32)

            @pl.when(kz == nz - 1)
            def _(b0=b0, b1=b1):
                b_ref[depth + 2, b0:b1, :] = jnp.zeros((b1 - b0, nx), jnp.float32)

            for z in list(range(HALO)) + list(range(depth - 2, depth + 2)):
                diffuse(z, start, stop + tail - start)
            z_chain(c)
            if c == 0:
                y_join(1)

        def dx(i):
            return dt2[pl.ds(i, depth, stride=tall_x), :]

        def rx(i):
            return cur2[pl.ds(i, depth, stride=tall_x), :]

        def put_x(i, v):
            vx2[pl.ds(i, depth, stride=tall_x), :] = v

        def z_piece(k):
            @pl.when(jnp.logical_not(outermost))
            def _():
                z_inward(k, 0)

        z_piece(0)
        y_begin(0)
        for k in range(1, chunks - 1):
            z_piece(k)

        y_join(0)
        z_piece(chunks - 1)
        turn(0)

        states = line_reduce(dx, rx, wx_ref, nx, SEGMENTS)
        x_chain, levels_x = line_chain(dx, states, nx, jnp.zeros_like)
        line_back(put_x, wx_ref, nx, unmerge_all(levels_x, *solve_pair(*x_chain[:5])))

        @pl.when(jnp.logical_not(outermost))
        def _():
            @pl.loop(0, chunks)
            def _(c):
                z_solve(c)

        @pl.loop(0, depth // 4)
        def _(k):
            for t in range(4):
                z = 4 * k + t
                xt_ref[z] = vx_ref[z, 0:nx, :].T

        y_end(1)
        y_end(0)

        for c in range(chunks):
            @pl.when(outermost)
            def _(c=c):
                z_solve(c)

            z_finish(c)

            @pl.when(step + 1 < STEPS)
            def _(c=c):
                send(sends[c], later)

        for b in range(2):
            y_copy(b).wait_send()
            for j in range(1, groups):
                y_spread(b, j).wait_send()

        for i in range(len(messages)):
            for chosen, thin in forms(i, True):
                @pl.when(chosen)
                def _(i=i, thin=thin):
                    halo(i, step, thin)[0].wait_send()

        @pl.loop(0, chunks)
        def _(c):
            z_copy(c, slot_out).wait_send()

            @pl.when(jnp.logical_not(outermost))
            def _():
                z_back(c).wait_send()

    @pl.loop(0, depth // 4)
    def _(k):
        for t in range(4):
            z = 4 * k + t
            out[z] = c_ref[0, z + HALO, PAD:PAD + cols, :].T


def on_device(volume, contrast):
    depth, nx, cols = volume.shape
    ny = lax.axis_size("gy")
    nz = lax.axis_size("gz")
    groups = ny // 2
    assert ny % 2 == 0 and nz % 2 == 0 and depth == 2 * BATCH == 4 * HALO
    rows = cols + 3 * PAD
    chunks = cols // CHUNK
    f32 = jnp.float32
    dma = pltpu.SemaphoreType.DMA
    count = len(message_plan(cols)[0])
    return pl.pallas_call(
        functools.partial(kernel, ny, nz),
        out_shape=jax.ShapeDtypeStruct(volume.shape, f32),
        in_specs=[pl.BlockSpec(memory_space=pl.ANY)] * 2,
        out_specs=pl.BlockSpec(memory_space=pltpu.VMEM),
        scratch_shapes=[
            pltpu.VMEM((STEPS, depth + 2 * HALO, rows, nx), f32),
            pltpu.VMEM((depth + 4, rows, nx), f32),
            pltpu.VMEM((depth + 4, rows + 16, nx), f32),
            pltpu.VMEM((depth + 4, rows, nx), f32),
            pltpu.VMEM((3 * nx, 2 * nx), jnp.bfloat16),
            pltpu.VMEM((depth + 2, rows, nx), f32),
            pltpu.VMEM((depth, nx + SKEW, cols), f32),
            pltpu.VMEM((3, nx, depth, cols), f32),
            pltpu.VMEM((2, 3, cols, BATCH, nx), f32),
            pltpu.VMEM((3, depth, cols, nx), f32),
            pltpu.VMEM((depth, nx + SKEW, cols), f32),
            pltpu.VMEM((depth, cols + SKEW, nx), f32),
            pltpu.VMEM((depth, cols, nx), f32),
            pltpu.VMEM((BATCH, cols + SKEW, nx), f32),
            pltpu.VMEM((depth, nx + SKEW, cols), f32),
            pltpu.VMEM((7, cols, nx), f32),
            pltpu.VMEM((6, cols, nx), f32),
            pltpu.VMEM((STEPS, chunks, 2, CHUNK, nx), f32),
            pltpu.VMEM((STEPS, 2, chunks, 2, CHUNK, nx), f32),
            pltpu.VMEM((STEPS, chunks, CHUNK, nx), f32),
            pltpu.VMEM((STEPS, chunks, CHUNK, nx), f32),
            pltpu.VMEM((STEPS, 2, 6, BATCH, nx), f32),
            pltpu.VMEM((STEPS, 2, 6, BATCH, nx), f32),
            pltpu.VMEM((STEPS, 2, groups, 5, BATCH, nx), f32),
            pltpu.VMEM((2, groups + 1, BATCH, nx), f32),
            pltpu.VMEM((1, nx), f32), dma((depth // HALO + 1,)),
            dma((STEPS, count)), dma((STEPS, count)),
            dma((STEPS, 2, chunks)), dma((STEPS, 2, chunks)),
            dma((STEPS, chunks)), dma((STEPS, chunks)),
            dma((STEPS, 2)), dma((STEPS, 2)),
            dma((STEPS, 2, groups)), dma((STEPS, 2, groups)),
        ],
        compiler_params=pltpu.CompilerParams(
            collective_id=0, has_side_effects=True, vmem_limit_bytes=52 * 2 ** 20
        ),
    )(volume, contrast.reshape(1, nx))


def solution(mesh):
    in_specs = (P("gz", None, "gy"), P())
    out_specs = P("gz", None, "gy")
    return jax.shard_map(
        on_device, mesh=mesh, in_specs=in_specs, out_specs=out_specs, check_vma=False
    )
```
